256 devices in a mesh: tmpl: 4 (over y), freq: 64 (over x, z, core).
Axes of the slice: x: 4, y: 4, z: 8, core: 2. Of those that a mesh axis runs over, the one named last changes fastest.
Arguments:
- strain: float32 [64, 524288], P('tmpl', 'freq'), may hold values from -6 to 6
- psd: float32 [512, 512], P(None, 'freq'), may hold values from 0.1 to 10
- templates: bfloat16 [1024, 2, 512, 512], P('tmpl', None, 'freq'), may hold values from -0.0234375 to 0.0234375
- cutoffs: int32 [1024], P('tmpl'), may hold values from 1 to 512, as said below
- lags: int32 [16], replicated, may hold values from 0 to 524287
Outputs:
- intersections: float32 [64, 32, 1024], P('freq', None, 'tmpl')
The draws below stay inside these ranges and needn't reach their ends.
Inputs may be any that keep to these rules, and one draw needn't show every extreme that they name: `cutoffs`: the cutoff counts do not increase along the template index.
All inputs are finite; a program needn't handle non-finite values.
Results may differ from the reference program's by a relative error of at most 0.004.
Values may be sent and summed in bfloat16 or wider, within the bound.
A program may use at most 128 MiB of HBM per device.

```python
import math
import jax
import jax.numpy as jnp
from jax import lax

A = 512
B = 1024
LEN = 524288
NB = 512
LAGS = 16
SEG = 64
TMPL = 1024


def draw_cutoffs(key, part):
    key_one = jax.random.fold_in(key, 11)
    key_two = jax.random.fold_in(key, 23)
    first_draw = jax.random.randint(key_one, (TMPL,), 1, NB + 1)
    second_draw = jax.random.randint(key_two, (TMPL,), 1, NB + 1)
    lowest = jnp.minimum(first_draw, second_draw)
    ordered = -jnp.sort(-lowest)
    ordered = ordered.at[0].set(NB).at[TMPL - 1].set(1)
    return ordered.astype(jnp.int32)


def plant(array, own_key, low, top_value):
    longest = array.shape.index(max(array.shape))
    spots = []
    for shift in (0, 1):
        where = [jax.random.randint(jax.random.fold_in(own_key, axis), (), 0, length) for axis, length in enumerate(array.shape)]
        where[longest] = (where[longest] + shift) % array.shape[longest]
        spots.append(tuple(where))
    return array.at[spots[0]].set(low).at[spots[1]].set(top_value)


def steps_of(own_key, shape, shards, smallest, top_value):
    def one(dim, parts):
        draws = jax.random.uniform(jax.random.fold_in(jax.random.fold_in(own_key, 6), dim), (parts,), jnp.float32, smallest / len(shards), top_value / len(shards))
        return jnp.repeat(jnp.exp(draws), shape[dim] // parts).reshape((-1,) + (1,) * (len(shape) - dim - 1))

    factor_of = one(*shards[0])
    for cut in shards[1:]:
        factor_of = factor_of * one(*cut)
    return factor_of


def noise(key, shape, width, limit, cuts=(), held_as=jnp.bfloat16):
    drawn = jax.random.normal(key, shape, jnp.float32) * width
    if len(cuts) > 0:
        drawn = steps_of(key, shape, cuts, -0.22, 0.18) * drawn
    return jnp.clip(drawn, min=-limit, max=limit).astype(held_as)


def setup_inputs(seed: int = 0) -> dict:
    seeds = jax.random.split(jax.random.key(seed), 6)
    return {
        "strain": noise(seeds[0], (SEG, LEN), 1.0, 6.0, ((0, 4), (1, 64)), jnp.float32),
        "psd": jnp.clip(jnp.exp(math.log(10.0) - 4.6051702 * jax.random.uniform(seeds[1], (NB, A), jnp.float32) ** steps_of(seeds[1], (NB, A), ((1, 64),), -0.2, 0.2)), 0.1, 10.0),
        "templates": noise(seeds[2], (TMPL, 2, NB, A), (NB * A // 4) ** -0.5, 0.0234375, ((0, 4), (2, 64))),
        "cutoffs": draw_cutoffs(jax.random.fold_in(seeds[5], 71), 0),
        "lags": plant(jax.random.randint(seeds[4], (LAGS,), 0, LEN), jax.random.fold_in(seeds[4], 1), 0, LEN - 1).astype(jnp.int32),
    }


two_pi = 2.0 * math.pi

def reference(strain, psd, templates, cutoffs, lags):
    spectrum = jnp.fft.rfft(strain, axis=1)[:, :LEN // 2]
    amplitude = jnp.sqrt(LEN * psd).reshape(1, NB * A)
    real_part = (jnp.real(spectrum) / amplitude).reshape(SEG, NB, A)
    imag_part = (jnp.imag(spectrum) / amplitude).reshape(SEG, NB, A)
    whitened = jnp.stack([real_part, imag_part], axis=1).astype(jnp.bfloat16)
    per_span = min(8, NB)
    span_total = NB // per_span
    position = jnp.arange(A, dtype=jnp.int32)

    def one_span(running, span_idx):
        offset = (span_idx * per_span).astype(jnp.int32)
        block_ids = offset + jnp.arange(per_span, dtype=jnp.int32)
        data_part = lax.dynamic_slice_in_dim(whitened, offset, per_span, 2).astype(jnp.float32)
        tmpl_part = lax.dynamic_slice_in_dim(templates, offset, per_span, 2)
        phase_int = (A * (lags[:, None] * block_ids[None, :] % B))[:, :, None] + (lags[:, None] * position[None, :] % LEN)[:, None, :]
        phase_angle = (phase_int % LEN).astype(jnp.float32) * (two_pi / LEN)
        lag_cos = jnp.cos(phase_angle)[None]
        lag_sin = jnp.sin(phase_angle)[None]
        data_real = data_part[:, 0][:, None]
        data_imag = data_part[:, 1][:, None]
        real_q = (data_real * lag_cos - data_imag * lag_sin).astype(jnp.bfloat16)
        imag_q = (data_real * lag_sin + data_imag * lag_cos).astype(jnp.bfloat16)
        real_rows = jnp.stack([real_q, imag_q], axis=2)
        imag_rows = jnp.stack([imag_q, -real_q], axis=2)
        lhs_rows = jnp.stack([real_rows, imag_rows], axis=1).reshape(SEG * 2 * LAGS, 2 * per_span * A).astype(jnp.float32)
        keep_mask = (block_ids[None, :] < cutoffs[:, None]).astype(jnp.bfloat16)
        masked = (tmpl_part * keep_mask[:, None, :, None]).reshape(TMPL, 2 * per_span * A).astype(jnp.float32)
        running = running + jnp.dot(lhs_rows, masked.T, precision=lax.Precision.HIGHEST)
        return (running, None)
    start_sum = jnp.zeros((SEG * 2 * LAGS, TMPL), jnp.float32)
    running, unused = lax.scan(one_span, start_sum, jnp.arange(span_total, dtype=jnp.int32))
    return running.reshape(SEG, 2 * LAGS, TMPL)
```

```python
import math

import jax
import jax.numpy as jnp
from jax import lax
from jax.experimental import pallas as pl
from jax.experimental.pallas import tpu as pltpu
from jax.sharding import PartitionSpec as P

A = 512
B = 1024
LEN = 524288
NB = 512


two_pi = 2.0 * math.pi


def cos_sin_table(row_ids, col_ids, modulus):
    product = row_ids[:, None] * col_ids[None, :] % modulus
    phase_angle = product.astype(jnp.float32) * (two_pi / modulus)
    return (jnp.cos(phase_angle), jnp.sin(phase_angle))


def intersect_kernel(ph_ref, dat_ref, tm_ref, out_ref, lhs_ref):
    step = pl.program_id(0)
    seg_count = dat_ref.shape[2]
    lag_total = ph_ref.shape[2]
    rows = seg_count * lag_total
    chunk = 8

    @pl.when(step == 0)
    def _():
        out_ref[...] = jnp.zeros_like(out_ref)

    lag_cos = ph_ref[0, 0][None]
    lag_sin = ph_ref[0, 1][None]

    def build(i, carry):
        s0 = pl.multiple_of(i * chunk, chunk)
        data_real = dat_ref[0, 0, pl.ds(s0, chunk), :].astype(jnp.float32)[:, None, :]
        data_imag = dat_ref[0, 1, pl.ds(s0, chunk), :].astype(jnp.float32)[:, None, :]
        real_q = data_real * lag_cos - data_imag * lag_sin
        imag_q = data_real * lag_sin + data_imag * lag_cos
        r0 = pl.multiple_of(i * chunk * lag_total, chunk * lag_total)
        lhs_ref[pl.ds(r0, chunk * lag_total), :] = real_q.reshape(chunk * lag_total, -1).astype(jnp.bfloat16)
        lhs_ref[pl.ds(rows + r0, chunk * lag_total), :] = imag_q.reshape(chunk * lag_total, -1).astype(jnp.bfloat16)
        return carry

    lax.fori_loop(0, seg_count // chunk, build, 0)
    dims = (((1,), (1,)), ((), ()))
    lhs = lhs_ref[...]
    with_re = lax.dot_general(lhs, tm_ref[0, 0], dims, preferred_element_type=jnp.float32)
    with_im = lax.dot_general(lhs, tm_ref[0, 1], dims, preferred_element_type=jnp.float32)
    real_sum = with_re[:rows] + with_im[rows:]
    imag_sum = with_re[rows:] - with_im[:rows]
    width = real_sum.shape[1]
    out_ref[:, 0:lag_total, :] += real_sum.reshape(seg_count, lag_total, width)
    out_ref[:, lag_total:, :] += imag_sum.reshape(seg_count, lag_total, width)


def intersect(seg_piece, templates, cutoffs, lags, first_block):
    seg_count, _, blocks_here, width = seg_piece.shape
    tmpl_local = templates.shape[0]
    lag_total = lags.shape[0]
    block_ids = first_block + jnp.arange(blocks_here, dtype=jnp.int32)
    position = jnp.arange(width, dtype=jnp.int32)
    phase_int = (A * (lags[:, None] * block_ids[None, :] % B))[:, :, None] + (
        lags[:, None] * position[None, :] % LEN
    )[:, None, :]
    phase_angle = (phase_int % LEN).astype(jnp.float32) * (two_pi / LEN)
    phases = jnp.stack([jnp.cos(phase_angle), jnp.sin(phase_angle)], axis=0).transpose(2, 0, 1, 3)
    keep = block_ids[None, None, :, None] < cutoffs[:, None, None, None]
    masked = jnp.where(keep, templates, jnp.zeros_like(templates)).transpose(2, 1, 0, 3)
    data = seg_piece.transpose(2, 1, 0, 3)
    rows = seg_count * lag_total
    flops = 2 * 2 * (2 * rows) * width * tmpl_local * blocks_here
    moved = masked.size * 2 + data.size * 2 + phases.size * 4 + seg_count * 2 * lag_total * tmpl_local * 4
    return pl.pallas_call(
        intersect_kernel,
        out_shape=jax.ShapeDtypeStruct((seg_count, 2 * lag_total, tmpl_local), jnp.float32),
        grid=(blocks_here,),
        in_specs=[
            pl.BlockSpec((1, 2, lag_total, width), lambda j: (j, 0, 0, 0)),
            pl.BlockSpec((1, 2, seg_count, width), lambda j: (j, 0, 0, 0)),
            pl.BlockSpec((1, 2, tmpl_local, width), lambda j: (j, 0, 0, 0)),
        ],
        out_specs=pl.BlockSpec((seg_count, 2 * lag_total, tmpl_local), lambda j: (0, 0, 0)),
        scratch_shapes=[pltpu.VMEM((2 * rows, width), jnp.bfloat16)],
        compiler_params=pltpu.CompilerParams(dimension_semantics=("arbitrary",)),
        cost_estimate=pl.CostEstimate(flops=flops, transcendentals=0, bytes_accessed=moved),
    )(phases, data, masked)


def on_device(strain, psd, templates, cutoffs, lags):
    freq_count = lax.axis_size("freq")
    freq_index = lax.axis_index("freq")
    seg_local = strain.shape[0]
    step_time = B // freq_count
    highest = lax.Precision.HIGHEST
    first_cos, first_sin = cos_sin_table(
        jnp.arange(A, dtype=jnp.int32), jnp.arange(A, dtype=jnp.int32), A
    )
    first_table = jnp.concatenate([first_cos, -first_sin], axis=0)
    time_ids = freq_index * step_time + jnp.arange(step_time, dtype=jnp.int32)
    twist_cos, twist_sin = cos_sin_table(jnp.arange(A, dtype=jnp.int32), time_ids, LEN)
    slab_blocks = strain.reshape(seg_local, A // freq_count, B)
    both_parts = jnp.einsum(
        "kn,snb->skb",
        first_table,
        lax.all_to_all(slab_blocks, "freq", split_axis=2, concat_axis=1, tiled=True),
        precision=highest,
    )
    half_rows = first_table.shape[0] // 2
    real_part = both_parts[:, :half_rows]
    imag_part = both_parts[:, half_rows:]
    second_cos, second_sin = cos_sin_table(
        jnp.arange(B, dtype=jnp.int32), jnp.arange(NB, dtype=jnp.int32), B
    )
    rotation = jnp.concatenate(
        [
            jnp.concatenate([second_cos, -second_sin], axis=1),
            jnp.concatenate([second_sin, second_cos], axis=1),
        ],
        axis=0,
    )
    amplitude = jnp.sqrt(LEN * psd)
    real_in = lax.all_to_all(
        real_part * twist_cos + imag_part * twist_sin,
        "freq",
        split_axis=1,
        concat_axis=2,
        tiled=True,
    )
    imag_in = lax.all_to_all(
        imag_part * twist_cos - real_part * twist_sin,
        "freq",
        split_axis=1,
        concat_axis=2,
        tiled=True,
    )
    joined = jnp.concatenate([real_in, imag_in], axis=2)
    both_out = jnp.einsum("spc,cm->smp", joined, rotation, precision=highest)
    both_out = both_out.reshape(joined.shape[0], 2, NB, joined.shape[1])
    whitened = (both_out / amplitude).astype(jnp.bfloat16)
    local_data = lax.all_to_all(whitened, "freq", split_axis=2, concat_axis=3, tiled=True)
    first_block = freq_index * (NB // freq_count)
    seg_piece = lax.all_gather(local_data, "tmpl", axis=0, tiled=True)
    partial_sums = intersect(seg_piece, templates, cutoffs, lags, first_block)
    return lax.psum_scatter(partial_sums, "freq", scatter_dimension=0, tiled=True)


def solution(mesh):
    placed = (P("tmpl", "freq"), P(None, "freq"), P("tmpl", None, "freq", None), P("tmpl"), P())
    return jax.shard_map(
        on_device, mesh=mesh, in_specs=placed, out_specs=P("freq", None, "tmpl"), check_vma=False
    )
```

```python
import math

import jax
import jax.numpy as jnp
from jax import lax
from jax.experimental import pallas as pl
from jax.experimental.pallas import tpu as pltpu
from jax.sharding import Mesh, PartitionSpec as P

A = 512
B = 1024
LEN = 524288
NB = 512


two_pi = 2.0 * math.pi
FREQ = ("fx", "fz", "fc")


def cos_sin_table(row_ids, col_ids, modulus):
    product = row_ids[:, None] * col_ids[None, :] % modulus
    phase_angle = product.astype(jnp.float32) * (two_pi / modulus)
    return (jnp.cos(phase_angle), jnp.sin(phase_angle))


def intersect_kernel(ph_ref, dat_ref, tm_ref, out_ref, lhs_ref):
    step = pl.program_id(0)
    seg_count = dat_ref.shape[2]
    lag_total = ph_ref.shape[2]
    rows = seg_count * lag_total
    chunk = 8

    @pl.when(step == 0)
    def _():
        out_ref[...] = jnp.zeros_like(out_ref)

    lag_cos = ph_ref[0, 0][None]
    lag_sin = ph_ref[0, 1][None]

    def build(i, carry):
        s0 = pl.multiple_of(i * chunk, chunk)
        data_real = dat_ref[0, 0, pl.ds(s0, chunk), :].astype(jnp.float32)[:, None, :]
        data_imag = dat_ref[0, 1, pl.ds(s0, chunk), :].astype(jnp.float32)[:, None, :]
        real_q = data_real * lag_cos - data_imag * lag_sin
        imag_q = data_real * lag_sin + data_imag * lag_cos
        r0 = pl.multiple_of(i * chunk * lag_total, chunk * lag_total)
        lhs_ref[pl.ds(r0, chunk * lag_total), :] = real_q.reshape(chunk * lag_total, -1).astype(jnp.bfloat16)
        lhs_ref[pl.ds(rows + r0, chunk * lag_total), :] = imag_q.reshape(chunk * lag_total, -1).astype(jnp.bfloat16)
        return carry

    lax.fori_loop(0, seg_count // chunk, build, 0)
    dims = (((1,), (1,)), ((), ()))
    lhs = lhs_ref[...]
    with_re = lax.dot_general(lhs, tm_ref[0, 0], dims, preferred_element_type=jnp.float32)
    with_im = lax.dot_general(lhs, tm_ref[0, 1], dims, preferred_element_type=jnp.float32)
    real_sum = with_re[:rows] + with_im[rows:]
    imag_sum = with_re[rows:] - with_im[:rows]
    width = real_sum.shape[1]
    out_ref[:, 0:lag_total, :] += real_sum.reshape(seg_count, lag_total, width)
    out_ref[:, lag_total:, :] += imag_sum.reshape(seg_count, lag_total, width)


def intersect(seg_piece, templates, cutoffs, lags, first_block):
    seg_count, _, blocks_here, width = seg_piece.shape
    tmpl_local = templates.shape[0]
    lag_total = lags.shape[0]
    block_ids = first_block + jnp.arange(blocks_here, dtype=jnp.int32)
    position = jnp.arange(width, dtype=jnp.int32)
    phase_int = (A * (lags[:, None] * block_ids[None, :] % B))[:, :, None] + (
        lags[:, None] * position[None, :] % LEN
    )[:, None, :]
    phase_angle = (phase_int % LEN).astype(jnp.float32) * (two_pi / LEN)
    phases = jnp.stack([jnp.cos(phase_angle), jnp.sin(phase_angle)], axis=0).transpose(2, 0, 1, 3)
    keep = block_ids[None, None, :, None] < cutoffs[:, None, None, None]
    masked = jnp.where(keep, templates, jnp.zeros_like(templates)).transpose(2, 1, 0, 3)
    data = seg_piece.transpose(2, 1, 0, 3)
    rows = seg_count * lag_total
    flops = 2 * 2 * (2 * rows) * width * tmpl_local * blocks_here
    moved = masked.size * 2 + data.size * 2 + phases.size * 4 + seg_count * 2 * lag_total * tmpl_local * 4
    return pl.pallas_call(
        intersect_kernel,
        out_shape=jax.ShapeDtypeStruct((seg_count, 2 * lag_total, tmpl_local), jnp.float32),
        grid=(blocks_here,),
        in_specs=[
            pl.BlockSpec((1, 2, lag_total, width), lambda j: (j, 0, 0, 0)),
            pl.BlockSpec((1, 2, seg_count, width), lambda j: (j, 0, 0, 0)),
            pl.BlockSpec((1, 2, tmpl_local, width), lambda j: (j, 0, 0, 0)),
        ],
        out_specs=pl.BlockSpec((seg_count, 2 * lag_total, tmpl_local), lambda j: (0, 0, 0)),
        scratch_shapes=[pltpu.VMEM((2 * rows, width), jnp.bfloat16)],
        compiler_params=pltpu.CompilerParams(dimension_semantics=("arbitrary",)),
        cost_estimate=pl.CostEstimate(flops=flops, transcendentals=0, bytes_accessed=moved),
    )(phases, data, masked)


def on_device(strain, psd, templates, cutoffs, lags):
    freq_count = lax.axis_size(FREQ)
    freq_index = lax.axis_index(FREQ)
    seg_local = strain.shape[0]
    step_time = B // freq_count
    highest = lax.Precision.HIGHEST
    first_cos, first_sin = cos_sin_table(
        jnp.arange(A, dtype=jnp.int32), jnp.arange(A, dtype=jnp.int32), A
    )
    first_table = jnp.concatenate([first_cos, -first_sin], axis=0)
    time_ids = freq_index * step_time + jnp.arange(step_time, dtype=jnp.int32)
    twist_cos, twist_sin = cos_sin_table(jnp.arange(A, dtype=jnp.int32), time_ids, LEN)
    slab_blocks = strain.reshape(seg_local, A // freq_count, B)
    both_parts = jnp.einsum(
        "kn,snb->skb",
        first_table,
        lax.all_to_all(slab_blocks, FREQ, split_axis=2, concat_axis=1, tiled=True),
        precision=highest,
    )
    half_rows = first_table.shape[0] // 2
    real_part = both_parts[:, :half_rows]
    imag_part = both_parts[:, half_rows:]
    second_cos, second_sin = cos_sin_table(
        jnp.arange(B, dtype=jnp.int32), jnp.arange(NB, dtype=jnp.int32), B
    )
    rotation = jnp.concatenate(
        [
            jnp.concatenate([second_cos, -second_sin], axis=1),
            jnp.concatenate([second_sin, second_cos], axis=1),
        ],
        axis=0,
    )
    amplitude = jnp.sqrt(LEN * psd)
    real_in = lax.all_to_all(
        real_part * twist_cos + imag_part * twist_sin,
        FREQ,
        split_axis=1,
        concat_axis=2,
        tiled=True,
    )
    imag_in = lax.all_to_all(
        imag_part * twist_cos - real_part * twist_sin,
        FREQ,
        split_axis=1,
        concat_axis=2,
        tiled=True,
    )
    joined = jnp.concatenate([real_in, imag_in], axis=2)
    both_out = jnp.einsum("spc,cm->smp", joined, rotation, precision=highest)
    both_out = both_out.reshape(joined.shape[0], 2, NB, joined.shape[1])
    whitened = (both_out / amplitude).astype(jnp.bfloat16)
    local_data = lax.all_to_all(whitened, FREQ, split_axis=2, concat_axis=3, tiled=True)
    first_block = freq_index * (NB // freq_count)
    seg_piece = lax.all_gather(local_data, "tmpl", axis=0, tiled=True)
    x_size, z_size, c_size = (lax.axis_size(name) for name in FREQ)
    seg_order = seg_piece.reshape((x_size, z_size, c_size) + seg_piece.shape[1:])
    seg_order = seg_order.transpose(2, 1, 0, 3, 4, 5).reshape(seg_piece.shape)
    partial_sums = intersect(seg_order, templates, cutoffs, lags, first_block)
    for name in ("fc", "fz", "fx"):
        partial_sums = lax.psum_scatter(partial_sums, name, scatter_dimension=0, tiled=True)
    return partial_sums


def solution(mesh):
    tmpl_size, freq_size = mesh.devices.shape
    split = Mesh(
        mesh.devices.reshape(tmpl_size, 4, freq_size // 8, 2), ("tmpl",) + FREQ
    )
    placed = (P("tmpl", FREQ), P(None, FREQ), P("tmpl", None, FREQ, None), P("tmpl"), P())
    return jax.shard_map(
        on_device, mesh=split, in_specs=placed, out_specs=P(FREQ, None, "tmpl"), check_vma=False
    )
```

```python
import math

import jax
import jax.numpy as jnp
from jax import lax
from jax.experimental import pallas as pl
from jax.experimental.pallas import tpu as pltpu
from jax.sharding import Mesh, PartitionSpec as P

A = 512
B = 1024
LEN = 524288
NB = 512


two_pi = 2.0 * math.pi
FREQ = ("fx", "fz", "fc")


def cos_sin_table(row_ids, col_ids, modulus):
    product = row_ids[:, None] * col_ids[None, :] % modulus
    phase_angle = product.astype(jnp.float32) * (two_pi / modulus)
    return (jnp.cos(phase_angle), jnp.sin(phase_angle))


def intersect_kernel(ph_ref, dat_ref, tm_ref, out_ref, lhs_ref):
    step = pl.program_id(0)
    seg_count = dat_ref.shape[2]
    lag_total = ph_ref.shape[2]
    rows = seg_count * lag_total
    chunk = 8

    @pl.when(step == 0)
    def _():
        out_ref[...] = jnp.zeros_like(out_ref)

    lag_cos = ph_ref[0, 0][None]
    lag_sin = ph_ref[0, 1][None]

    def build(i, carry):
        s0 = pl.multiple_of(i * chunk, chunk)
        data_real = dat_ref[0, 0, pl.ds(s0, chunk), :].astype(jnp.float32)[:, None, :]
        data_imag = dat_ref[0, 1, pl.ds(s0, chunk), :].astype(jnp.float32)[:, None, :]
        real_q = data_real * lag_cos - data_imag * lag_sin
        imag_q = data_real * lag_sin + data_imag * lag_cos
        r0 = pl.multiple_of(i * chunk * lag_total, chunk * lag_total)
        lhs_ref[pl.ds(r0, chunk * lag_total), :] = real_q.reshape(chunk * lag_total, -1).astype(jnp.bfloat16)
        lhs_ref[pl.ds(rows + r0, chunk * lag_total), :] = imag_q.reshape(chunk * lag_total, -1).astype(jnp.bfloat16)
        return carry

    lax.fori_loop(0, seg_count // chunk, build, 0)
    dims = (((1,), (1,)), ((), ()))
    lhs = lhs_ref[...]
    with_re = lax.dot_general(lhs, tm_ref[0, 0], dims, preferred_element_type=jnp.float32)
    with_im = lax.dot_general(lhs, tm_ref[0, 1], dims, preferred_element_type=jnp.float32)
    real_sum = with_re[:rows] + with_im[rows:]
    imag_sum = with_re[rows:] - with_im[:rows]
    width = real_sum.shape[1]
    out_ref[:, 0:lag_total, :] += real_sum.reshape(seg_count, lag_total, width)
    out_ref[:, lag_total:, :] += imag_sum.reshape(seg_count, lag_total, width)


def intersect(seg_piece, templates, cutoffs, lags, first_block):
    seg_count, _, blocks_here, width = seg_piece.shape
    tmpl_local = templates.shape[0]
    lag_total = lags.shape[0]
    block_ids = first_block + jnp.arange(blocks_here, dtype=jnp.int32)
    position = jnp.arange(width, dtype=jnp.int32)
    phase_int = (A * (lags[:, None] * block_ids[None, :] % B))[:, :, None] + (
        lags[:, None] * position[None, :] % LEN
    )[:, None, :]
    phase_angle = (phase_int % LEN).astype(jnp.float32) * (two_pi / LEN)
    phases = jnp.stack([jnp.cos(phase_angle), jnp.sin(phase_angle)], axis=0).transpose(2, 0, 1, 3)
    keep = block_ids[None, None, :, None] < cutoffs[:, None, None, None]
    masked = jnp.where(keep, templates, jnp.zeros_like(templates)).transpose(2, 1, 0, 3)
    data = seg_piece.transpose(2, 1, 0, 3)
    rows = seg_count * lag_total
    flops = 2 * 2 * (2 * rows) * width * tmpl_local * blocks_here
    moved = masked.size * 2 + data.size * 2 + phases.size * 4 + seg_count * 2 * lag_total * tmpl_local * 4
    return pl.pallas_call(
        intersect_kernel,
        out_shape=jax.ShapeDtypeStruct((seg_count, 2 * lag_total, tmpl_local), jnp.float32),
        grid=(blocks_here,),
        in_specs=[
            pl.BlockSpec((1, 2, lag_total, width), lambda j: (j, 0, 0, 0)),
            pl.BlockSpec((1, 2, seg_count, width), lambda j: (j, 0, 0, 0)),
            pl.BlockSpec((1, 2, tmpl_local, width), lambda j: (j, 0, 0, 0)),
        ],
        out_specs=pl.BlockSpec((seg_count, 2 * lag_total, tmpl_local), lambda j: (0, 0, 0)),
        scratch_shapes=[pltpu.VMEM((2 * rows, width), jnp.bfloat16)],
        compiler_params=pltpu.CompilerParams(dimension_semantics=("arbitrary",)),
        cost_estimate=pl.CostEstimate(flops=flops, transcendentals=0, bytes_accessed=moved),
    )(phases, data, masked)


def on_device(strain, psd, templates, cutoffs, lags):
    freq_count = lax.axis_size(FREQ)
    freq_index = lax.axis_index(FREQ)
    seg_local = strain.shape[0]
    step_time = B // freq_count
    highest = lax.Precision.HIGHEST
    first_cos, first_sin = cos_sin_table(
        jnp.arange(A, dtype=jnp.int32), jnp.arange(A, dtype=jnp.int32), A
    )
    first_table = jnp.concatenate([first_cos, -first_sin], axis=0)
    time_ids = freq_index * step_time + jnp.arange(step_time, dtype=jnp.int32)
    twist_cos, twist_sin = cos_sin_table(jnp.arange(A, dtype=jnp.int32), time_ids, LEN)
    slab_blocks = strain.reshape(seg_local, A // freq_count, B)
    both_parts = jnp.einsum(
        "kn,snb->skb",
        first_table,
        lax.all_to_all(slab_blocks, FREQ, split_axis=2, concat_axis=1, tiled=True),
        precision=highest,
    )
    half_rows = first_table.shape[0] // 2
    real_part = both_parts[:, :half_rows]
    imag_part = both_parts[:, half_rows:]
    second_cos, second_sin = cos_sin_table(
        jnp.arange(B, dtype=jnp.int32), jnp.arange(NB, dtype=jnp.int32), B
    )
    rotation = jnp.concatenate(
        [
            jnp.concatenate([second_cos, -second_sin], axis=1),
            jnp.concatenate([second_sin, second_cos], axis=1),
        ],
        axis=0,
    )
    amplitude = jnp.sqrt(LEN * psd)
    twisted = jnp.stack(
        [real_part * twist_cos + imag_part * twist_sin, imag_part * twist_cos - real_part * twist_sin],
        axis=2,
    )
    joined = lax.all_to_all(twisted, FREQ, split_axis=1, concat_axis=3, tiled=True)
    joined = joined.reshape(joined.shape[0], joined.shape[1], -1)
    both_out = jnp.einsum("spc,cm->smp", joined, rotation, precision=highest)
    both_out = both_out.reshape(joined.shape[0], 2, NB, joined.shape[1])
    whitened = (both_out / amplitude).astype(jnp.bfloat16)
    local_data = lax.all_to_all(whitened, FREQ, split_axis=2, concat_axis=3, tiled=True)
    first_block = freq_index * (NB // freq_count)
    seg_piece = lax.all_gather(local_data, "tmpl", axis=0, tiled=True)
    x_size, z_size, c_size = (lax.axis_size(name) for name in FREQ)
    seg_order = seg_piece.reshape((x_size, z_size, c_size) + seg_piece.shape[1:])
    seg_order = seg_order.transpose(2, 1, 0, 3, 4, 5).reshape(seg_piece.shape)
    partial_sums = intersect(seg_order, templates, cutoffs, lags, first_block)
    for name in ("fc", ("fz", "fx")):
        partial_sums = lax.psum_scatter(partial_sums, name, scatter_dimension=0, tiled=True)
    return partial_sums


def solution(mesh):
    tmpl_size, freq_size = mesh.devices.shape
    split = Mesh(
        mesh.devices.reshape(tmpl_size, 4, freq_size // 8, 2), ("tmpl",) + FREQ
    )
    placed = (P("tmpl", FREQ), P(None, FREQ), P("tmpl", None, FREQ, None), P("tmpl"), P())
    return jax.shard_map(
        on_device, mesh=split, in_specs=placed, out_specs=P(FREQ, None, "tmpl"), check_vma=False
    )
```

```python
import functools
import math

import jax
import jax.numpy as jnp
from jax import lax
from jax.experimental import pallas as pl
from jax.experimental.pallas import tpu as pltpu
from jax.sharding import Mesh, PartitionSpec as P

A = 512
B = 1024
LEN = 524288
NB = 512


two_pi = 2.0 * math.pi
FREQ = ("fx", "fz", "fc")


def cos_sin_table(row_ids, col_ids, modulus):
    product = row_ids[:, None] * col_ids[None, :] % modulus
    phase_angle = product.astype(jnp.float32) * (two_pi / modulus)
    return (jnp.cos(phase_angle), jnp.sin(phase_angle))


def intersect_kernel(ph_ref, dat_ref, tm_ref, out_ref, lhs_ref):
    step = pl.program_id(0)
    seg_count = dat_ref.shape[2]
    lag_total = ph_ref.shape[2]
    rows = seg_count * lag_total
    chunk = 8

    @pl.when(step == 0)
    def _():
        out_ref[...] = jnp.zeros_like(out_ref)

    lag_cos = ph_ref[0, 0][None]
    lag_sin = ph_ref[0, 1][None]

    def build(i, carry):
        s0 = pl.multiple_of(i * chunk, chunk)
        data_real = dat_ref[0, 0, pl.ds(s0, chunk), :].astype(jnp.float32)[:, None, :]
        data_imag = dat_ref[0, 1, pl.ds(s0, chunk), :].astype(jnp.float32)[:, None, :]
        real_q = data_real * lag_cos - data_imag * lag_sin
        imag_q = data_real * lag_sin + data_imag * lag_cos
        r0 = pl.multiple_of(i * chunk * lag_total, chunk * lag_total)
        lhs_ref[pl.ds(r0, chunk * lag_total), :] = real_q.reshape(chunk * lag_total, -1).astype(jnp.bfloat16)
        lhs_ref[pl.ds(rows + r0, chunk * lag_total), :] = imag_q.reshape(chunk * lag_total, -1).astype(jnp.bfloat16)
        return carry

    lax.fori_loop(0, seg_count // chunk, build, 0)
    dims = (((1,), (1,)), ((), ()))
    lhs = lhs_ref[...]
    with_re = lax.dot_general(lhs, tm_ref[0, 0], dims, preferred_element_type=jnp.float32)
    with_im = lax.dot_general(lhs, tm_ref[0, 1], dims, preferred_element_type=jnp.float32)
    real_sum = with_re[:rows] + with_im[rows:]
    imag_sum = with_re[rows:] - with_im[:rows]
    width = real_sum.shape[1]
    out_ref[:, 0:lag_total, :] += real_sum.reshape(seg_count, lag_total, width)
    out_ref[:, lag_total:, :] += imag_sum.reshape(seg_count, lag_total, width)


def intersect(seg_piece, templates, cutoffs, lags, first_block):
    seg_count, _, blocks_here, width = seg_piece.shape
    tmpl_local = templates.shape[0]
    lag_total = lags.shape[0]
    block_ids = first_block + jnp.arange(blocks_here, dtype=jnp.int32)
    position = jnp.arange(width, dtype=jnp.int32)
    phase_int = (A * (lags[:, None] * block_ids[None, :] % B))[:, :, None] + (
        lags[:, None] * position[None, :] % LEN
    )[:, None, :]
    phase_angle = (phase_int % LEN).astype(jnp.float32) * (two_pi / LEN)
    phases = jnp.stack([jnp.cos(phase_angle), jnp.sin(phase_angle)], axis=0).transpose(2, 0, 1, 3)
    keep = block_ids[None, None, :, None] < cutoffs[:, None, None, None]
    masked = jnp.where(keep, templates, jnp.zeros_like(templates)).transpose(2, 1, 0, 3)
    data = seg_piece.transpose(2, 1, 0, 3)
    rows = seg_count * lag_total
    flops = 2 * 2 * (2 * rows) * width * tmpl_local * blocks_here
    moved = masked.size * 2 + data.size * 2 + phases.size * 4 + seg_count * 2 * lag_total * tmpl_local * 4
    return pl.pallas_call(
        intersect_kernel,
        out_shape=jax.ShapeDtypeStruct((seg_count, 2 * lag_total, tmpl_local), jnp.float32),
        grid=(blocks_here,),
        in_specs=[
            pl.BlockSpec((1, 2, lag_total, width), lambda j: (j, 0, 0, 0)),
            pl.BlockSpec((1, 2, seg_count, width), lambda j: (j, 0, 0, 0)),
            pl.BlockSpec((1, 2, tmpl_local, width), lambda j: (j, 0, 0, 0)),
        ],
        out_specs=pl.BlockSpec((seg_count, 2 * lag_total, tmpl_local), lambda j: (0, 0, 0)),
        scratch_shapes=[pltpu.VMEM((2 * rows, width), jnp.bfloat16)],
        compiler_params=pltpu.CompilerParams(dimension_semantics=("arbitrary",)),
        cost_estimate=pl.CostEstimate(flops=flops, transcendentals=0, bytes_accessed=moved),
    )(phases, data, masked)


def scatter_kernel(axis, size, x_ref, o_ref, recv_ref, send_sem, recv_sem):
    me = lax.axis_index(axis)
    piece = o_ref.shape[0]
    mesh_ids = pl.DeviceIdType.MESH
    barrier = pltpu.get_barrier_semaphore()
    for k in range(1, size):
        peer = lax.rem(me + k, size)
        pl.semaphore_signal(barrier, inc=1, device_id={axis: peer}, device_id_type=mesh_ids)
    pl.semaphore_wait(barrier, size - 1)
    copies = []
    for k in range(1, size):
        peer = lax.rem(me + k, size)
        copy = pltpu.make_async_remote_copy(
            src_ref=x_ref.at[pl.ds(peer * piece, piece)],
            dst_ref=recv_ref.at[k],
            send_sem=send_sem.at[k],
            recv_sem=recv_sem.at[k],
            device_id={axis: peer},
            device_id_type=mesh_ids,
        )
        copy.start()
        copies.append(copy)
    for copy in copies:
        copy.wait()
    total = x_ref[pl.ds(me * piece, piece)]
    for k in range(1, size):
        total = total + recv_ref[k]
    o_ref[...] = total


def scatter_sum(parts, axis, collective_id):
    size = lax.axis_size(axis)
    piece = parts.shape[0] // size
    out_shape = (piece,) + parts.shape[1:]
    vmem = pltpu.VMEM
    return pl.pallas_call(
        functools.partial(scatter_kernel, axis, size),
        out_shape=jax.ShapeDtypeStruct(out_shape, parts.dtype),
        in_specs=[pl.BlockSpec(memory_space=vmem)],
        out_specs=pl.BlockSpec(memory_space=vmem),
        scratch_shapes=[
            vmem((size,) + out_shape, parts.dtype),
            pltpu.SemaphoreType.DMA((size,)),
            pltpu.SemaphoreType.DMA((size,)),
        ],
        compiler_params=pltpu.CompilerParams(collective_id=collective_id, has_side_effects=True),
    )(parts)


def on_device(strain, psd, templates, cutoffs, lags):
    freq_count = lax.axis_size(FREQ)
    freq_index = lax.axis_index(FREQ)
    seg_local = strain.shape[0]
    step_time = B // freq_count
    highest = lax.Precision.HIGHEST
    first_cos, first_sin = cos_sin_table(
        jnp.arange(A, dtype=jnp.int32), jnp.arange(A, dtype=jnp.int32), A
    )
    first_table = jnp.concatenate([first_cos, -first_sin], axis=0)
    time_ids = freq_index * step_time + jnp.arange(step_time, dtype=jnp.int32)
    twist_cos, twist_sin = cos_sin_table(jnp.arange(A, dtype=jnp.int32), time_ids, LEN)
    slab_blocks = strain.reshape(seg_local, A // freq_count, B)
    both_parts = jnp.einsum(
        "kn,snb->skb",
        first_table,
        lax.all_to_all(slab_blocks, FREQ, split_axis=2, concat_axis=1, tiled=True),
        precision=highest,
    )
    half_rows = first_table.shape[0] // 2
    real_part = both_parts[:, :half_rows]
    imag_part = both_parts[:, half_rows:]
    second_cos, second_sin = cos_sin_table(
        jnp.arange(B, dtype=jnp.int32), jnp.arange(NB, dtype=jnp.int32), B
    )
    rotation = jnp.concatenate(
        [
            jnp.concatenate([second_cos, -second_sin], axis=1),
            jnp.concatenate([second_sin, second_cos], axis=1),
        ],
        axis=0,
    )
    amplitude = jnp.sqrt(LEN * psd)
    twisted = jnp.stack(
        [real_part * twist_cos + imag_part * twist_sin, imag_part * twist_cos - real_part * twist_sin],
        axis=2,
    )
    joined = lax.all_to_all(twisted, FREQ, split_axis=1, concat_axis=3, tiled=True)
    joined = joined.reshape(joined.shape[0], joined.shape[1], -1)
    both_out = jnp.einsum("spc,cm->smp", joined, rotation, precision=highest)
    both_out = both_out.reshape(joined.shape[0], 2, NB, joined.shape[1])
    whitened = (both_out / amplitude).astype(jnp.bfloat16)
    local_data = lax.all_to_all(whitened, FREQ, split_axis=2, concat_axis=3, tiled=True)
    first_block = freq_index * (NB // freq_count)
    seg_piece = lax.all_gather(local_data, "tmpl", axis=0, tiled=True)
    x_size, z_size, c_size = (lax.axis_size(name) for name in FREQ)
    seg_order = seg_piece.reshape((x_size, z_size, c_size) + seg_piece.shape[1:])
    seg_order = seg_order.transpose(2, 1, 0, 3, 4, 5).reshape(seg_piece.shape)
    partial_sums = intersect(seg_order, templates, cutoffs, lags, first_block)
    for collective_id, name in enumerate(("fc", "fz", "fx")):
        partial_sums = scatter_sum(partial_sums, name, collective_id + 1)
    return partial_sums


def solution(mesh):
    tmpl_size, freq_size = mesh.devices.shape
    split = Mesh(
        mesh.devices.reshape(tmpl_size, 4, freq_size // 8, 2), ("tmpl",) + FREQ
    )
    placed = (P("tmpl", FREQ), P(None, FREQ), P("tmpl", None, FREQ, None), P("tmpl"), P())
    return jax.shard_map(
        on_device, mesh=split, in_specs=placed, out_specs=P(FREQ, None, "tmpl"), check_vma=False
    )
```

```python
import functools
import math

import jax
import jax.numpy as jnp
from jax import lax
from jax.experimental import pallas as pl
from jax.experimental.pallas import tpu as pltpu
from jax.sharding import Mesh, PartitionSpec as P

A = 512
B = 1024
LEN = 524288
NB = 512


two_pi = 2.0 * math.pi
FREQ = ("fx", "fz", "fc")


def cos_sin_table(row_ids, col_ids, modulus):
    product = row_ids[:, None] * col_ids[None, :] % modulus
    phase_angle = product.astype(jnp.float32) * (two_pi / modulus)
    return (jnp.cos(phase_angle), jnp.sin(phase_angle))


def intersect_kernel(ph_ref, dat_ref, tm_ref, out_ref, lhs_ref):
    step = pl.program_id(0)
    seg_count = dat_ref.shape[2]
    lag_total = ph_ref.shape[2]
    rows = seg_count * lag_total
    chunk = 8

    @pl.when(step == 0)
    def _():
        out_ref[...] = jnp.zeros_like(out_ref)

    lag_cos = ph_ref[0, 0][None]
    lag_sin = ph_ref[0, 1][None]

    def build(i, carry):
        s0 = pl.multiple_of(i * chunk, chunk)
        data_real = dat_ref[0, 0, pl.ds(s0, chunk), :].astype(jnp.float32)[:, None, :]
        data_imag = dat_ref[0, 1, pl.ds(s0, chunk), :].astype(jnp.float32)[:, None, :]
        real_q = data_real * lag_cos - data_imag * lag_sin
        imag_q = data_real * lag_sin + data_imag * lag_cos
        r0 = pl.multiple_of(i * chunk * lag_total, chunk * lag_total)
        lhs_ref[pl.ds(r0, chunk * lag_total), :] = real_q.reshape(chunk * lag_total, -1).astype(jnp.bfloat16)
        lhs_ref[pl.ds(rows + r0, chunk * lag_total), :] = imag_q.reshape(chunk * lag_total, -1).astype(jnp.bfloat16)
        return carry

    lax.fori_loop(0, seg_count // chunk, build, 0)
    dims = (((1,), (1,)), ((), ()))
    lhs = lhs_ref[...]
    with_re = lax.dot_general(lhs, tm_ref[0, 0], dims, preferred_element_type=jnp.float32)
    with_im = lax.dot_general(lhs, tm_ref[0, 1], dims, preferred_element_type=jnp.float32)
    real_sum = with_re[:rows] + with_im[rows:]
    imag_sum = with_re[rows:] - with_im[:rows]
    width = real_sum.shape[1]
    out_ref[:, 0:lag_total, :] += real_sum.reshape(seg_count, lag_total, width)
    out_ref[:, lag_total:, :] += imag_sum.reshape(seg_count, lag_total, width)


def intersect(data, templates, cutoffs, lags, first_block):
    blocks_here, _, seg_count, width = data.shape
    tmpl_local = templates.shape[0]
    lag_total = lags.shape[0]
    block_ids = first_block + jnp.arange(blocks_here, dtype=jnp.int32)
    position = jnp.arange(width, dtype=jnp.int32)
    phase_int = (A * (lags[:, None] * block_ids[None, :] % B))[:, :, None] + (
        lags[:, None] * position[None, :] % LEN
    )[:, None, :]
    phase_angle = (phase_int % LEN).astype(jnp.float32) * (two_pi / LEN)
    phases = jnp.stack([jnp.cos(phase_angle), jnp.sin(phase_angle)], axis=0).transpose(2, 0, 1, 3)
    keep = block_ids[None, None, :, None] < cutoffs[:, None, None, None]
    masked = jnp.where(keep, templates, jnp.zeros_like(templates)).transpose(2, 1, 0, 3)
    rows = seg_count * lag_total
    flops = 2 * 2 * (2 * rows) * width * tmpl_local * blocks_here
    moved = masked.size * 2 + data.size * 2 + phases.size * 4 + seg_count * 2 * lag_total * tmpl_local * 4
    return pl.pallas_call(
        intersect_kernel,
        out_shape=jax.ShapeDtypeStruct((seg_count, 2 * lag_total, tmpl_local), jnp.float32),
        grid=(blocks_here,),
        in_specs=[
            pl.BlockSpec((1, 2, lag_total, width), lambda j: (j, 0, 0, 0)),
            pl.BlockSpec((1, 2, seg_count, width), lambda j: (j, 0, 0, 0)),
            pl.BlockSpec((1, 2, tmpl_local, width), lambda j: (j, 0, 0, 0)),
        ],
        out_specs=pl.BlockSpec((seg_count, 2 * lag_total, tmpl_local), lambda j: (0, 0, 0)),
        scratch_shapes=[pltpu.VMEM((2 * rows, width), jnp.bfloat16)],
        compiler_params=pltpu.CompilerParams(dimension_semantics=("arbitrary",)),
        cost_estimate=pl.CostEstimate(flops=flops, transcendentals=0, bytes_accessed=moved),
    )(phases, data, masked)


def scatter_kernel(axis, size, x_ref, o_ref, recv_ref, send_sem, recv_sem):
    me = lax.axis_index(axis)
    piece = o_ref.shape[0]
    mesh_ids = pl.DeviceIdType.MESH
    barrier = pltpu.get_barrier_semaphore()
    for k in range(1, size):
        peer = lax.rem(me + k, size)
        pl.semaphore_signal(barrier, inc=1, device_id={axis: peer}, device_id_type=mesh_ids)
    pl.semaphore_wait(barrier, size - 1)
    copies = []
    for k in range(1, size):
        peer = lax.rem(me + k, size)
        copy = pltpu.make_async_remote_copy(
            src_ref=x_ref.at[pl.ds(peer * piece, piece)],
            dst_ref=recv_ref.at[k],
            send_sem=send_sem.at[k],
            recv_sem=recv_sem.at[k],
            device_id={axis: peer},
            device_id_type=mesh_ids,
        )
        copy.start()
        copies.append(copy)
    for copy in copies:
        copy.wait()
    total = x_ref[pl.ds(me * piece, piece)]
    for k in range(1, size):
        total = total + recv_ref[k]
    o_ref[...] = total


def scatter_sum(parts, axis, collective_id):
    size = lax.axis_size(axis)
    piece = parts.shape[0] // size
    out_shape = (piece,) + parts.shape[1:]
    vmem = pltpu.VMEM
    return pl.pallas_call(
        functools.partial(scatter_kernel, axis, size),
        out_shape=jax.ShapeDtypeStruct(out_shape, parts.dtype),
        in_specs=[pl.BlockSpec(memory_space=vmem)],
        out_specs=pl.BlockSpec(memory_space=vmem),
        scratch_shapes=[
            vmem((size,) + out_shape, parts.dtype),
            pltpu.SemaphoreType.DMA((size,)),
            pltpu.SemaphoreType.DMA((size,)),
        ],
        compiler_params=pltpu.CompilerParams(collective_id=collective_id, has_side_effects=True),
    )(parts)


def spectrum_blocks(strain, psd):
    freq_count = lax.axis_size(FREQ)
    freq_index = lax.axis_index(FREQ)
    seg_local = strain.shape[0]
    rows_here = A // freq_count
    cols_here = B // freq_count
    highest = lax.Precision.HIGHEST
    first_cos, first_sin = cos_sin_table(
        jnp.arange(A, dtype=jnp.int32), jnp.arange(A, dtype=jnp.int32), A
    )
    first_table = jnp.concatenate([first_cos, -first_sin], axis=0)
    sent = strain.reshape(seg_local, rows_here, freq_count, cols_here).transpose(2, 1, 3, 0)
    sent = sent.reshape(freq_count, rows_here, cols_here * seg_local)
    slab = lax.all_to_all(sent, FREQ, 0, 0, tiled=True).reshape(A, cols_here * seg_local)
    both_parts = jnp.dot(first_table, slab, precision=highest)
    real_part = both_parts[:A]
    imag_part = both_parts[A:]
    time_ids = freq_index * cols_here + jnp.arange(cols_here, dtype=jnp.int32)
    twist_cos, twist_sin = cos_sin_table(jnp.arange(A, dtype=jnp.int32), time_ids, LEN)
    twist_cos = jnp.repeat(twist_cos, seg_local, axis=1)
    twist_sin = jnp.repeat(twist_sin, seg_local, axis=1)
    twisted = jnp.stack(
        [real_part * twist_cos + imag_part * twist_sin, imag_part * twist_cos - real_part * twist_sin]
    )
    p_here = A // freq_count
    twisted = twisted.reshape(2, freq_count, p_here, cols_here, seg_local).transpose(1, 3, 0, 2, 4)
    twisted = twisted.reshape(freq_count, cols_here, 2 * p_here * seg_local)
    columns = lax.all_to_all(twisted, FREQ, 0, 0, tiled=True).reshape(B, 2 * p_here * seg_local)
    second_cos, second_sin = cos_sin_table(
        jnp.arange(NB, dtype=jnp.int32), jnp.arange(B, dtype=jnp.int32), B
    )
    with_cos = jnp.dot(second_cos, columns, precision=highest).reshape(NB, 2, p_here, seg_local)
    with_sin = jnp.dot(second_sin, columns, precision=highest).reshape(NB, 2, p_here, seg_local)
    amplitude = jnp.sqrt(LEN * psd)[:, :, None]
    real_out = (with_cos[:, 0] + with_sin[:, 1]) / amplitude
    imag_out = (with_cos[:, 1] - with_sin[:, 0]) / amplitude
    whitened = jnp.stack([real_out, imag_out], axis=1).astype(jnp.bfloat16)
    j_here = NB // freq_count
    whitened = whitened.reshape(freq_count, j_here, 2, p_here, seg_local)
    return lax.all_to_all(whitened, FREQ, 0, 0, tiled=True)


def on_device(strain, psd, templates, cutoffs, lags):
    freq_index = lax.axis_index(FREQ)
    received = spectrum_blocks(strain, psd)
    freq_count, j_here, _, p_here, seg_local = received.shape
    gathered = lax.all_gather(received, "tmpl", axis=0)
    tmpl_count = gathered.shape[0]
    x_size, z_size, c_size = (lax.axis_size(name) for name in FREQ)
    data = gathered.transpose(2, 3, 0, 5, 1, 4).reshape(
        j_here, 2, x_size, z_size, c_size, freq_count * p_here
    )
    data = data.transpose(0, 1, 4, 3, 2, 5).reshape(j_here, 2, tmpl_count * seg_local, -1)
    first_block = freq_index * j_here
    partial_sums = intersect(data, templates, cutoffs, lags, first_block)
    for collective_id, name in enumerate(("fc", "fz", "fx")):
        partial_sums = scatter_sum(partial_sums, name, collective_id + 1)
    return partial_sums


def solution(mesh):
    tmpl_size, freq_size = mesh.devices.shape
    split = Mesh(
        mesh.devices.reshape(tmpl_size, 4, freq_size // 8, 2), ("tmpl",) + FREQ
    )
    placed = (P("tmpl", FREQ), P(None, FREQ), P("tmpl", None, FREQ, None), P("tmpl"), P())
    return jax.shard_map(
        on_device, mesh=split, in_specs=placed, out_specs=P(FREQ, None, "tmpl"), check_vma=False
    )
```

```python
import functools
import math

import jax
import jax.numpy as jnp
from jax import lax
from jax.experimental import pallas as pl
from jax.experimental.pallas import tpu as pltpu
from jax.sharding import Mesh, PartitionSpec as P

A = 512
B = 1024
LEN = 524288
NB = 512


two_pi = 2.0 * math.pi
FREQ = ("fx", "fz", "fc")


def cos_sin_table(row_ids, col_ids, modulus):
    product = row_ids[:, None] * col_ids[None, :] % modulus
    phase_angle = product.astype(jnp.float32) * (two_pi / modulus)
    return (jnp.cos(phase_angle), jnp.sin(phase_angle))


def intersect_kernel(ph_ref, dat_ref, tm_ref, out_ref, lhs_ref):
    step = pl.program_id(0)
    seg_count = dat_ref.shape[2]
    lag_total = ph_ref.shape[2]
    rows = seg_count * lag_total
    chunk = 8

    @pl.when(step == 0)
    def _():
        out_ref[...] = jnp.zeros_like(out_ref)

    lag_cos = ph_ref[0, 0][None]
    lag_sin = ph_ref[0, 1][None]

    def build(i, carry):
        s0 = pl.multiple_of(i * chunk, chunk)
        data_real = dat_ref[0, 0, pl.ds(s0, chunk), :].astype(jnp.float32)[:, None, :]
        data_imag = dat_ref[0, 1, pl.ds(s0, chunk), :].astype(jnp.float32)[:, None, :]
        real_q = data_real * lag_cos - data_imag * lag_sin
        imag_q = data_real * lag_sin + data_imag * lag_cos
        r0 = pl.multiple_of(i * chunk * lag_total, chunk * lag_total)
        lhs_ref[pl.ds(r0, chunk * lag_total), :] = real_q.reshape(chunk * lag_total, -1).astype(jnp.bfloat16)
        lhs_ref[pl.ds(rows + r0, chunk * lag_total), :] = imag_q.reshape(chunk * lag_total, -1).astype(jnp.bfloat16)
        return carry

    lax.fori_loop(0, seg_count // chunk, build, 0)
    dims = (((1,), (1,)), ((), ()))
    lhs = lhs_ref[...]
    with_re = lax.dot_general(lhs, tm_ref[0, 0], dims, preferred_element_type=jnp.float32)
    with_im = lax.dot_general(lhs, tm_ref[0, 1], dims, preferred_element_type=jnp.float32)
    real_sum = with_re[:rows] + with_im[rows:]
    imag_sum = with_re[rows:] - with_im[:rows]
    width = real_sum.shape[1]
    out_ref[:, 0:lag_total, :] += real_sum.reshape(seg_count, lag_total, width)
    out_ref[:, lag_total:, :] += imag_sum.reshape(seg_count, lag_total, width)


def intersect(data, templates, cutoffs, lags, first_block):
    blocks_here, _, seg_count, width = data.shape
    tmpl_local = templates.shape[0]
    lag_total = lags.shape[0]
    block_ids = first_block + jnp.arange(blocks_here, dtype=jnp.int32)
    position = jnp.arange(width, dtype=jnp.int32)
    phase_int = (A * (lags[:, None] * block_ids[None, :] % B))[:, :, None] + (
        lags[:, None] * position[None, :] % LEN
    )[:, None, :]
    phase_angle = (phase_int % LEN).astype(jnp.float32) * (two_pi / LEN)
    phases = jnp.stack([jnp.cos(phase_angle), jnp.sin(phase_angle)], axis=0).transpose(2, 0, 1, 3)
    keep = block_ids[None, None, :, None] < cutoffs[:, None, None, None]
    masked = jnp.where(keep, templates, jnp.zeros_like(templates)).transpose(2, 1, 0, 3)
    rows = seg_count * lag_total
    flops = 2 * 2 * (2 * rows) * width * tmpl_local * blocks_here
    moved = masked.size * 2 + data.size * 2 + phases.size * 4 + seg_count * 2 * lag_total * tmpl_local * 4
    return pl.pallas_call(
        intersect_kernel,
        out_shape=jax.ShapeDtypeStruct((seg_count, 2 * lag_total, tmpl_local), jnp.float32),
        grid=(blocks_here,),
        in_specs=[
            pl.BlockSpec((1, 2, lag_total, width), lambda j: (j, 0, 0, 0)),
            pl.BlockSpec((1, 2, seg_count, width), lambda j: (j, 0, 0, 0)),
            pl.BlockSpec((1, 2, tmpl_local, width), lambda j: (j, 0, 0, 0)),
        ],
        out_specs=pl.BlockSpec((seg_count, 2 * lag_total, tmpl_local), lambda j: (0, 0, 0)),
        scratch_shapes=[pltpu.VMEM((2 * rows, width), jnp.bfloat16)],
        compiler_params=pltpu.CompilerParams(dimension_semantics=("arbitrary",)),
        cost_estimate=pl.CostEstimate(flops=flops, transcendentals=0, bytes_accessed=moved),
    )(phases, data, masked)


def scatter_kernel(axis, size, x_ref, o_ref, recv_ref, send_sem, recv_sem):
    me = lax.axis_index(axis)
    piece = o_ref.shape[0]
    mesh_ids = pl.DeviceIdType.MESH
    barrier = pltpu.get_barrier_semaphore()
    for k in range(1, size):
        peer = lax.rem(me + k, size)
        pl.semaphore_signal(barrier, inc=1, device_id={axis: peer}, device_id_type=mesh_ids)
    pl.semaphore_wait(barrier, size - 1)
    copies = []
    for k in range(1, size):
        peer = lax.rem(me + k, size)
        copy = pltpu.make_async_remote_copy(
            src_ref=x_ref.at[pl.ds(peer * piece, piece)],
            dst_ref=recv_ref.at[k],
            send_sem=send_sem.at[k],
            recv_sem=recv_sem.at[k],
            device_id={axis: peer},
            device_id_type=mesh_ids,
        )
        copy.start()
        copies.append(copy)
    for copy in copies:
        copy.wait()
    total = x_ref[pl.ds(me * piece, piece)]
    for k in range(1, size):
        total = total + recv_ref[k]
    o_ref[...] = total


def scatter_sum(parts, axis, collective_id):
    size = lax.axis_size(axis)
    piece = parts.shape[0] // size
    out_shape = (piece,) + parts.shape[1:]
    vmem = pltpu.VMEM
    return pl.pallas_call(
        functools.partial(scatter_kernel, axis, size),
        out_shape=jax.ShapeDtypeStruct(out_shape, parts.dtype),
        in_specs=[pl.BlockSpec(memory_space=vmem)],
        out_specs=pl.BlockSpec(memory_space=vmem),
        scratch_shapes=[
            vmem((size,) + out_shape, parts.dtype),
            pltpu.SemaphoreType.DMA((size,)),
            pltpu.SemaphoreType.DMA((size,)),
        ],
        compiler_params=pltpu.CompilerParams(collective_id=collective_id, has_side_effects=True),
    )(parts)


def spectrum_blocks(strain, psd):
    freq_count = lax.axis_size(FREQ)
    freq_index = lax.axis_index(FREQ)
    seg_local = strain.shape[0]
    rows_here = A // freq_count
    cols_here = B // freq_count
    highest = lax.Precision.HIGHEST
    first_cos, first_sin = cos_sin_table(
        jnp.arange(A, dtype=jnp.int32), jnp.arange(A, dtype=jnp.int32), A
    )
    first_table = jnp.concatenate([first_cos, -first_sin], axis=0)
    sent = strain.reshape(seg_local, rows_here, freq_count, cols_here).transpose(2, 1, 3, 0)
    sent = sent.reshape(freq_count, rows_here, cols_here * seg_local)
    slab = lax.all_to_all(sent, FREQ, 0, 0, tiled=True).reshape(A, cols_here * seg_local)
    both_parts = jnp.dot(first_table, slab, precision=highest)
    real_part = both_parts[:A]
    imag_part = both_parts[A:]
    time_ids = freq_index * cols_here + jnp.arange(cols_here, dtype=jnp.int32)
    twist_cos, twist_sin = cos_sin_table(jnp.arange(A, dtype=jnp.int32), time_ids, LEN)
    twist_cos = jnp.repeat(twist_cos, seg_local, axis=1)
    twist_sin = jnp.repeat(twist_sin, seg_local, axis=1)
    twisted = jnp.stack(
        [real_part * twist_cos + imag_part * twist_sin, imag_part * twist_cos - real_part * twist_sin]
    )
    p_here = A // freq_count
    twisted = twisted.reshape(2, freq_count, p_here, cols_here, seg_local).transpose(1, 3, 0, 2, 4)
    twisted = twisted.reshape(freq_count, cols_here, 2 * p_here * seg_local)
    columns = lax.all_to_all(twisted, FREQ, 0, 0, tiled=True).reshape(B, 2 * p_here * seg_local)
    second_cos, second_sin = cos_sin_table(
        jnp.arange(NB, dtype=jnp.int32), jnp.arange(B, dtype=jnp.int32), B
    )
    with_cos = jnp.dot(second_cos, columns, precision=highest).reshape(NB, 2, p_here, seg_local)
    with_sin = jnp.dot(second_sin, columns, precision=highest).reshape(NB, 2, p_here, seg_local)
    amplitude = jnp.sqrt(LEN * psd)[:, :, None]
    real_out = (with_cos[:, 0] + with_sin[:, 1]) / amplitude
    imag_out = (with_cos[:, 1] - with_sin[:, 0]) / amplitude
    whitened = jnp.stack([real_out, imag_out], axis=1).transpose(3, 1, 0, 2).astype(jnp.bfloat16)
    return lax.all_to_all(whitened, FREQ, split_axis=2, concat_axis=3, tiled=True)


def on_device(strain, psd, templates, cutoffs, lags):
    freq_index = lax.axis_index(FREQ)
    local_data = spectrum_blocks(strain, psd)
    seg_piece = lax.all_gather(local_data, "tmpl", axis=0, tiled=True)
    x_size, z_size, c_size = (lax.axis_size(name) for name in FREQ)
    seg_order = seg_piece.reshape((x_size, z_size, c_size) + seg_piece.shape[1:])
    seg_order = seg_order.transpose(2, 1, 0, 3, 4, 5).reshape(seg_piece.shape)
    data = seg_order.transpose(2, 1, 0, 3)
    j_here = data.shape[0]
    first_block = freq_index * j_here
    partial_sums = intersect(data, templates, cutoffs, lags, first_block)
    for collective_id, name in enumerate(("fc", "fz", "fx")):
        partial_sums = scatter_sum(partial_sums, name, collective_id + 1)
    return partial_sums


def solution(mesh):
    tmpl_size, freq_size = mesh.devices.shape
    split = Mesh(
        mesh.devices.reshape(tmpl_size, 4, freq_size // 8, 2), ("tmpl",) + FREQ
    )
    placed = (P("tmpl", FREQ), P(None, FREQ), P("tmpl", None, FREQ, None), P("tmpl"), P())
    return jax.shard_map(
        on_device, mesh=split, in_specs=placed, out_specs=P(FREQ, None, "tmpl"), check_vma=False
    )
```

```python
import functools
import math

import jax
import jax.numpy as jnp
from jax import lax
from jax.experimental import pallas as pl
from jax.experimental.pallas import tpu as pltpu
from jax.sharding import Mesh, PartitionSpec as P

A = 512
B = 1024
LEN = 524288
NB = 512


two_pi = 2.0 * math.pi
FREQ = ("fx", "fz", "fc")


def cos_sin_table(row_ids, col_ids, modulus):
    product = row_ids[:, None] * col_ids[None, :] % modulus
    phase_angle = product.astype(jnp.float32) * (two_pi / modulus)
    return (jnp.cos(phase_angle), jnp.sin(phase_angle))


def intersect_kernel(ph_ref, dat_ref, tm_ref, out_ref, lhs_ref):
    step = pl.program_id(0)
    seg_count = dat_ref.shape[2]
    lag_total = ph_ref.shape[2]
    rows = seg_count * lag_total
    chunk = 8

    @pl.when(step == 0)
    def _():
        out_ref[...] = jnp.zeros_like(out_ref)

    lag_cos = ph_ref[0, 0][None]
    lag_sin = ph_ref[0, 1][None]

    def build(i, carry):
        s0 = pl.multiple_of(i * chunk, chunk)
        data_real = dat_ref[0, 0, pl.ds(s0, chunk), :].astype(jnp.float32)[:, None, :]
        data_imag = dat_ref[0, 1, pl.ds(s0, chunk), :].astype(jnp.float32)[:, None, :]
        real_q = data_real * lag_cos - data_imag * lag_sin
        imag_q = data_real * lag_sin + data_imag * lag_cos
        r0 = pl.multiple_of(i * chunk * lag_total, chunk * lag_total)
        lhs_ref[pl.ds(r0, chunk * lag_total), :] = real_q.reshape(chunk * lag_total, -1).astype(jnp.bfloat16)
        lhs_ref[pl.ds(rows + r0, chunk * lag_total), :] = imag_q.reshape(chunk * lag_total, -1).astype(jnp.bfloat16)
        return carry

    lax.fori_loop(0, seg_count // chunk, build, 0)
    dims = (((1,), (1,)), ((), ()))
    lhs = lhs_ref[...]
    with_re = lax.dot_general(lhs, tm_ref[0, 0], dims, preferred_element_type=jnp.float32)
    with_im = lax.dot_general(lhs, tm_ref[0, 1], dims, preferred_element_type=jnp.float32)
    real_sum = with_re[:rows] + with_im[rows:]
    imag_sum = with_re[rows:] - with_im[:rows]
    width = real_sum.shape[1]
    out_ref[:, 0:lag_total, :] += real_sum.reshape(seg_count, lag_total, width)
    out_ref[:, lag_total:, :] += imag_sum.reshape(seg_count, lag_total, width)


def intersect(data, templates, cutoffs, lags, first_block):
    blocks_here, _, seg_count, width = data.shape
    tmpl_local = templates.shape[0]
    lag_total = lags.shape[0]
    block_ids = first_block + jnp.arange(blocks_here, dtype=jnp.int32)
    position = jnp.arange(width, dtype=jnp.int32)
    phase_int = (A * (lags[:, None] * block_ids[None, :] % B))[:, :, None] + (
        lags[:, None] * position[None, :] % LEN
    )[:, None, :]
    phase_angle = (phase_int % LEN).astype(jnp.float32) * (two_pi / LEN)
    phases = jnp.stack([jnp.cos(phase_angle), jnp.sin(phase_angle)], axis=0).transpose(2, 0, 1, 3)
    keep = block_ids[None, None, :, None] < cutoffs[:, None, None, None]
    masked = jnp.where(keep, templates, jnp.zeros_like(templates)).transpose(2, 1, 0, 3)
    rows = seg_count * lag_total
    flops = 2 * 2 * (2 * rows) * width * tmpl_local * blocks_here
    moved = masked.size * 2 + data.size * 2 + phases.size * 4 + seg_count * 2 * lag_total * tmpl_local * 4
    return pl.pallas_call(
        intersect_kernel,
        out_shape=jax.ShapeDtypeStruct((seg_count, 2 * lag_total, tmpl_local), jnp.float32),
        grid=(blocks_here,),
        in_specs=[
            pl.BlockSpec((1, 2, lag_total, width), lambda j: (j, 0, 0, 0)),
            pl.BlockSpec((1, 2, seg_count, width), lambda j: (j, 0, 0, 0)),
            pl.BlockSpec((1, 2, tmpl_local, width), lambda j: (j, 0, 0, 0)),
        ],
        out_specs=pl.BlockSpec((seg_count, 2 * lag_total, tmpl_local), lambda j: (0, 0, 0)),
        scratch_shapes=[pltpu.VMEM((2 * rows, width), jnp.bfloat16)],
        compiler_params=pltpu.CompilerParams(dimension_semantics=("arbitrary",)),
        cost_estimate=pl.CostEstimate(flops=flops, transcendentals=0, bytes_accessed=moved),
    )(phases, data, masked)


def scatter_kernel(axis, size, x_ref, o_ref, recv_ref, send_sem, recv_sem):
    me = lax.axis_index(axis)
    piece = o_ref.shape[0]
    mesh_ids = pl.DeviceIdType.MESH
    barrier = pltpu.get_barrier_semaphore()
    for k in range(1, size):
        peer = lax.rem(me + k, size)
        pl.semaphore_signal(barrier, inc=1, device_id={axis: peer}, device_id_type=mesh_ids)
    pl.semaphore_wait(barrier, size - 1)
    copies = []
    for k in range(1, size):
        peer = lax.rem(me + k, size)
        copy = pltpu.make_async_remote_copy(
            src_ref=x_ref.at[pl.ds(peer * piece, piece)],
            dst_ref=recv_ref.at[k],
            send_sem=send_sem.at[k],
            recv_sem=recv_sem.at[k],
            device_id={axis: peer},
            device_id_type=mesh_ids,
        )
        copy.start()
        copies.append(copy)
    for copy in copies:
        copy.wait()
    total = x_ref[pl.ds(me * piece, piece)]
    for k in range(1, size):
        total = total + recv_ref[k]
    o_ref[...] = total


def scatter_sum(parts, axis, collective_id):
    size = lax.axis_size(axis)
    piece = parts.shape[0] // size
    out_shape = (piece,) + parts.shape[1:]
    vmem = pltpu.VMEM
    return pl.pallas_call(
        functools.partial(scatter_kernel, axis, size),
        out_shape=jax.ShapeDtypeStruct(out_shape, parts.dtype),
        in_specs=[pl.BlockSpec(memory_space=vmem)],
        out_specs=pl.BlockSpec(memory_space=vmem),
        scratch_shapes=[
            vmem((size,) + out_shape, parts.dtype),
            pltpu.SemaphoreType.DMA((size,)),
            pltpu.SemaphoreType.DMA((size,)),
        ],
        compiler_params=pltpu.CompilerParams(collective_id=collective_id, has_side_effects=True),
    )(parts)


def spectrum_blocks(strain, psd):
    freq_count = lax.axis_size(FREQ)
    freq_index = lax.axis_index(FREQ)
    seg_local = strain.shape[0]
    rows_here = A // freq_count
    cols_here = B // freq_count
    highest = lax.Precision.HIGHEST
    first_cos, first_sin = cos_sin_table(
        jnp.arange(A, dtype=jnp.int32), jnp.arange(A, dtype=jnp.int32), A
    )
    first_table = jnp.concatenate([first_cos, -first_sin], axis=0)
    sent = strain.reshape(seg_local, rows_here, freq_count, cols_here).transpose(2, 1, 3, 0)
    sent = sent.reshape(freq_count, rows_here, cols_here * seg_local)
    slab = lax.all_to_all(sent, FREQ, 0, 0, tiled=True).reshape(A, cols_here * seg_local)
    both_parts = jnp.dot(first_table, slab, precision=highest)
    real_part = both_parts[:A]
    imag_part = both_parts[A:]
    time_ids = freq_index * cols_here + jnp.arange(cols_here, dtype=jnp.int32)
    twist_cos, twist_sin = cos_sin_table(jnp.arange(A, dtype=jnp.int32), time_ids, LEN)
    twist_cos = jnp.repeat(twist_cos, seg_local, axis=1)
    twist_sin = jnp.repeat(twist_sin, seg_local, axis=1)
    twisted = jnp.stack(
        [real_part * twist_cos + imag_part * twist_sin, imag_part * twist_cos - real_part * twist_sin]
    )
    p_here = A // freq_count
    twisted = twisted.reshape(2, freq_count, p_here, cols_here, seg_local).transpose(1, 3, 0, 2, 4)
    twisted = twisted.reshape(freq_count, cols_here, 2 * p_here * seg_local)
    columns = lax.all_to_all(twisted, FREQ, 0, 0, tiled=True).reshape(B, 2 * p_here * seg_local)
    split = 32
    j_ids = jnp.arange(NB, dtype=jnp.int32)
    high_cos, high_sin = cos_sin_table(j_ids, split * jnp.arange(B // split, dtype=jnp.int32), B)
    low_cos, low_sin = cos_sin_table(j_ids, jnp.arange(split, dtype=jnp.int32), B)
    second_cos = (
        high_cos[:, :, None] * low_cos[:, None, :] - high_sin[:, :, None] * low_sin[:, None, :]
    ).reshape(NB, B)
    second_sin = (
        high_sin[:, :, None] * low_cos[:, None, :] + high_cos[:, :, None] * low_sin[:, None, :]
    ).reshape(NB, B)
    with_cos = jnp.dot(second_cos, columns, precision=highest).reshape(NB, 2, p_here, seg_local)
    with_sin = jnp.dot(second_sin, columns, precision=highest).reshape(NB, 2, p_here, seg_local)
    amplitude = jnp.sqrt(LEN * psd)[:, :, None]
    real_out = (with_cos[:, 0] + with_sin[:, 1]) / amplitude
    imag_out = (with_cos[:, 1] - with_sin[:, 0]) / amplitude
    whitened = jnp.stack([real_out, imag_out], axis=1).transpose(3, 1, 0, 2).astype(jnp.bfloat16)
    return lax.all_to_all(whitened, FREQ, split_axis=2, concat_axis=3, tiled=True)


def on_device(strain, psd, templates, cutoffs, lags):
    freq_index = lax.axis_index(FREQ)
    local_data = spectrum_blocks(strain, psd)
    seg_piece = lax.all_gather(local_data, "tmpl", axis=0, tiled=True)
    x_size, z_size, c_size = (lax.axis_size(name) for name in FREQ)
    seg_order = seg_piece.reshape((x_size, z_size, c_size) + seg_piece.shape[1:])
    seg_order = seg_order.transpose(2, 1, 0, 3, 4, 5).reshape(seg_piece.shape)
    data = seg_order.transpose(2, 1, 0, 3)
    j_here = data.shape[0]
    first_block = freq_index * j_here
    partial_sums = intersect(data, templates, cutoffs, lags, first_block)
    for collective_id, name in enumerate(("fc", "fz", "fx")):
        partial_sums = scatter_sum(partial_sums, name, collective_id + 1)
    return partial_sums


def solution(mesh):
    tmpl_size, freq_size = mesh.devices.shape
    split = Mesh(
        mesh.devices.reshape(tmpl_size, 4, freq_size // 8, 2), ("tmpl",) + FREQ
    )
    placed = (P("tmpl", FREQ), P(None, FREQ), P("tmpl", None, FREQ, None), P("tmpl"), P())
    return jax.shard_map(
        on_device, mesh=split, in_specs=placed, out_specs=P(FREQ, None, "tmpl"), check_vma=False
    )
```

```python
import functools
import math

import jax
import jax.numpy as jnp
from jax import lax
from jax.experimental import pallas as pl
from jax.experimental.pallas import tpu as pltpu
from jax.sharding import Mesh, PartitionSpec as P

A = 512
B = 1024
LEN = 524288
NB = 512


two_pi = 2.0 * math.pi
FREQ = ("fx", "fz", "fc")


def cos_sin_table(row_ids, col_ids, modulus):
    product = row_ids[:, None] * col_ids[None, :] % modulus
    phase_angle = product.astype(jnp.float32) * (two_pi / modulus)
    return (jnp.cos(phase_angle), jnp.sin(phase_angle))


def intersect_kernel(ph_ref, dat_ref, tm_ref, out_ref, lhs_ref):
    step = pl.program_id(0)
    seg_count = dat_ref.shape[2]
    lag_total = ph_ref.shape[2]
    rows = seg_count * lag_total
    chunk = 8

    @pl.when(step == 0)
    def _():
        out_ref[...] = jnp.zeros_like(out_ref)

    lag_cos = ph_ref[0, 0][None]
    lag_sin = ph_ref[0, 1][None]

    def build(i, carry):
        s0 = pl.multiple_of(i * chunk, chunk)
        data_real = dat_ref[0, 0, pl.ds(s0, chunk), :].astype(jnp.float32)[:, None, :]
        data_imag = dat_ref[0, 1, pl.ds(s0, chunk), :].astype(jnp.float32)[:, None, :]
        real_q = data_real * lag_cos - data_imag * lag_sin
        imag_q = data_real * lag_sin + data_imag * lag_cos
        r0 = pl.multiple_of(i * chunk * lag_total, chunk * lag_total)
        lhs_ref[pl.ds(r0, chunk * lag_total), :] = real_q.reshape(chunk * lag_total, -1).astype(jnp.bfloat16)
        lhs_ref[pl.ds(rows + r0, chunk * lag_total), :] = imag_q.reshape(chunk * lag_total, -1).astype(jnp.bfloat16)
        return carry

    lax.fori_loop(0, seg_count // chunk, build, 0)
    dims = (((1,), (1,)), ((), ()))
    lhs = lhs_ref[...]
    with_re = lax.dot_general(lhs, tm_ref[0, 0], dims, preferred_element_type=jnp.float32)
    with_im = lax.dot_general(lhs, tm_ref[0, 1], dims, preferred_element_type=jnp.float32)
    real_sum = with_re[:rows] + with_im[rows:]
    imag_sum = with_re[rows:] - with_im[:rows]
    width = real_sum.shape[1]
    out_ref[:, 0:lag_total, :] += real_sum.reshape(seg_count, lag_total, width)
    out_ref[:, lag_total:, :] += imag_sum.reshape(seg_count, lag_total, width)


def intersect(data, templates, cutoffs, lags, first_block):
    blocks_here, _, seg_count, width = data.shape
    tmpl_local = templates.shape[0]
    lag_total = lags.shape[0]
    block_ids = first_block + jnp.arange(blocks_here, dtype=jnp.int32)
    position = jnp.arange(width, dtype=jnp.int32)
    phase_int = (A * (lags[:, None] * block_ids[None, :] % B))[:, :, None] + (
        lags[:, None] * position[None, :] % LEN
    )[:, None, :]
    phase_angle = (phase_int % LEN).astype(jnp.float32) * (two_pi / LEN)
    phases = jnp.stack([jnp.cos(phase_angle), jnp.sin(phase_angle)], axis=0).transpose(2, 0, 1, 3)
    keep = block_ids[None, None, :, None] < cutoffs[:, None, None, None]
    masked = jnp.where(keep, templates, jnp.zeros_like(templates)).transpose(2, 1, 0, 3)
    rows = seg_count * lag_total
    flops = 2 * 2 * (2 * rows) * width * tmpl_local * blocks_here
    moved = masked.size * 2 + data.size * 2 + phases.size * 4 + seg_count * 2 * lag_total * tmpl_local * 4
    return pl.pallas_call(
        intersect_kernel,
        out_shape=jax.ShapeDtypeStruct((seg_count, 2 * lag_total, tmpl_local), jnp.float32),
        grid=(blocks_here,),
        in_specs=[
            pl.BlockSpec((1, 2, lag_total, width), lambda j: (j, 0, 0, 0)),
            pl.BlockSpec((1, 2, seg_count, width), lambda j: (j, 0, 0, 0)),
            pl.BlockSpec((1, 2, tmpl_local, width), lambda j: (j, 0, 0, 0)),
        ],
        out_specs=pl.BlockSpec((seg_count, 2 * lag_total, tmpl_local), lambda j: (0, 0, 0)),
        scratch_shapes=[pltpu.VMEM((2 * rows, width), jnp.bfloat16)],
        compiler_params=pltpu.CompilerParams(dimension_semantics=("arbitrary",)),
        cost_estimate=pl.CostEstimate(flops=flops, transcendentals=0, bytes_accessed=moved),
    )(phases, data, masked)


def scatter_kernel(axis, size, x_ref, o_ref, recv_ref, send_sem, recv_sem):
    me = lax.axis_index(axis)
    piece = o_ref.shape[0]
    mesh_ids = pl.DeviceIdType.MESH
    barrier = pltpu.get_barrier_semaphore()
    for k in range(1, size):
        peer = lax.rem(me + k, size)
        pl.semaphore_signal(barrier, inc=1, device_id={axis: peer}, device_id_type=mesh_ids)
    pl.semaphore_wait(barrier, size - 1)
    copies = []
    for k in range(1, size):
        peer = lax.rem(me + k, size)
        copy = pltpu.make_async_remote_copy(
            src_ref=x_ref.at[pl.ds(peer * piece, piece)],
            dst_ref=recv_ref.at[k],
            send_sem=send_sem.at[k],
            recv_sem=recv_sem.at[k],
            device_id={axis: peer},
            device_id_type=mesh_ids,
        )
        copy.start()
        copies.append(copy)
    for copy in copies:
        copy.wait()
    total = x_ref[pl.ds(me * piece, piece)]
    for k in range(1, size):
        total = total + recv_ref[k]
    o_ref[...] = total


def scatter_sum(parts, axis, collective_id):
    size = lax.axis_size(axis)
    piece = parts.shape[0] // size
    out_shape = (piece,) + parts.shape[1:]
    vmem = pltpu.VMEM
    return pl.pallas_call(
        functools.partial(scatter_kernel, axis, size),
        out_shape=jax.ShapeDtypeStruct(out_shape, parts.dtype),
        in_specs=[pl.BlockSpec(memory_space=vmem)],
        out_specs=pl.BlockSpec(memory_space=vmem),
        scratch_shapes=[
            vmem((size,) + out_shape, parts.dtype),
            pltpu.SemaphoreType.DMA((size,)),
            pltpu.SemaphoreType.DMA((size,)),
        ],
        compiler_params=pltpu.CompilerParams(collective_id=collective_id, has_side_effects=True),
    )(parts)


def spectrum_blocks(strain, psd):
    freq_count = lax.axis_size(FREQ)
    freq_index = lax.axis_index(FREQ)
    seg_local = strain.shape[0]
    rows_here = A // freq_count
    cols_here = B // freq_count
    highest = lax.Precision.HIGHEST
    first_cos, first_sin = cos_sin_table(
        jnp.arange(A, dtype=jnp.int32), jnp.arange(A, dtype=jnp.int32), A
    )
    first_table = jnp.concatenate([first_cos, -first_sin], axis=0)
    sent = strain.reshape(seg_local, rows_here, freq_count, cols_here).transpose(2, 1, 3, 0)
    sent = sent.reshape(freq_count, rows_here, cols_here * seg_local)
    slab = lax.all_to_all(sent, FREQ, 0, 0, tiled=True).reshape(A, cols_here * seg_local)
    both_parts = jnp.dot(first_table, slab, precision=highest)
    real_part = both_parts[:A]
    imag_part = both_parts[A:]
    time_ids = freq_index * cols_here + jnp.arange(cols_here, dtype=jnp.int32)
    twist_cos, twist_sin = cos_sin_table(jnp.arange(A, dtype=jnp.int32), time_ids, LEN)
    twist_cos = jnp.repeat(twist_cos, seg_local, axis=1)
    twist_sin = jnp.repeat(twist_sin, seg_local, axis=1)
    twisted = jnp.stack(
        [real_part * twist_cos + imag_part * twist_sin, imag_part * twist_cos - real_part * twist_sin]
    )
    p_here = A // freq_count
    twisted = twisted.reshape(2, freq_count, p_here, cols_here, seg_local).transpose(1, 3, 0, 2, 4)
    twisted = twisted.reshape(freq_count, cols_here, 2 * p_here * seg_local)
    columns = lax.all_to_all(twisted, FREQ, 0, 0, tiled=True).reshape(B, 2 * p_here * seg_local)
    split = 32
    j_ids = jnp.arange(NB, dtype=jnp.int32)
    high_cos, high_sin = cos_sin_table(j_ids, split * jnp.arange(B // split, dtype=jnp.int32), B)
    low_cos, low_sin = cos_sin_table(j_ids, jnp.arange(split, dtype=jnp.int32), B)
    second_cos = (
        high_cos[:, :, None] * low_cos[:, None, :] - high_sin[:, :, None] * low_sin[:, None, :]
    ).reshape(NB, B)
    second_sin = (
        high_sin[:, :, None] * low_cos[:, None, :] + high_cos[:, :, None] * low_sin[:, None, :]
    ).reshape(NB, B)
    with_cos = jnp.dot(second_cos, columns, precision=highest).reshape(NB, 2, p_here, seg_local)
    with_sin = jnp.dot(second_sin, columns, precision=highest).reshape(NB, 2, p_here, seg_local)
    amplitude = jnp.sqrt(LEN * psd)[:, :, None]
    real_out = (with_cos[:, 0] + with_sin[:, 1]) / amplitude
    imag_out = (with_cos[:, 1] - with_sin[:, 0]) / amplitude
    whitened = jnp.stack([real_out, imag_out], axis=1).transpose(3, 1, 0, 2).astype(jnp.bfloat16)
    return lax.all_to_all(whitened, FREQ, split_axis=2, concat_axis=3, tiled=True)


def on_device(strain, psd, templates, cutoffs, lags):
    freq_index = lax.axis_index(FREQ)
    local_data = spectrum_blocks(strain, psd)
    seg_piece = lax.all_gather(local_data, "tmpl", axis=0, tiled=True)
    x_size, z_size, c_size = (lax.axis_size(name) for name in FREQ)
    seg_order = seg_piece.reshape((x_size, z_size, c_size) + seg_piece.shape[1:])
    seg_order = seg_order.transpose(2, 0, 1, 3, 4, 5).reshape(seg_piece.shape)
    data = seg_order.transpose(2, 1, 0, 3)
    j_here = data.shape[0]
    first_block = freq_index * j_here
    partial_sums = intersect(data, templates, cutoffs, lags, first_block)
    for collective_id, name in enumerate(("fc", "fx", "fz")):
        partial_sums = scatter_sum(partial_sums, name, collective_id + 1)
    return partial_sums


def solution(mesh):
    tmpl_size, freq_size = mesh.devices.shape
    split = Mesh(
        mesh.devices.reshape(tmpl_size, 4, freq_size // 8, 2), ("tmpl",) + FREQ
    )
    placed = (P("tmpl", FREQ), P(None, FREQ), P("tmpl", None, FREQ, None), P("tmpl"), P())
    return jax.shard_map(
        on_device, mesh=split, in_specs=placed, out_specs=P(FREQ, None, "tmpl"), check_vma=False
    )
```

```python
import functools
import math

import jax
import jax.numpy as jnp
from jax import lax
from jax.experimental import pallas as pl
from jax.experimental.pallas import tpu as pltpu
from jax.sharding import Mesh, PartitionSpec as P

A = 512
B = 1024
LEN = 524288
NB = 512


two_pi = 2.0 * math.pi
FREQ = ("fx", "fz", "fc")


def cos_sin_table(row_ids, col_ids, modulus):
    product = row_ids[:, None] * col_ids[None, :] % modulus
    phase_angle = product.astype(jnp.float32) * (two_pi / modulus)
    return (jnp.cos(phase_angle), jnp.sin(phase_angle))


def intersect_kernel(ph_ref, dat_ref, tm_ref, out_ref, lhs_ref):
    step = pl.program_id(0)
    seg_count = dat_ref.shape[2]
    lag_total = ph_ref.shape[2]
    rows = seg_count * lag_total
    chunk = 8

    @pl.when(step == 0)
    def _():
        out_ref[...] = jnp.zeros_like(out_ref)

    lag_cos = ph_ref[0, 0][None]
    lag_sin = ph_ref[0, 1][None]

    def build(i, carry):
        s0 = pl.multiple_of(i * chunk, chunk)
        data_real = dat_ref[0, 0, pl.ds(s0, chunk), :].astype(jnp.float32)[:, None, :]
        data_imag = dat_ref[0, 1, pl.ds(s0, chunk), :].astype(jnp.float32)[:, None, :]
        real_q = data_real * lag_cos - data_imag * lag_sin
        imag_q = data_real * lag_sin + data_imag * lag_cos
        r0 = pl.multiple_of(i * chunk * lag_total, chunk * lag_total)
        lhs_ref[pl.ds(r0, chunk * lag_total), :] = real_q.reshape(chunk * lag_total, -1).astype(jnp.bfloat16)
        lhs_ref[pl.ds(rows + r0, chunk * lag_total), :] = imag_q.reshape(chunk * lag_total, -1).astype(jnp.bfloat16)
        return carry

    lax.fori_loop(0, seg_count // chunk, build, 0)
    dims = (((1,), (1,)), ((), ()))
    lhs = lhs_ref[...]
    with_re = lax.dot_general(lhs, tm_ref[0, 0], dims, preferred_element_type=jnp.float32)
    with_im = lax.dot_general(lhs, tm_ref[0, 1], dims, preferred_element_type=jnp.float32)
    real_sum = with_re[:rows] + with_im[rows:]
    imag_sum = with_re[rows:] - with_im[:rows]
    width = real_sum.shape[1]
    out_ref[:, 0:lag_total, :] += real_sum.reshape(seg_count, lag_total, width)
    out_ref[:, lag_total:, :] += imag_sum.reshape(seg_count, lag_total, width)


def intersect(data, templates, cutoffs, lags, first_block):
    blocks_here, _, seg_count, width = data.shape
    tmpl_local = templates.shape[0]
    lag_total = lags.shape[0]
    block_ids = first_block + jnp.arange(blocks_here, dtype=jnp.int32)
    position = jnp.arange(width, dtype=jnp.int32)
    phase_int = (A * (lags[:, None] * block_ids[None, :] % B))[:, :, None] + (
        lags[:, None] * position[None, :] % LEN
    )[:, None, :]
    phase_angle = (phase_int % LEN).astype(jnp.float32) * (two_pi / LEN)
    phases = jnp.stack([jnp.cos(phase_angle), jnp.sin(phase_angle)], axis=0).transpose(2, 0, 1, 3)
    keep = block_ids[None, None, :, None] < cutoffs[:, None, None, None]
    masked = jnp.where(keep, templates, jnp.zeros_like(templates)).transpose(2, 1, 0, 3)
    rows = seg_count * lag_total
    flops = 2 * 2 * (2 * rows) * width * tmpl_local * blocks_here
    moved = masked.size * 2 + data.size * 2 + phases.size * 4 + seg_count * 2 * lag_total * tmpl_local * 4
    return pl.pallas_call(
        intersect_kernel,
        out_shape=jax.ShapeDtypeStruct((seg_count, 2 * lag_total, tmpl_local), jnp.float32),
        grid=(blocks_here,),
        in_specs=[
            pl.BlockSpec((1, 2, lag_total, width), lambda j: (j, 0, 0, 0)),
            pl.BlockSpec((1, 2, seg_count, width), lambda j: (j, 0, 0, 0)),
            pl.BlockSpec((1, 2, tmpl_local, width), lambda j: (j, 0, 0, 0)),
        ],
        out_specs=pl.BlockSpec((seg_count, 2 * lag_total, tmpl_local), lambda j: (0, 0, 0)),
        scratch_shapes=[pltpu.VMEM((2 * rows, width), jnp.bfloat16)],
        compiler_params=pltpu.CompilerParams(dimension_semantics=("arbitrary",)),
        cost_estimate=pl.CostEstimate(flops=flops, transcendentals=0, bytes_accessed=moved),
    )(phases, data, masked)


def scatter_kernel(axis, size, x_ref, o_ref, recv_ref, send_sem, recv_sem):
    me = lax.axis_index(axis)
    piece = o_ref.shape[0]
    mesh_ids = pl.DeviceIdType.MESH
    barrier = pltpu.get_barrier_semaphore()
    for k in range(1, size):
        peer = lax.rem(me + k, size)
        pl.semaphore_signal(barrier, inc=1, device_id={axis: peer}, device_id_type=mesh_ids)
    pl.semaphore_wait(barrier, size - 1)
    copies = []
    for k in range(1, size):
        peer = lax.rem(me + k, size)
        copy = pltpu.make_async_remote_copy(
            src_ref=x_ref.at[pl.ds(peer * piece, piece)],
            dst_ref=recv_ref.at[k],
            send_sem=send_sem.at[k],
            recv_sem=recv_sem.at[k],
            device_id={axis: peer},
            device_id_type=mesh_ids,
        )
        copy.start()
        copies.append(copy)
    for copy in copies:
        copy.wait()
    total = x_ref[pl.ds(me * piece, piece)]
    for k in range(1, size):
        total = total + recv_ref[k]
    o_ref[...] = total


def scatter_sum(parts, axis, collective_id):
    size = lax.axis_size(axis)
    piece = parts.shape[0] // size
    out_shape = (piece,) + parts.shape[1:]
    vmem = pltpu.VMEM
    return pl.pallas_call(
        functools.partial(scatter_kernel, axis, size),
        out_shape=jax.ShapeDtypeStruct(out_shape, parts.dtype),
        in_specs=[pl.BlockSpec(memory_space=vmem)],
        out_specs=pl.BlockSpec(memory_space=vmem),
        scratch_shapes=[
            vmem((size,) + out_shape, parts.dtype),
            pltpu.SemaphoreType.DMA((size,)),
            pltpu.SemaphoreType.DMA((size,)),
        ],
        compiler_params=pltpu.CompilerParams(collective_id=collective_id, has_side_effects=True),
    )(parts)


def gather_kernel(axis, size, x_ref, o_ref, send_sem, recv_sem):
    me = lax.axis_index(axis)
    mesh_ids = pl.DeviceIdType.MESH
    barrier = pltpu.get_barrier_semaphore()
    for k in range(1, size):
        peer = lax.rem(me + k, size)
        pl.semaphore_signal(barrier, inc=1, device_id={axis: peer}, device_id_type=mesh_ids)
    pl.semaphore_wait(barrier, size - 1)
    copies = []
    for k in range(1, size):
        peer = lax.rem(me + k, size)
        copy = pltpu.make_async_remote_copy(
            src_ref=x_ref,
            dst_ref=o_ref.at[me],
            send_sem=send_sem.at[k],
            recv_sem=recv_sem.at[k],
            device_id={axis: peer},
            device_id_type=mesh_ids,
        )
        copy.start()
        copies.append(copy)
    o_ref[me] = x_ref[...]
    for copy in copies:
        copy.wait()


def gather_all(block, axis, collective_id):
    size = lax.axis_size(axis)
    vmem = pltpu.VMEM
    return pl.pallas_call(
        functools.partial(gather_kernel, axis, size),
        out_shape=jax.ShapeDtypeStruct((size,) + block.shape, block.dtype),
        in_specs=[pl.BlockSpec(memory_space=vmem)],
        out_specs=pl.BlockSpec(memory_space=vmem),
        scratch_shapes=[pltpu.SemaphoreType.DMA((size,)), pltpu.SemaphoreType.DMA((size,))],
        compiler_params=pltpu.CompilerParams(collective_id=collective_id, has_side_effects=True),
    )(block)


def spectrum_blocks(strain, psd):
    freq_count = lax.axis_size(FREQ)
    freq_index = lax.axis_index(FREQ)
    seg_local = strain.shape[0]
    rows_here = A // freq_count
    cols_here = B // freq_count
    highest = lax.Precision.HIGHEST
    first_cos, first_sin = cos_sin_table(
        jnp.arange(A, dtype=jnp.int32), jnp.arange(A, dtype=jnp.int32), A
    )
    first_table = jnp.concatenate([first_cos, -first_sin], axis=0)
    sent = strain.reshape(seg_local, rows_here, freq_count, cols_here).transpose(2, 1, 3, 0)
    sent = sent.reshape(freq_count, rows_here, cols_here * seg_local)
    slab = lax.all_to_all(sent, FREQ, 0, 0, tiled=True).reshape(A, cols_here * seg_local)
    both_parts = jnp.dot(first_table, slab, precision=highest)
    real_part = both_parts[:A]
    imag_part = both_parts[A:]
    time_ids = freq_index * cols_here + jnp.arange(cols_here, dtype=jnp.int32)
    twist_cos, twist_sin = cos_sin_table(jnp.arange(A, dtype=jnp.int32), time_ids, LEN)
    twist_cos = jnp.repeat(twist_cos, seg_local, axis=1)
    twist_sin = jnp.repeat(twist_sin, seg_local, axis=1)
    twisted = jnp.stack(
        [real_part * twist_cos + imag_part * twist_sin, imag_part * twist_cos - real_part * twist_sin]
    )
    p_here = A // freq_count
    twisted = twisted.reshape(2, freq_count, p_here, cols_here, seg_local).transpose(1, 3, 0, 2, 4)
    twisted = twisted.reshape(freq_count, cols_here, 2 * p_here * seg_local)
    columns = lax.all_to_all(twisted, FREQ, 0, 0, tiled=True).reshape(B, 2 * p_here * seg_local)
    split = 32
    j_ids = jnp.arange(NB, dtype=jnp.int32)
    high_cos, high_sin = cos_sin_table(j_ids, split * jnp.arange(B // split, dtype=jnp.int32), B)
    low_cos, low_sin = cos_sin_table(j_ids, jnp.arange(split, dtype=jnp.int32), B)
    second_cos = (
        high_cos[:, :, None] * low_cos[:, None, :] - high_sin[:, :, None] * low_sin[:, None, :]
    ).reshape(NB, B)
    second_sin = (
        high_sin[:, :, None] * low_cos[:, None, :] + high_cos[:, :, None] * low_sin[:, None, :]
    ).reshape(NB, B)
    with_cos = jnp.dot(second_cos, columns, precision=highest).reshape(NB, 2, p_here, seg_local)
    with_sin = jnp.dot(second_sin, columns, precision=highest).reshape(NB, 2, p_here, seg_local)
    amplitude = jnp.sqrt(LEN * psd)[:, :, None]
    real_out = (with_cos[:, 0] + with_sin[:, 1]) / amplitude
    imag_out = (with_cos[:, 1] - with_sin[:, 0]) / amplitude
    whitened = jnp.stack([real_out, imag_out], axis=1).transpose(3, 1, 0, 2).astype(jnp.bfloat16)
    return lax.all_to_all(whitened, FREQ, split_axis=2, concat_axis=3, tiled=True)


def on_device(strain, psd, templates, cutoffs, lags):
    freq_index = lax.axis_index(FREQ)
    local_data = spectrum_blocks(strain, psd)
    seg_piece = gather_all(local_data, "tmpl", 4)
    seg_piece = seg_piece.reshape((-1,) + local_data.shape[1:])
    x_size, z_size, c_size = (lax.axis_size(name) for name in FREQ)
    seg_order = seg_piece.reshape((x_size, z_size, c_size) + seg_piece.shape[1:])
    seg_order = seg_order.transpose(2, 0, 1, 3, 4, 5).reshape(seg_piece.shape)
    data = seg_order.transpose(2, 1, 0, 3)
    j_here = data.shape[0]
    first_block = freq_index * j_here
    partial_sums = intersect(data, templates, cutoffs, lags, first_block)
    for collective_id, name in enumerate(("fc", "fx", "fz")):
        partial_sums = scatter_sum(partial_sums, name, collective_id + 1)
    return partial_sums


def solution(mesh):
    tmpl_size, freq_size = mesh.devices.shape
    split = Mesh(
        mesh.devices.reshape(tmpl_size, 4, freq_size // 8, 2), ("tmpl",) + FREQ
    )
    placed = (P("tmpl", FREQ), P(None, FREQ), P("tmpl", None, FREQ, None), P("tmpl"), P())
    return jax.shard_map(
        on_device, mesh=split, in_specs=placed, out_specs=P(FREQ, None, "tmpl"), check_vma=False
    )
```

```python
import functools
import math

import jax
import jax.numpy as jnp
from jax import lax
from jax.experimental import pallas as pl
from jax.experimental.pallas import tpu as pltpu
from jax.sharding import Mesh, PartitionSpec as P

A = 512
B = 1024
LEN = 524288
NB = 512


two_pi = 2.0 * math.pi
FREQ = ("fx", "fz", "fc")


def cos_sin_table(row_ids, col_ids, modulus):
    product = row_ids[:, None] * col_ids[None, :] % modulus
    phase_angle = product.astype(jnp.float32) * (two_pi / modulus)
    return (jnp.cos(phase_angle), jnp.sin(phase_angle))


def intersect_kernel(ph_ref, dat_ref, tm_ref, out_ref, lhs_ref):
    step = pl.program_id(0)
    seg_count = dat_ref.shape[2]
    lag_total = ph_ref.shape[2]
    rows = seg_count * lag_total
    chunk = 8

    @pl.when(step == 0)
    def _():
        out_ref[...] = jnp.zeros_like(out_ref)

    lag_cos = ph_ref[0, 0][None]
    lag_sin = ph_ref[0, 1][None]

    def build(i, carry):
        s0 = pl.multiple_of(i * chunk, chunk)
        data_real = dat_ref[0, 0, pl.ds(s0, chunk), :].astype(jnp.float32)[:, None, :]
        data_imag = dat_ref[0, 1, pl.ds(s0, chunk), :].astype(jnp.float32)[:, None, :]
        real_q = data_real * lag_cos - data_imag * lag_sin
        imag_q = data_real * lag_sin + data_imag * lag_cos
        r0 = pl.multiple_of(i * chunk * lag_total, chunk * lag_total)
        lhs_ref[pl.ds(r0, chunk * lag_total), :] = real_q.reshape(chunk * lag_total, -1).astype(jnp.bfloat16)
        lhs_ref[pl.ds(rows + r0, chunk * lag_total), :] = imag_q.reshape(chunk * lag_total, -1).astype(jnp.bfloat16)
        return carry

    lax.fori_loop(0, seg_count // chunk, build, 0)
    dims = (((1,), (1,)), ((), ()))
    lhs = lhs_ref[...]
    with_re = lax.dot_general(lhs, tm_ref[0, 0], dims, preferred_element_type=jnp.float32)
    with_im = lax.dot_general(lhs, tm_ref[0, 1], dims, preferred_element_type=jnp.float32)
    real_sum = with_re[:rows] + with_im[rows:]
    imag_sum = with_re[rows:] - with_im[:rows]
    width = real_sum.shape[1]
    out_ref[:, 0:lag_total, :] += real_sum.reshape(seg_count, lag_total, width)
    out_ref[:, lag_total:, :] += imag_sum.reshape(seg_count, lag_total, width)


def intersect(data, templates, cutoffs, lags, first_block):
    blocks_here, _, seg_count, width = data.shape
    tmpl_local = templates.shape[0]
    lag_total = lags.shape[0]
    block_ids = first_block + jnp.arange(blocks_here, dtype=jnp.int32)
    position = jnp.arange(width, dtype=jnp.int32)
    phase_int = (A * (lags[:, None] * block_ids[None, :] % B))[:, :, None] + (
        lags[:, None] * position[None, :] % LEN
    )[:, None, :]
    phase_angle = (phase_int % LEN).astype(jnp.float32) * (two_pi / LEN)
    phases = jnp.stack([jnp.cos(phase_angle), jnp.sin(phase_angle)], axis=0).transpose(2, 0, 1, 3)
    keep = block_ids[None, None, :, None] < cutoffs[:, None, None, None]
    masked = jnp.where(keep, templates, jnp.zeros_like(templates)).transpose(2, 1, 0, 3)
    rows = seg_count * lag_total
    flops = 2 * 2 * (2 * rows) * width * tmpl_local * blocks_here
    moved = masked.size * 2 + data.size * 2 + phases.size * 4 + seg_count * 2 * lag_total * tmpl_local * 4
    return pl.pallas_call(
        intersect_kernel,
        out_shape=jax.ShapeDtypeStruct((seg_count, 2 * lag_total, tmpl_local), jnp.float32),
        grid=(blocks_here,),
        in_specs=[
            pl.BlockSpec((1, 2, lag_total, width), lambda j: (j, 0, 0, 0)),
            pl.BlockSpec((1, 2, seg_count, width), lambda j: (j, 0, 0, 0)),
            pl.BlockSpec((1, 2, tmpl_local, width), lambda j: (j, 0, 0, 0)),
        ],
        out_specs=pl.BlockSpec((seg_count, 2 * lag_total, tmpl_local), lambda j: (0, 0, 0)),
        scratch_shapes=[pltpu.VMEM((2 * rows, width), jnp.bfloat16)],
        compiler_params=pltpu.CompilerParams(dimension_semantics=("arbitrary",)),
        cost_estimate=pl.CostEstimate(flops=flops, transcendentals=0, bytes_accessed=moved),
    )(phases, data, masked)


def scatter_kernel(axis, size, x_ref, o_ref, recv_ref, send_sem, recv_sem):
    me = lax.axis_index(axis)
    piece = o_ref.shape[0]
    mesh_ids = pl.DeviceIdType.MESH
    barrier = pltpu.get_barrier_semaphore()
    for k in range(1, size):
        peer = lax.rem(me + k, size)
        pl.semaphore_signal(barrier, inc=1, device_id={axis: peer}, device_id_type=mesh_ids)
    pl.semaphore_wait(barrier, size - 1)
    copies = []
    for k in range(1, size):
        peer = lax.rem(me + k, size)
        copy = pltpu.make_async_remote_copy(
            src_ref=x_ref.at[pl.ds(peer * piece, piece)],
            dst_ref=recv_ref.at[k],
            send_sem=send_sem.at[k],
            recv_sem=recv_sem.at[k],
            device_id={axis: peer},
            device_id_type=mesh_ids,
        )
        copy.start()
        copies.append(copy)
    for copy in copies:
        copy.wait()
    total = x_ref[pl.ds(me * piece, piece)]
    for k in range(1, size):
        total = total + recv_ref[k]
    o_ref[...] = total


def scatter_sum(parts, axis, collective_id):
    size = lax.axis_size(axis)
    piece = parts.shape[0] // size
    out_shape = (piece,) + parts.shape[1:]
    vmem = pltpu.VMEM
    return pl.pallas_call(
        functools.partial(scatter_kernel, axis, size),
        out_shape=jax.ShapeDtypeStruct(out_shape, parts.dtype),
        in_specs=[pl.BlockSpec(memory_space=vmem)],
        out_specs=pl.BlockSpec(memory_space=vmem),
        scratch_shapes=[
            vmem((size,) + out_shape, parts.dtype),
            pltpu.SemaphoreType.DMA((size,)),
            pltpu.SemaphoreType.DMA((size,)),
        ],
        compiler_params=pltpu.CompilerParams(collective_id=collective_id, has_side_effects=True),
    )(parts)


def gather_kernel(axis, size, x_ref, o_ref, send_sem, recv_sem):
    me = lax.axis_index(axis)
    mesh_ids = pl.DeviceIdType.MESH
    barrier = pltpu.get_barrier_semaphore()
    for k in range(1, size):
        peer = lax.rem(me + k, size)
        pl.semaphore_signal(barrier, inc=1, device_id={axis: peer}, device_id_type=mesh_ids)
    pl.semaphore_wait(barrier, size - 1)
    copies = []
    for k in range(1, size):
        peer = lax.rem(me + k, size)
        copy = pltpu.make_async_remote_copy(
            src_ref=x_ref,
            dst_ref=o_ref.at[me],
            send_sem=send_sem.at[k],
            recv_sem=recv_sem.at[k],
            device_id={axis: peer},
            device_id_type=mesh_ids,
        )
        copy.start()
        copies.append(copy)
    o_ref[me] = x_ref[...]
    for copy in copies:
        copy.wait()


def gather_all(block, axis, collective_id):
    size = lax.axis_size(axis)
    vmem = pltpu.VMEM
    return pl.pallas_call(
        functools.partial(gather_kernel, axis, size),
        out_shape=jax.ShapeDtypeStruct((size,) + block.shape, block.dtype),
        in_specs=[pl.BlockSpec(memory_space=vmem)],
        out_specs=pl.BlockSpec(memory_space=vmem),
        scratch_shapes=[pltpu.SemaphoreType.DMA((size,)), pltpu.SemaphoreType.DMA((size,))],
        compiler_params=pltpu.CompilerParams(collective_id=collective_id, has_side_effects=True),
    )(block)


def spectrum_blocks(strain, psd):
    freq_count = lax.axis_size(FREQ)
    freq_index = lax.axis_index(FREQ)
    seg_local = strain.shape[0]
    rows_here = A // freq_count
    cols_here = B // freq_count
    highest = lax.Precision.HIGHEST
    first_cos, first_sin = cos_sin_table(
        jnp.arange(A, dtype=jnp.int32), jnp.arange(A, dtype=jnp.int32), A
    )
    first_table = jnp.concatenate([first_cos, -first_sin], axis=0)
    sent = strain.reshape(seg_local, rows_here, freq_count, cols_here).transpose(2, 1, 3, 0)
    sent = sent.reshape(freq_count, rows_here, cols_here * seg_local)
    slab = lax.all_to_all(sent, FREQ, 0, 0, tiled=True).reshape(A, cols_here * seg_local)
    both_parts = jnp.dot(first_table, slab, precision=highest)
    real_part = both_parts[:A]
    imag_part = both_parts[A:]
    time_ids = freq_index * cols_here + jnp.arange(cols_here, dtype=jnp.int32)
    twist_cos, twist_sin = cos_sin_table(jnp.arange(A, dtype=jnp.int32), time_ids, LEN)
    p_here = A // freq_count
    shaped = (freq_count, p_here, cols_here * seg_local)
    real_part = real_part.reshape(shaped)
    imag_part = imag_part.reshape(shaped)
    twist_cos = jnp.repeat(twist_cos, seg_local, axis=1).reshape(shaped)
    twist_sin = jnp.repeat(twist_sin, seg_local, axis=1).reshape(shaped)
    twisted = jnp.stack(
        [real_part * twist_cos + imag_part * twist_sin, imag_part * twist_cos - real_part * twist_sin],
        axis=1,
    )
    twisted = twisted.reshape(freq_count, 2 * p_here, cols_here * seg_local)
    columns = lax.all_to_all(twisted, FREQ, 0, 0, tiled=True)
    columns = columns.reshape(freq_count, 2, p_here, cols_here, seg_local).transpose(0, 3, 1, 2, 4)
    columns = columns.reshape(B, 2 * p_here * seg_local)
    split = 32
    j_ids = jnp.arange(NB, dtype=jnp.int32)
    high_cos, high_sin = cos_sin_table(j_ids, split * jnp.arange(B // split, dtype=jnp.int32), B)
    low_cos, low_sin = cos_sin_table(j_ids, jnp.arange(split, dtype=jnp.int32), B)
    second_cos = (
        high_cos[:, :, None] * low_cos[:, None, :] - high_sin[:, :, None] * low_sin[:, None, :]
    ).reshape(NB, B)
    second_sin = (
        high_sin[:, :, None] * low_cos[:, None, :] + high_cos[:, :, None] * low_sin[:, None, :]
    ).reshape(NB, B)
    with_cos = jnp.dot(second_cos, columns, precision=highest).reshape(NB, 2, p_here, seg_local)
    with_sin = jnp.dot(second_sin, columns, precision=highest).reshape(NB, 2, p_here, seg_local)
    amplitude = jnp.sqrt(LEN * psd)[:, :, None]
    real_out = (with_cos[:, 0] + with_sin[:, 1]) / amplitude
    imag_out = (with_cos[:, 1] - with_sin[:, 0]) / amplitude
    whitened = jnp.stack([real_out, imag_out], axis=1).transpose(3, 1, 0, 2).astype(jnp.bfloat16)
    return lax.all_to_all(whitened, FREQ, split_axis=2, concat_axis=3, tiled=True)


def on_device(strain, psd, templates, cutoffs, lags):
    freq_index = lax.axis_index(FREQ)
    local_data = spectrum_blocks(strain, psd)
    seg_piece = gather_all(local_data, "tmpl", 4)
    seg_piece = seg_piece.reshape((-1,) + local_data.shape[1:])
    x_size, z_size, c_size = (lax.axis_size(name) for name in FREQ)
    seg_order = seg_piece.reshape((x_size, z_size, c_size) + seg_piece.shape[1:])
    seg_order = seg_order.transpose(2, 0, 1, 3, 4, 5).reshape(seg_piece.shape)
    data = seg_order.transpose(2, 1, 0, 3)
    j_here = data.shape[0]
    first_block = freq_index * j_here
    partial_sums = intersect(data, templates, cutoffs, lags, first_block)
    for collective_id, name in enumerate(("fc", "fx", "fz")):
        partial_sums = scatter_sum(partial_sums, name, collective_id + 1)
    return partial_sums


def solution(mesh):
    tmpl_size, freq_size = mesh.devices.shape
    split = Mesh(
        mesh.devices.reshape(tmpl_size, 4, freq_size // 8, 2), ("tmpl",) + FREQ
    )
    placed = (P("tmpl", FREQ), P(None, FREQ), P("tmpl", None, FREQ, None), P("tmpl"), P())
    return jax.shard_map(
        on_device, mesh=split, in_specs=placed, out_specs=P(FREQ, None, "tmpl"), check_vma=False
    )
```

```python
import functools
import math

import jax
import jax.numpy as jnp
from jax import lax
from jax.experimental import pallas as pl
from jax.experimental.pallas import tpu as pltpu
from jax.sharding import Mesh, PartitionSpec as P

A = 512
B = 1024
LEN = 524288
NB = 512


two_pi = 2.0 * math.pi
FREQ = ("fx", "fz", "fc")


def cos_sin_table(row_ids, col_ids, modulus):
    product = row_ids[:, None] * col_ids[None, :] % modulus
    phase_angle = product.astype(jnp.float32) * (two_pi / modulus)
    return (jnp.cos(phase_angle), jnp.sin(phase_angle))


def intersect_kernel(ph_ref, dat_ref, tm_ref, out_ref, lhs_ref):
    step = pl.program_id(0)
    seg_count = dat_ref.shape[2]
    lag_total = ph_ref.shape[2]
    rows = seg_count * lag_total
    chunk = 8

    @pl.when(step == 0)
    def _():
        out_ref[...] = jnp.zeros_like(out_ref)

    lag_cos = ph_ref[0, 0][None]
    lag_sin = ph_ref[0, 1][None]

    def build(i, carry):
        s0 = pl.multiple_of(i * chunk, chunk)
        data_real = dat_ref[0, 0, pl.ds(s0, chunk), :].astype(jnp.float32)[:, None, :]
        data_imag = dat_ref[0, 1, pl.ds(s0, chunk), :].astype(jnp.float32)[:, None, :]
        real_q = data_real * lag_cos - data_imag * lag_sin
        imag_q = data_real * lag_sin + data_imag * lag_cos
        r0 = pl.multiple_of(i * chunk * lag_total, chunk * lag_total)
        lhs_ref[pl.ds(r0, chunk * lag_total), :] = real_q.reshape(chunk * lag_total, -1).astype(jnp.bfloat16)
        lhs_ref[pl.ds(rows + r0, chunk * lag_total), :] = imag_q.reshape(chunk * lag_total, -1).astype(jnp.bfloat16)
        return carry

    lax.fori_loop(0, seg_count // chunk, build, 0)
    dims = (((1,), (1,)), ((), ()))
    lhs = lhs_ref[...]
    with_re = lax.dot_general(lhs, tm_ref[0, 0], dims, preferred_element_type=jnp.float32)
    with_im = lax.dot_general(lhs, tm_ref[0, 1], dims, preferred_element_type=jnp.float32)
    real_sum = with_re[:rows] + with_im[rows:]
    imag_sum = with_re[rows:] - with_im[:rows]
    width = real_sum.shape[1]
    out_ref[:, 0:lag_total, :] += real_sum.reshape(seg_count, lag_total, width)
    out_ref[:, lag_total:, :] += imag_sum.reshape(seg_count, lag_total, width)


def intersect(data, templates, cutoffs, lags, first_block):
    blocks_here, _, seg_count, width = data.shape
    tmpl_local = templates.shape[0]
    lag_total = lags.shape[0]
    block_ids = first_block + jnp.arange(blocks_here, dtype=jnp.int32)
    position = jnp.arange(width, dtype=jnp.int32)
    phase_int = (A * (lags[:, None] * block_ids[None, :] % B))[:, :, None] + (
        lags[:, None] * position[None, :] % LEN
    )[:, None, :]
    phase_angle = (phase_int % LEN).astype(jnp.float32) * (two_pi / LEN)
    phases = jnp.stack([jnp.cos(phase_angle), jnp.sin(phase_angle)], axis=0).transpose(2, 0, 1, 3)
    keep = block_ids[None, None, :, None] < cutoffs[:, None, None, None]
    masked = jnp.where(keep, templates, jnp.zeros_like(templates)).transpose(2, 1, 0, 3)
    rows = seg_count * lag_total
    flops = 2 * 2 * (2 * rows) * width * tmpl_local * blocks_here
    moved = masked.size * 2 + data.size * 2 + phases.size * 4 + seg_count * 2 * lag_total * tmpl_local * 4
    return pl.pallas_call(
        intersect_kernel,
        out_shape=jax.ShapeDtypeStruct((seg_count, 2 * lag_total, tmpl_local), jnp.float32),
        grid=(blocks_here,),
        in_specs=[
            pl.BlockSpec((1, 2, lag_total, width), lambda j: (j, 0, 0, 0)),
            pl.BlockSpec((1, 2, seg_count, width), lambda j: (j, 0, 0, 0)),
            pl.BlockSpec((1, 2, tmpl_local, width), lambda j: (j, 0, 0, 0)),
        ],
        out_specs=pl.BlockSpec((seg_count, 2 * lag_total, tmpl_local), lambda j: (0, 0, 0)),
        scratch_shapes=[pltpu.VMEM((2 * rows, width), jnp.bfloat16)],
        compiler_params=pltpu.CompilerParams(dimension_semantics=("arbitrary",)),
        cost_estimate=pl.CostEstimate(flops=flops, transcendentals=0, bytes_accessed=moved),
    )(phases, data, masked)


def scatter_kernel(axis, size, x_ref, o_ref, recv_ref, send_sem, recv_sem):
    me = lax.axis_index(axis)
    piece = o_ref.shape[0]
    mesh_ids = pl.DeviceIdType.MESH
    barrier = pltpu.get_barrier_semaphore()
    for k in range(1, size):
        peer = lax.rem(me + k, size)
        pl.semaphore_signal(barrier, inc=1, device_id={axis: peer}, device_id_type=mesh_ids)
    pl.semaphore_wait(barrier, size - 1)
    copies = []
    for k in range(1, size):
        peer = lax.rem(me + k, size)
        copy = pltpu.make_async_remote_copy(
            src_ref=x_ref.at[pl.ds(peer * piece, piece)],
            dst_ref=recv_ref.at[k],
            send_sem=send_sem.at[k],
            recv_sem=recv_sem.at[k],
            device_id={axis: peer},
            device_id_type=mesh_ids,
        )
        copy.start()
        copies.append(copy)
    for copy in copies:
        copy.wait()
    total = x_ref[pl.ds(me * piece, piece)]
    for k in range(1, size):
        total = total + recv_ref[k]
    o_ref[...] = total


def scatter_sum(parts, axis, collective_id):
    size = lax.axis_size(axis)
    piece = parts.shape[0] // size
    out_shape = (piece,) + parts.shape[1:]
    vmem = pltpu.VMEM
    return pl.pallas_call(
        functools.partial(scatter_kernel, axis, size),
        out_shape=jax.ShapeDtypeStruct(out_shape, parts.dtype),
        in_specs=[pl.BlockSpec(memory_space=vmem)],
        out_specs=pl.BlockSpec(memory_space=vmem),
        scratch_shapes=[
            vmem((size,) + out_shape, parts.dtype),
            pltpu.SemaphoreType.DMA((size,)),
            pltpu.SemaphoreType.DMA((size,)),
        ],
        compiler_params=pltpu.CompilerParams(collective_id=collective_id, has_side_effects=True),
    )(parts)


def gather_kernel(axis, size, x_ref, o_ref, send_sem, recv_sem):
    me = lax.axis_index(axis)
    mesh_ids = pl.DeviceIdType.MESH
    barrier = pltpu.get_barrier_semaphore()
    for k in range(1, size):
        peer = lax.rem(me + k, size)
        pl.semaphore_signal(barrier, inc=1, device_id={axis: peer}, device_id_type=mesh_ids)
    pl.semaphore_wait(barrier, size - 1)
    copies = []
    for k in range(1, size):
        peer = lax.rem(me + k, size)
        copy = pltpu.make_async_remote_copy(
            src_ref=x_ref,
            dst_ref=o_ref.at[me],
            send_sem=send_sem.at[k],
            recv_sem=recv_sem.at[k],
            device_id={axis: peer},
            device_id_type=mesh_ids,
        )
        copy.start()
        copies.append(copy)
    o_ref[me] = x_ref[...]
    for copy in copies:
        copy.wait()


def gather_all(block, axis, collective_id):
    size = lax.axis_size(axis)
    vmem = pltpu.VMEM
    return pl.pallas_call(
        functools.partial(gather_kernel, axis, size),
        out_shape=jax.ShapeDtypeStruct((size,) + block.shape, block.dtype),
        in_specs=[pl.BlockSpec(memory_space=vmem)],
        out_specs=pl.BlockSpec(memory_space=vmem),
        scratch_shapes=[pltpu.SemaphoreType.DMA((size,)), pltpu.SemaphoreType.DMA((size,))],
        compiler_params=pltpu.CompilerParams(collective_id=collective_id, has_side_effects=True),
    )(block)


def spectrum_blocks(strain, psd):
    freq_count = lax.axis_size(FREQ)
    freq_index = lax.axis_index(FREQ)
    seg_local = strain.shape[0]
    rows_here = A // freq_count
    cols_here = B // freq_count
    highest = lax.Precision.HIGHEST
    first_cos, first_sin = cos_sin_table(
        jnp.arange(A, dtype=jnp.int32), jnp.arange(A, dtype=jnp.int32), A
    )
    first_table = jnp.concatenate([first_cos, -first_sin], axis=0)
    sent = strain.reshape(seg_local, rows_here, freq_count, cols_here).transpose(2, 1, 3, 0)
    sent = sent.reshape(freq_count, rows_here, cols_here * seg_local)
    slab = lax.all_to_all(sent, FREQ, 0, 0, tiled=True).reshape(A, cols_here * seg_local)
    both_parts = jnp.dot(first_table, slab, precision=highest)
    real_part = both_parts[:A]
    imag_part = both_parts[A:]
    column_ids = jnp.arange(cols_here * seg_local, dtype=jnp.int32) // seg_local
    time_ids = freq_index * cols_here + column_ids
    twist_cos, twist_sin = cos_sin_table(jnp.arange(A, dtype=jnp.int32), time_ids, LEN)
    p_here = A // freq_count
    shaped = (freq_count, p_here, cols_here * seg_local)
    real_part = real_part.reshape(shaped)
    imag_part = imag_part.reshape(shaped)
    twist_cos = twist_cos.reshape(shaped)
    twist_sin = twist_sin.reshape(shaped)
    twisted = jnp.stack(
        [real_part * twist_cos + imag_part * twist_sin, imag_part * twist_cos - real_part * twist_sin],
        axis=1,
    )
    twisted = twisted.reshape(freq_count, 2 * p_here, cols_here * seg_local)
    columns = lax.all_to_all(twisted, FREQ, 0, 0, tiled=True)
    columns = columns.reshape(freq_count, 2, p_here, cols_here, seg_local).transpose(0, 3, 1, 2, 4)
    columns = columns.reshape(B, 2 * p_here * seg_local)
    split = 32
    j_ids = jnp.arange(NB, dtype=jnp.int32)
    high_cos, high_sin = cos_sin_table(j_ids, split * jnp.arange(B // split, dtype=jnp.int32), B)
    low_cos, low_sin = cos_sin_table(j_ids, jnp.arange(split, dtype=jnp.int32), B)
    second_cos = (
        high_cos[:, :, None] * low_cos[:, None, :] - high_sin[:, :, None] * low_sin[:, None, :]
    ).reshape(NB, B)
    second_sin = (
        high_sin[:, :, None] * low_cos[:, None, :] + high_cos[:, :, None] * low_sin[:, None, :]
    ).reshape(NB, B)
    with_cos = jnp.dot(second_cos, columns, precision=highest).reshape(NB, 2, p_here, seg_local)
    with_sin = jnp.dot(second_sin, columns, precision=highest).reshape(NB, 2, p_here, seg_local)
    amplitude = jnp.sqrt(LEN * psd)[:, :, None]
    real_out = (with_cos[:, 0] + with_sin[:, 1]) / amplitude
    imag_out = (with_cos[:, 1] - with_sin[:, 0]) / amplitude
    whitened = jnp.stack([real_out, imag_out], axis=1).transpose(3, 1, 0, 2).astype(jnp.bfloat16)
    return lax.all_to_all(whitened, FREQ, split_axis=2, concat_axis=3, tiled=True)


def on_device(strain, psd, templates, cutoffs, lags):
    freq_index = lax.axis_index(FREQ)
    local_data = spectrum_blocks(strain, psd)
    seg_piece = gather_all(local_data, "tmpl", 4)
    seg_piece = seg_piece.reshape((-1,) + local_data.shape[1:])
    x_size, z_size, c_size = (lax.axis_size(name) for name in FREQ)
    seg_order = seg_piece.reshape((x_size, z_size, c_size) + seg_piece.shape[1:])
    seg_order = seg_order.transpose(2, 0, 1, 3, 4, 5).reshape(seg_piece.shape)
    data = seg_order.transpose(2, 1, 0, 3)
    j_here = data.shape[0]
    first_block = freq_index * j_here
    partial_sums = intersect(data, templates, cutoffs, lags, first_block)
    for collective_id, name in enumerate(("fc", "fx", "fz")):
        partial_sums = scatter_sum(partial_sums, name, collective_id + 1)
    return partial_sums


def solution(mesh):
    tmpl_size, freq_size = mesh.devices.shape
    split = Mesh(
        mesh.devices.reshape(tmpl_size, 4, freq_size // 8, 2), ("tmpl",) + FREQ
    )
    placed = (P("tmpl", FREQ), P(None, FREQ), P("tmpl", None, FREQ, None), P("tmpl"), P())
    return jax.shard_map(
        on_device, mesh=split, in_specs=placed, out_specs=P(FREQ, None, "tmpl"), check_vma=False
    )
```

```python
import functools
import math

import jax
import jax.numpy as jnp
from jax import lax
from jax.experimental import pallas as pl
from jax.experimental.pallas import tpu as pltpu
from jax.sharding import Mesh, PartitionSpec as P

A = 512
B = 1024
LEN = 524288
NB = 512


two_pi = 2.0 * math.pi
FREQ = ("fx", "fz", "fc")


def cos_sin_table(row_ids, col_ids, modulus):
    product = row_ids[:, None] * col_ids[None, :] % modulus
    phase_angle = product.astype(jnp.float32) * (two_pi / modulus)
    return (jnp.cos(phase_angle), jnp.sin(phase_angle))


def intersect_kernel(ph_ref, dat_ref, tm_ref, out_ref, lhs_ref):
    step = pl.program_id(0)
    seg_count = dat_ref.shape[2]
    lag_total = ph_ref.shape[2]
    rows = seg_count * lag_total
    chunk = 8

    @pl.when(step == 0)
    def _():
        out_ref[...] = jnp.zeros_like(out_ref)

    lag_cos = ph_ref[0, 0][None]
    lag_sin = ph_ref[0, 1][None]

    def build(i, carry):
        s0 = pl.multiple_of(i * chunk, chunk)
        data_real = dat_ref[0, 0, pl.ds(s0, chunk), :].astype(jnp.float32)[:, None, :]
        data_imag = dat_ref[0, 1, pl.ds(s0, chunk), :].astype(jnp.float32)[:, None, :]
        real_q = data_real * lag_cos - data_imag * lag_sin
        imag_q = data_real * lag_sin + data_imag * lag_cos
        r0 = pl.multiple_of(i * chunk * lag_total, chunk * lag_total)
        lhs_ref[pl.ds(r0, chunk * lag_total), :] = real_q.reshape(chunk * lag_total, -1).astype(jnp.bfloat16)
        lhs_ref[pl.ds(rows + r0, chunk * lag_total), :] = imag_q.reshape(chunk * lag_total, -1).astype(jnp.bfloat16)
        return carry

    lax.fori_loop(0, seg_count // chunk, build, 0)
    dims = (((1,), (0,)), ((), ()))
    lhs = lhs_ref[...]
    with_re = lax.dot_general(lhs, tm_ref[0, 0], dims, preferred_element_type=jnp.float32)
    with_im = lax.dot_general(lhs, tm_ref[0, 1], dims, preferred_element_type=jnp.float32)
    real_sum = with_re[:rows] + with_im[rows:]
    imag_sum = with_re[rows:] - with_im[:rows]
    width = real_sum.shape[1]
    out_ref[:, 0:lag_total, :] += real_sum.reshape(seg_count, lag_total, width)
    out_ref[:, lag_total:, :] += imag_sum.reshape(seg_count, lag_total, width)


def intersect(data, templates, cutoffs, lags, first_block):
    blocks_here, _, seg_count, width = data.shape
    tmpl_local = templates.shape[0]
    lag_total = lags.shape[0]
    block_ids = first_block + jnp.arange(blocks_here, dtype=jnp.int32)
    position = jnp.arange(width, dtype=jnp.int32)
    phase_int = (A * (lags[:, None] * block_ids[None, :] % B))[:, :, None] + (
        lags[:, None] * position[None, :] % LEN
    )[:, None, :]
    phase_angle = (phase_int % LEN).astype(jnp.float32) * (two_pi / LEN)
    phases = jnp.stack([jnp.cos(phase_angle), jnp.sin(phase_angle)], axis=0).transpose(2, 0, 1, 3)
    keep = block_ids[None, None, :, None] < cutoffs[:, None, None, None]
    masked = jnp.where(keep, templates, jnp.zeros_like(templates)).transpose(2, 1, 3, 0)
    rows = seg_count * lag_total
    flops = 2 * 2 * (2 * rows) * width * tmpl_local * blocks_here
    moved = masked.size * 2 + data.size * 2 + phases.size * 4 + seg_count * 2 * lag_total * tmpl_local * 4
    return pl.pallas_call(
        intersect_kernel,
        out_shape=jax.ShapeDtypeStruct((seg_count, 2 * lag_total, tmpl_local), jnp.float32),
        grid=(blocks_here,),
        in_specs=[
            pl.BlockSpec((1, 2, lag_total, width), lambda j: (j, 0, 0, 0)),
            pl.BlockSpec((1, 2, seg_count, width), lambda j: (j, 0, 0, 0)),
            pl.BlockSpec((1, 2, width, tmpl_local), lambda j: (j, 0, 0, 0)),
        ],
        out_specs=pl.BlockSpec((seg_count, 2 * lag_total, tmpl_local), lambda j: (0, 0, 0)),
        scratch_shapes=[pltpu.VMEM((2 * rows, width), jnp.bfloat16)],
        compiler_params=pltpu.CompilerParams(dimension_semantics=("arbitrary",)),
        cost_estimate=pl.CostEstimate(flops=flops, transcendentals=0, bytes_accessed=moved),
    )(phases, data, masked)


def scatter_kernel(axis, size, x_ref, o_ref, recv_ref, send_sem, recv_sem):
    me = lax.axis_index(axis)
    piece = o_ref.shape[0]
    mesh_ids = pl.DeviceIdType.MESH
    barrier = pltpu.get_barrier_semaphore()
    for k in range(1, size):
        peer = lax.rem(me + k, size)
        pl.semaphore_signal(barrier, inc=1, device_id={axis: peer}, device_id_type=mesh_ids)
    pl.semaphore_wait(barrier, size - 1)
    copies = []
    for k in range(1, size):
        peer = lax.rem(me + k, size)
        copy = pltpu.make_async_remote_copy(
            src_ref=x_ref.at[pl.ds(peer * piece, piece)],
            dst_ref=recv_ref.at[k],
            send_sem=send_sem.at[k],
            recv_sem=recv_sem.at[k],
            device_id={axis: peer},
            device_id_type=mesh_ids,
        )
        copy.start()
        copies.append(copy)
    for copy in copies:
        copy.wait()
    total = x_ref[pl.ds(me * piece, piece)]
    for k in range(1, size):
        total = total + recv_ref[k]
    o_ref[...] = total


def scatter_sum(parts, axis, collective_id):
    size = lax.axis_size(axis)
    piece = parts.shape[0] // size
    out_shape = (piece,) + parts.shape[1:]
    vmem = pltpu.VMEM
    return pl.pallas_call(
        functools.partial(scatter_kernel, axis, size),
        out_shape=jax.ShapeDtypeStruct(out_shape, parts.dtype),
        in_specs=[pl.BlockSpec(memory_space=vmem)],
        out_specs=pl.BlockSpec(memory_space=vmem),
        scratch_shapes=[
            vmem((size,) + out_shape, parts.dtype),
            pltpu.SemaphoreType.DMA((size,)),
            pltpu.SemaphoreType.DMA((size,)),
        ],
        compiler_params=pltpu.CompilerParams(collective_id=collective_id, has_side_effects=True),
    )(parts)


def gather_kernel(axis, size, x_ref, o_ref, send_sem, recv_sem):
    me = lax.axis_index(axis)
    mesh_ids = pl.DeviceIdType.MESH
    barrier = pltpu.get_barrier_semaphore()
    for k in range(1, size):
        peer = lax.rem(me + k, size)
        pl.semaphore_signal(barrier, inc=1, device_id={axis: peer}, device_id_type=mesh_ids)
    pl.semaphore_wait(barrier, size - 1)
    copies = []
    for k in range(1, size):
        peer = lax.rem(me + k, size)
        copy = pltpu.make_async_remote_copy(
            src_ref=x_ref,
            dst_ref=o_ref.at[me],
            send_sem=send_sem.at[k],
            recv_sem=recv_sem.at[k],
            device_id={axis: peer},
            device_id_type=mesh_ids,
        )
        copy.start()
        copies.append(copy)
    o_ref[me] = x_ref[...]
    for copy in copies:
        copy.wait()


def gather_all(block, axis, collective_id):
    size = lax.axis_size(axis)
    vmem = pltpu.VMEM
    return pl.pallas_call(
        functools.partial(gather_kernel, axis, size),
        out_shape=jax.ShapeDtypeStruct((size,) + block.shape, block.dtype),
        in_specs=[pl.BlockSpec(memory_space=vmem)],
        out_specs=pl.BlockSpec(memory_space=vmem),
        scratch_shapes=[pltpu.SemaphoreType.DMA((size,)), pltpu.SemaphoreType.DMA((size,))],
        compiler_params=pltpu.CompilerParams(collective_id=collective_id, has_side_effects=True),
    )(block)


def spectrum_blocks(strain, psd):
    freq_count = lax.axis_size(FREQ)
    freq_index = lax.axis_index(FREQ)
    seg_local = strain.shape[0]
    rows_here = A // freq_count
    cols_here = B // freq_count
    highest = lax.Precision.HIGHEST
    first_cos, first_sin = cos_sin_table(
        jnp.arange(A, dtype=jnp.int32), jnp.arange(A, dtype=jnp.int32), A
    )
    first_table = jnp.concatenate([first_cos, -first_sin], axis=0)
    sent = strain.reshape(seg_local, rows_here, freq_count, cols_here).transpose(2, 1, 3, 0)
    sent = sent.reshape(freq_count, rows_here, cols_here * seg_local)
    slab = lax.all_to_all(sent, FREQ, 0, 0, tiled=True).reshape(A, cols_here * seg_local)
    both_parts = jnp.dot(first_table, slab, precision=highest)
    real_part = both_parts[:A]
    imag_part = both_parts[A:]
    time_ids = freq_index * cols_here + jnp.arange(cols_here, dtype=jnp.int32)
    twist_cos, twist_sin = cos_sin_table(jnp.arange(A, dtype=jnp.int32), time_ids, LEN)
    twist_cos = jnp.repeat(twist_cos, seg_local, axis=1)
    twist_sin = jnp.repeat(twist_sin, seg_local, axis=1)
    twisted = jnp.stack(
        [real_part * twist_cos + imag_part * twist_sin, imag_part * twist_cos - real_part * twist_sin]
    )
    p_here = A // freq_count
    twisted = twisted.reshape(2, freq_count, p_here, cols_here, seg_local).transpose(1, 3, 0, 2, 4)
    twisted = twisted.reshape(freq_count, cols_here, 2 * p_here * seg_local)
    columns = lax.all_to_all(twisted, FREQ, 0, 0, tiled=True).reshape(B, 2 * p_here * seg_local)
    split = 32
    j_ids = jnp.arange(NB, dtype=jnp.int32)
    high_cos, high_sin = cos_sin_table(j_ids, split * jnp.arange(B // split, dtype=jnp.int32), B)
    low_cos, low_sin = cos_sin_table(j_ids, jnp.arange(split, dtype=jnp.int32), B)
    second_cos = (
        high_cos[:, :, None] * low_cos[:, None, :] - high_sin[:, :, None] * low_sin[:, None, :]
    ).reshape(NB, B)
    second_sin = (
        high_sin[:, :, None] * low_cos[:, None, :] + high_cos[:, :, None] * low_sin[:, None, :]
    ).reshape(NB, B)
    with_cos = jnp.dot(second_cos, columns, precision=highest).reshape(NB, 2, p_here, seg_local)
    with_sin = jnp.dot(second_sin, columns, precision=highest).reshape(NB, 2, p_here, seg_local)
    amplitude = jnp.sqrt(LEN * psd)[:, :, None]
    real_out = (with_cos[:, 0] + with_sin[:, 1]) / amplitude
    imag_out = (with_cos[:, 1] - with_sin[:, 0]) / amplitude
    whitened = jnp.stack([real_out, imag_out], axis=1).transpose(3, 1, 0, 2).astype(jnp.bfloat16)
    return lax.all_to_all(whitened, FREQ, split_axis=2, concat_axis=3, tiled=True)


def on_device(strain, psd, templates, cutoffs, lags):
    freq_index = lax.axis_index(FREQ)
    local_data = spectrum_blocks(strain, psd)
    seg_piece = gather_all(local_data, "tmpl", 4)
    seg_piece = seg_piece.reshape((-1,) + local_data.shape[1:])
    x_size, z_size, c_size = (lax.axis_size(name) for name in FREQ)
    seg_order = seg_piece.reshape((x_size, z_size, c_size) + seg_piece.shape[1:])
    seg_order = seg_order.transpose(2, 0, 1, 3, 4, 5).reshape(seg_piece.shape)
    data = seg_order.transpose(2, 1, 0, 3)
    j_here = data.shape[0]
    first_block = freq_index * j_here
    partial_sums = intersect(data, templates, cutoffs, lags, first_block)
    for collective_id, name in enumerate(("fc", "fx", "fz")):
        partial_sums = scatter_sum(partial_sums, name, collective_id + 1)
    return partial_sums


def solution(mesh):
    tmpl_size, freq_size = mesh.devices.shape
    split = Mesh(
        mesh.devices.reshape(tmpl_size, 4, freq_size // 8, 2), ("tmpl",) + FREQ
    )
    placed = (P("tmpl", FREQ), P(None, FREQ), P("tmpl", None, FREQ, None), P("tmpl"), P())
    return jax.shard_map(
        on_device, mesh=split, in_specs=placed, out_specs=P(FREQ, None, "tmpl"), check_vma=False
    )
```

```python
import functools
import math

import jax
import jax.numpy as jnp
from jax import lax
from jax.experimental import pallas as pl
from jax.experimental.pallas import tpu as pltpu
from jax.sharding import Mesh, PartitionSpec as P

A = 512
B = 1024
LEN = 524288
NB = 512


two_pi = 2.0 * math.pi
FREQ = ("fx", "fz", "fc")


def cos_sin_table(row_ids, col_ids, modulus):
    product = row_ids[:, None] * col_ids[None, :] % modulus
    phase_angle = product.astype(jnp.float32) * (two_pi / modulus)
    return (jnp.cos(phase_angle), jnp.sin(phase_angle))


def intersect_kernel(ph_ref, dat_ref, tm_ref, out_ref, lhs_ref):
    step = pl.program_id(0)
    tmpl_count, _, _, core_count, chunk, _ = dat_ref.shape
    seg_count = tmpl_count * core_count * chunk
    lag_total = ph_ref.shape[2]
    rows = seg_count * lag_total

    @pl.when(step == 0)
    def _():
        out_ref[...] = jnp.zeros_like(out_ref)

    lag_cos = ph_ref[0, 0][None]
    lag_sin = ph_ref[0, 1][None]

    def build(i, carry):
        row = lax.rem(i, tmpl_count)
        core = i // tmpl_count
        data_real = dat_ref[row, 0, 0, core].astype(jnp.float32)[:, None, :]
        data_imag = dat_ref[row, 0, 1, core].astype(jnp.float32)[:, None, :]
        real_q = data_real * lag_cos - data_imag * lag_sin
        imag_q = data_real * lag_sin + data_imag * lag_cos
        r0 = pl.multiple_of(i * chunk * lag_total, chunk * lag_total)
        lhs_ref[pl.ds(r0, chunk * lag_total), :] = real_q.reshape(chunk * lag_total, -1).astype(jnp.bfloat16)
        lhs_ref[pl.ds(rows + r0, chunk * lag_total), :] = imag_q.reshape(chunk * lag_total, -1).astype(jnp.bfloat16)
        return carry

    lax.fori_loop(0, seg_count // chunk, build, 0)
    dims = (((1,), (0,)), ((), ()))
    lhs = lhs_ref[...]
    with_re = lax.dot_general(lhs, tm_ref[0, 0], dims, preferred_element_type=jnp.float32)
    with_im = lax.dot_general(lhs, tm_ref[0, 1], dims, preferred_element_type=jnp.float32)
    real_sum = with_re[:rows] + with_im[rows:]
    imag_sum = with_re[rows:] - with_im[:rows]
    width = real_sum.shape[1]
    out_ref[:, 0:lag_total, :] += real_sum.reshape(seg_count, lag_total, width)
    out_ref[:, lag_total:, :] += imag_sum.reshape(seg_count, lag_total, width)


def intersect(data, templates, cutoffs, lags, first_block):
    tmpl_count, blocks_here, _, core_count, chunk, width = data.shape
    seg_count = tmpl_count * core_count * chunk
    tmpl_local = templates.shape[0]
    lag_total = lags.shape[0]
    block_ids = first_block + jnp.arange(blocks_here, dtype=jnp.int32)
    position = jnp.arange(width, dtype=jnp.int32)
    phase_int = (A * (lags[:, None] * block_ids[None, :] % B))[:, :, None] + (
        lags[:, None] * position[None, :] % LEN
    )[:, None, :]
    phase_angle = (phase_int % LEN).astype(jnp.float32) * (two_pi / LEN)
    phases = jnp.stack([jnp.cos(phase_angle), jnp.sin(phase_angle)], axis=0).transpose(2, 0, 1, 3)
    keep = block_ids[None, None, :, None] < cutoffs[:, None, None, None]
    masked = jnp.where(keep, templates, jnp.zeros_like(templates)).transpose(2, 1, 3, 0)
    rows = seg_count * lag_total
    flops = 2 * 2 * (2 * rows) * width * tmpl_local * blocks_here
    moved = masked.size * 2 + data.size * 2 + phases.size * 4 + seg_count * 2 * lag_total * tmpl_local * 4
    return pl.pallas_call(
        intersect_kernel,
        out_shape=jax.ShapeDtypeStruct((seg_count, 2 * lag_total, tmpl_local), jnp.float32),
        grid=(blocks_here,),
        in_specs=[
            pl.BlockSpec((1, 2, lag_total, width), lambda j: (j, 0, 0, 0)),
            pl.BlockSpec((tmpl_count, 1, 2, core_count, chunk, width), lambda j: (0, j, 0, 0, 0, 0)),
            pl.BlockSpec((1, 2, width, tmpl_local), lambda j: (j, 0, 0, 0)),
        ],
        out_specs=pl.BlockSpec((seg_count, 2 * lag_total, tmpl_local), lambda j: (0, 0, 0)),
        scratch_shapes=[pltpu.VMEM((2 * rows, width), jnp.bfloat16)],
        compiler_params=pltpu.CompilerParams(dimension_semantics=("arbitrary",)),
        cost_estimate=pl.CostEstimate(flops=flops, transcendentals=0, bytes_accessed=moved),
    )(phases, data, masked)


def scatter_kernel(axis, size, x_ref, o_ref, recv_ref, send_sem, recv_sem):
    me = lax.axis_index(axis)
    piece = o_ref.shape[0]
    mesh_ids = pl.DeviceIdType.MESH
    barrier = pltpu.get_barrier_semaphore()
    for k in range(1, size):
        peer = lax.rem(me + k, size)
        pl.semaphore_signal(barrier, inc=1, device_id={axis: peer}, device_id_type=mesh_ids)
    pl.semaphore_wait(barrier, size - 1)
    copies = []
    for k in range(1, size):
        peer = lax.rem(me + k, size)
        copy = pltpu.make_async_remote_copy(
            src_ref=x_ref.at[pl.ds(peer * piece, piece)],
            dst_ref=recv_ref.at[k],
            send_sem=send_sem.at[k],
            recv_sem=recv_sem.at[k],
            device_id={axis: peer},
            device_id_type=mesh_ids,
        )
        copy.start()
        copies.append(copy)
    for copy in copies:
        copy.wait()
    total = x_ref[pl.ds(me * piece, piece)]
    for k in range(1, size):
        total = total + recv_ref[k]
    o_ref[...] = total


def scatter_sum(parts, axis, collective_id):
    size = lax.axis_size(axis)
    piece = parts.shape[0] // size
    out_shape = (piece,) + parts.shape[1:]
    vmem = pltpu.VMEM
    return pl.pallas_call(
        functools.partial(scatter_kernel, axis, size),
        out_shape=jax.ShapeDtypeStruct(out_shape, parts.dtype),
        in_specs=[pl.BlockSpec(memory_space=vmem)],
        out_specs=pl.BlockSpec(memory_space=vmem),
        scratch_shapes=[
            vmem((size,) + out_shape, parts.dtype),
            pltpu.SemaphoreType.DMA((size,)),
            pltpu.SemaphoreType.DMA((size,)),
        ],
        compiler_params=pltpu.CompilerParams(collective_id=collective_id, has_side_effects=True),
    )(parts)


def gather_kernel(axis, size, x_ref, o_ref, send_sem, recv_sem):
    me = lax.axis_index(axis)
    mesh_ids = pl.DeviceIdType.MESH
    barrier = pltpu.get_barrier_semaphore()
    for k in range(1, size):
        peer = lax.rem(me + k, size)
        pl.semaphore_signal(barrier, inc=1, device_id={axis: peer}, device_id_type=mesh_ids)
    pl.semaphore_wait(barrier, size - 1)
    copies = []
    for k in range(1, size):
        peer = lax.rem(me + k, size)
        copy = pltpu.make_async_remote_copy(
            src_ref=x_ref,
            dst_ref=o_ref.at[me],
            send_sem=send_sem.at[k],
            recv_sem=recv_sem.at[k],
            device_id={axis: peer},
            device_id_type=mesh_ids,
        )
        copy.start()
        copies.append(copy)
    o_ref[me] = x_ref[...]
    for copy in copies:
        copy.wait()


def gather_all(block, axis, collective_id):
    size = lax.axis_size(axis)
    vmem = pltpu.VMEM
    return pl.pallas_call(
        functools.partial(gather_kernel, axis, size),
        out_shape=jax.ShapeDtypeStruct((size,) + block.shape, block.dtype),
        in_specs=[pl.BlockSpec(memory_space=vmem)],
        out_specs=pl.BlockSpec(memory_space=vmem),
        scratch_shapes=[pltpu.SemaphoreType.DMA((size,)), pltpu.SemaphoreType.DMA((size,))],
        compiler_params=pltpu.CompilerParams(collective_id=collective_id, has_side_effects=True),
    )(block)


def spectrum_blocks(strain, psd):
    freq_count = lax.axis_size(FREQ)
    freq_index = lax.axis_index(FREQ)
    seg_local = strain.shape[0]
    rows_here = A // freq_count
    cols_here = B // freq_count
    highest = lax.Precision.HIGHEST
    first_cos, first_sin = cos_sin_table(
        jnp.arange(A, dtype=jnp.int32), jnp.arange(A, dtype=jnp.int32), A
    )
    first_table = jnp.concatenate([first_cos, -first_sin], axis=0)
    sent = strain.reshape(seg_local, rows_here, freq_count, cols_here).transpose(2, 1, 3, 0)
    sent = sent.reshape(freq_count, rows_here, cols_here * seg_local)
    slab = lax.all_to_all(sent, FREQ, 0, 0, tiled=True).reshape(A, cols_here * seg_local)
    both_parts = jnp.dot(first_table, slab, precision=highest)
    real_part = both_parts[:A]
    imag_part = both_parts[A:]
    time_ids = freq_index * cols_here + jnp.arange(cols_here, dtype=jnp.int32)
    twist_cos, twist_sin = cos_sin_table(jnp.arange(A, dtype=jnp.int32), time_ids, LEN)
    twist_cos = jnp.repeat(twist_cos, seg_local, axis=1)
    twist_sin = jnp.repeat(twist_sin, seg_local, axis=1)
    twisted = jnp.stack(
        [real_part * twist_cos + imag_part * twist_sin, imag_part * twist_cos - real_part * twist_sin]
    )
    p_here = A // freq_count
    twisted = twisted.reshape(2, freq_count, p_here, cols_here, seg_local).transpose(1, 3, 0, 2, 4)
    twisted = twisted.reshape(freq_count, cols_here, 2 * p_here * seg_local)
    columns = lax.all_to_all(twisted, FREQ, 0, 0, tiled=True).reshape(B, 2 * p_here * seg_local)
    split = 32
    j_ids = jnp.arange(NB, dtype=jnp.int32)
    high_cos, high_sin = cos_sin_table(j_ids, split * jnp.arange(B // split, dtype=jnp.int32), B)
    low_cos, low_sin = cos_sin_table(j_ids, jnp.arange(split, dtype=jnp.int32), B)
    second_cos = (
        high_cos[:, :, None] * low_cos[:, None, :] - high_sin[:, :, None] * low_sin[:, None, :]
    ).reshape(NB, B)
    second_sin = (
        high_sin[:, :, None] * low_cos[:, None, :] + high_cos[:, :, None] * low_sin[:, None, :]
    ).reshape(NB, B)
    with_cos = jnp.dot(second_cos, columns, precision=highest).reshape(NB, 2, p_here, seg_local)
    with_sin = jnp.dot(second_sin, columns, precision=highest).reshape(NB, 2, p_here, seg_local)
    amplitude = jnp.sqrt(LEN * psd)[:, :, None]
    real_out = (with_cos[:, 0] + with_sin[:, 1]) / amplitude
    imag_out = (with_cos[:, 1] - with_sin[:, 0]) / amplitude
    whitened = jnp.stack([real_out, imag_out], axis=1).transpose(3, 1, 0, 2).astype(jnp.bfloat16)
    return lax.all_to_all(whitened, FREQ, split_axis=2, concat_axis=3, tiled=True)


def on_device(strain, psd, templates, cutoffs, lags):
    freq_index = lax.axis_index(FREQ)
    local_data = spectrum_blocks(strain, psd)
    x_size, z_size, c_size = (lax.axis_size(name) for name in FREQ)
    seg_local, _, j_here, width = local_data.shape
    local = local_data.reshape(z_size, c_size, 2, j_here, width).transpose(3, 2, 1, 0, 4)
    data = gather_all(local, "tmpl", 4)
    first_block = freq_index * j_here
    partial_sums = intersect(data, templates, cutoffs, lags, first_block)
    for collective_id, name in enumerate(("fc", "fx", "fz")):
        partial_sums = scatter_sum(partial_sums, name, collective_id + 1)
    return partial_sums


def solution(mesh):
    tmpl_size, freq_size = mesh.devices.shape
    split = Mesh(
        mesh.devices.reshape(tmpl_size, 4, freq_size // 8, 2), ("tmpl",) + FREQ
    )
    placed = (P("tmpl", FREQ), P(None, FREQ), P("tmpl", None, FREQ, None), P("tmpl"), P())
    return jax.shard_map(
        on_device, mesh=split, in_specs=placed, out_specs=P(FREQ, None, "tmpl"), check_vma=False
    )
```

```python
import functools
import math

import jax
import jax.numpy as jnp
from jax import lax
from jax.experimental import pallas as pl
from jax.experimental.pallas import tpu as pltpu
from jax.sharding import Mesh, PartitionSpec as P

A = 512
B = 1024
LEN = 524288
NB = 512


two_pi = 2.0 * math.pi
FREQ = ("fx", "fz", "fc")


def cos_sin_table(row_ids, col_ids, modulus):
    product = row_ids[:, None] * col_ids[None, :] % modulus
    phase_angle = product.astype(jnp.float32) * (two_pi / modulus)
    return (jnp.cos(phase_angle), jnp.sin(phase_angle))


def intersect_kernel(ph_ref, dat_ref, tm_ref, out_ref, lhs_ref):
    step = pl.program_id(0)
    seg_count = dat_ref.shape[2]
    lag_total = ph_ref.shape[2]
    rows = seg_count * lag_total
    chunk = 8

    @pl.when(step == 0)
    def _():
        out_ref[...] = jnp.zeros_like(out_ref)

    lag_cos = ph_ref[0, 0][None]
    lag_sin = ph_ref[0, 1][None]

    def build(i, carry):
        s0 = pl.multiple_of(i * chunk, chunk)
        data_real = dat_ref[0, 0, pl.ds(s0, chunk), :].astype(jnp.float32)[:, None, :]
        data_imag = dat_ref[0, 1, pl.ds(s0, chunk), :].astype(jnp.float32)[:, None, :]
        real_q = data_real * lag_cos - data_imag * lag_sin
        imag_q = data_real * lag_sin + data_imag * lag_cos
        r0 = pl.multiple_of(i * chunk * lag_total, chunk * lag_total)
        lhs_ref[pl.ds(r0, chunk * lag_total), :] = real_q.reshape(chunk * lag_total, -1).astype(jnp.bfloat16)
        lhs_ref[pl.ds(rows + r0, chunk * lag_total), :] = imag_q.reshape(chunk * lag_total, -1).astype(jnp.bfloat16)
        return carry

    lax.fori_loop(0, seg_count // chunk, build, 0)
    dims = (((1,), (1,)), ((), ()))
    lhs = lhs_ref[...]
    with_re = lax.dot_general(lhs, tm_ref[0, 0], dims, preferred_element_type=jnp.float32)
    with_im = lax.dot_general(lhs, tm_ref[0, 1], dims, preferred_element_type=jnp.float32)
    real_sum = with_re[:rows] + with_im[rows:]
    imag_sum = with_re[rows:] - with_im[:rows]
    width = real_sum.shape[1]
    out_ref[:, 0:lag_total, :] += real_sum.reshape(seg_count, lag_total, width)
    out_ref[:, lag_total:, :] += imag_sum.reshape(seg_count, lag_total, width)


def intersect(data, templates, cutoffs, lags, first_block):
    blocks_here, _, seg_count, width = data.shape
    tmpl_local = templates.shape[0]
    lag_total = lags.shape[0]
    block_ids = first_block + jnp.arange(blocks_here, dtype=jnp.int32)
    position = jnp.arange(width, dtype=jnp.int32)
    phase_int = (A * (lags[:, None] * block_ids[None, :] % B))[:, :, None] + (
        lags[:, None] * position[None, :] % LEN
    )[:, None, :]
    phase_angle = (phase_int % LEN).astype(jnp.float32) * (two_pi / LEN)
    phases = jnp.stack([jnp.cos(phase_angle), jnp.sin(phase_angle)], axis=0).transpose(2, 0, 1, 3)
    keep = block_ids[None, None, :, None] < cutoffs[:, None, None, None]
    masked = jnp.where(keep, templates, jnp.zeros_like(templates)).transpose(2, 1, 0, 3)
    rows = seg_count * lag_total
    flops = 2 * 2 * (2 * rows) * width * tmpl_local * blocks_here
    moved = masked.size * 2 + data.size * 2 + phases.size * 4 + seg_count * 2 * lag_total * tmpl_local * 4
    return pl.pallas_call(
        intersect_kernel,
        out_shape=jax.ShapeDtypeStruct((seg_count, 2 * lag_total, tmpl_local), jnp.float32),
        grid=(blocks_here,),
        in_specs=[
            pl.BlockSpec((1, 2, lag_total, width), lambda j: (j, 0, 0, 0)),
            pl.BlockSpec((1, 2, seg_count, width), lambda j: (j, 0, 0, 0)),
            pl.BlockSpec((1, 2, tmpl_local, width), lambda j: (j, 0, 0, 0)),
        ],
        out_specs=pl.BlockSpec((seg_count, 2 * lag_total, tmpl_local), lambda j: (0, 0, 0)),
        scratch_shapes=[pltpu.VMEM((2 * rows, width), jnp.bfloat16)],
        compiler_params=pltpu.CompilerParams(dimension_semantics=("arbitrary",)),
        cost_estimate=pl.CostEstimate(flops=flops, transcendentals=0, bytes_accessed=moved),
    )(phases, data, masked)


def peer_id(axes, flat):
    coords = {}
    for name in reversed(axes):
        coords[name] = lax.rem(flat, lax.axis_size(name))
        flat = flat // lax.axis_size(name)
    return coords


def scatter_kernel(axes, size, x_ref, o_ref, recv_ref, send_sem, recv_sem):
    me = lax.axis_index(axes)
    piece = o_ref.shape[0]
    mesh_ids = pl.DeviceIdType.MESH
    barrier = pltpu.get_barrier_semaphore()
    for k in range(1, size):
        peer = peer_id(axes, lax.rem(me + k, size))
        pl.semaphore_signal(barrier, inc=1, device_id=peer, device_id_type=mesh_ids)
    pl.semaphore_wait(barrier, size - 1)
    copies = []
    for k in range(1, size):
        flat = lax.rem(me + k, size)
        copy = pltpu.make_async_remote_copy(
            src_ref=x_ref.at[pl.ds(flat * piece, piece)],
            dst_ref=recv_ref.at[k],
            send_sem=send_sem.at[k],
            recv_sem=recv_sem.at[k],
            device_id=peer_id(axes, flat),
            device_id_type=mesh_ids,
        )
        copy.start()
        copies.append(copy)
    for copy in copies:
        copy.wait()
    total = x_ref[pl.ds(me * piece, piece)]
    for k in range(1, size):
        total = total + recv_ref[k]
    o_ref[...] = total


def scatter_sum(parts, axes, collective_id):
    size = lax.axis_size(axes)
    piece = parts.shape[0] // size
    out_shape = (piece,) + parts.shape[1:]
    vmem = pltpu.VMEM
    return pl.pallas_call(
        functools.partial(scatter_kernel, axes, size),
        out_shape=jax.ShapeDtypeStruct(out_shape, parts.dtype),
        in_specs=[pl.BlockSpec(memory_space=vmem)],
        out_specs=pl.BlockSpec(memory_space=vmem),
        scratch_shapes=[
            vmem((size,) + out_shape, parts.dtype),
            pltpu.SemaphoreType.DMA((size,)),
            pltpu.SemaphoreType.DMA((size,)),
        ],
        compiler_params=pltpu.CompilerParams(collective_id=collective_id, has_side_effects=True),
    )(parts)


def gather_kernel(axis, size, x_ref, o_ref, send_sem, recv_sem):
    me = lax.axis_index(axis)
    mesh_ids = pl.DeviceIdType.MESH
    barrier = pltpu.get_barrier_semaphore()
    for k in range(1, size):
        peer = lax.rem(me + k, size)
        pl.semaphore_signal(barrier, inc=1, device_id={axis: peer}, device_id_type=mesh_ids)
    pl.semaphore_wait(barrier, size - 1)
    copies = []
    for k in range(1, size):
        peer = lax.rem(me + k, size)
        copy = pltpu.make_async_remote_copy(
            src_ref=x_ref,
            dst_ref=o_ref.at[me],
            send_sem=send_sem.at[k],
            recv_sem=recv_sem.at[k],
            device_id={axis: peer},
            device_id_type=mesh_ids,
        )
        copy.start()
        copies.append(copy)
    o_ref[me] = x_ref[...]
    for copy in copies:
        copy.wait()


def gather_all(block, axis, collective_id):
    size = lax.axis_size(axis)
    vmem = pltpu.VMEM
    return pl.pallas_call(
        functools.partial(gather_kernel, axis, size),
        out_shape=jax.ShapeDtypeStruct((size,) + block.shape, block.dtype),
        in_specs=[pl.BlockSpec(memory_space=vmem)],
        out_specs=pl.BlockSpec(memory_space=vmem),
        scratch_shapes=[pltpu.SemaphoreType.DMA((size,)), pltpu.SemaphoreType.DMA((size,))],
        compiler_params=pltpu.CompilerParams(collective_id=collective_id, has_side_effects=True),
    )(block)


def spectrum_blocks(strain, psd):
    freq_count = lax.axis_size(FREQ)
    freq_index = lax.axis_index(FREQ)
    seg_local = strain.shape[0]
    rows_here = A // freq_count
    cols_here = B // freq_count
    highest = lax.Precision.HIGHEST
    first_cos, first_sin = cos_sin_table(
        jnp.arange(A, dtype=jnp.int32), jnp.arange(A, dtype=jnp.int32), A
    )
    first_table = jnp.concatenate([first_cos, -first_sin], axis=0)
    sent = strain.reshape(seg_local, rows_here, freq_count, cols_here).transpose(2, 1, 3, 0)
    sent = sent.reshape(freq_count, rows_here, cols_here * seg_local)
    slab = lax.all_to_all(sent, FREQ, 0, 0, tiled=True).reshape(A, cols_here * seg_local)
    both_parts = jnp.dot(first_table, slab, precision=highest)
    real_part = both_parts[:A]
    imag_part = both_parts[A:]
    time_ids = freq_index * cols_here + jnp.arange(cols_here, dtype=jnp.int32)
    twist_cos, twist_sin = cos_sin_table(jnp.arange(A, dtype=jnp.int32), time_ids, LEN)
    twist_cos = jnp.repeat(twist_cos, seg_local, axis=1)
    twist_sin = jnp.repeat(twist_sin, seg_local, axis=1)
    twisted = jnp.stack(
        [real_part * twist_cos + imag_part * twist_sin, imag_part * twist_cos - real_part * twist_sin]
    )
    p_here = A // freq_count
    twisted = twisted.reshape(2, freq_count, p_here, cols_here, seg_local).transpose(1, 3, 0, 2, 4)
    twisted = twisted.reshape(freq_count, cols_here, 2 * p_here * seg_local)
    columns = lax.all_to_all(twisted, FREQ, 0, 0, tiled=True).reshape(B, 2 * p_here * seg_local)
    split = 32
    j_ids = jnp.arange(NB, dtype=jnp.int32)
    high_cos, high_sin = cos_sin_table(j_ids, split * jnp.arange(B // split, dtype=jnp.int32), B)
    low_cos, low_sin = cos_sin_table(j_ids, jnp.arange(split, dtype=jnp.int32), B)
    second_cos = (
        high_cos[:, :, None] * low_cos[:, None, :] - high_sin[:, :, None] * low_sin[:, None, :]
    ).reshape(NB, B)
    second_sin = (
        high_sin[:, :, None] * low_cos[:, None, :] + high_cos[:, :, None] * low_sin[:, None, :]
    ).reshape(NB, B)
    with_cos = jnp.dot(second_cos, columns, precision=highest).reshape(NB, 2, p_here, seg_local)
    with_sin = jnp.dot(second_sin, columns, precision=highest).reshape(NB, 2, p_here, seg_local)
    amplitude = jnp.sqrt(LEN * psd)[:, :, None]
    real_out = (with_cos[:, 0] + with_sin[:, 1]) / amplitude
    imag_out = (with_cos[:, 1] - with_sin[:, 0]) / amplitude
    whitened = jnp.stack([real_out, imag_out], axis=1).transpose(3, 1, 0, 2).astype(jnp.bfloat16)
    return lax.all_to_all(whitened, FREQ, split_axis=2, concat_axis=3, tiled=True)


def on_device(strain, psd, templates, cutoffs, lags):
    freq_index = lax.axis_index(FREQ)
    local_data = spectrum_blocks(strain, psd)
    seg_piece = gather_all(local_data, "tmpl", 4)
    seg_piece = seg_piece.reshape((-1,) + local_data.shape[1:])
    x_size, z_size, c_size = (lax.axis_size(name) for name in FREQ)
    seg_order = seg_piece.reshape((x_size, z_size, c_size) + seg_piece.shape[1:])
    seg_order = seg_order.transpose(2, 0, 1, 3, 4, 5).reshape(seg_piece.shape)
    data = seg_order.transpose(2, 1, 0, 3)
    j_here = data.shape[0]
    first_block = freq_index * j_here
    partial_sums = intersect(data, templates, cutoffs, lags, first_block)
    for collective_id, axes in enumerate((("fc",), ("fx", "fz"))):
        partial_sums = scatter_sum(partial_sums, axes, collective_id + 1)
    return partial_sums


def solution(mesh):
    tmpl_size, freq_size = mesh.devices.shape
    split = Mesh(
        mesh.devices.reshape(tmpl_size, 4, freq_size // 8, 2), ("tmpl",) + FREQ
    )
    placed = (P("tmpl", FREQ), P(None, FREQ), P("tmpl", None, FREQ, None), P("tmpl"), P())
    return jax.shard_map(
        on_device, mesh=split, in_specs=placed, out_specs=P(FREQ, None, "tmpl"), check_vma=False
    )
```

```python
import functools
import math

import jax
import jax.numpy as jnp
from jax import lax
from jax.experimental import pallas as pl
from jax.experimental.pallas import tpu as pltpu
from jax.sharding import Mesh, PartitionSpec as P

A = 512
B = 1024
LEN = 524288
NB = 512


two_pi = 2.0 * math.pi
FREQ = ("fx", "fz", "fc")


def cos_sin_table(row_ids, col_ids, modulus):
    product = row_ids[:, None] * col_ids[None, :] % modulus
    phase_angle = product.astype(jnp.float32) * (two_pi / modulus)
    return (jnp.cos(phase_angle), jnp.sin(phase_angle))


def intersect_kernel(ph_ref, dat_ref, tm_ref, out_ref, lhs_ref):
    step = pl.program_id(0)
    seg_count = dat_ref.shape[2]
    lag_total = ph_ref.shape[2]
    rows = seg_count * lag_total
    chunk = 8

    @pl.when(step == 0)
    def _():
        out_ref[...] = jnp.zeros_like(out_ref)

    lag_cos = ph_ref[0, 0][None]
    lag_sin = ph_ref[0, 1][None]

    def build(i, carry):
        s0 = pl.multiple_of(i * chunk, chunk)
        data_real = dat_ref[0, 0, pl.ds(s0, chunk), :].astype(jnp.float32)[:, None, :]
        data_imag = dat_ref[0, 1, pl.ds(s0, chunk), :].astype(jnp.float32)[:, None, :]
        real_q = data_real * lag_cos - data_imag * lag_sin
        imag_q = data_real * lag_sin + data_imag * lag_cos
        r0 = pl.multiple_of(i * chunk * lag_total, chunk * lag_total)
        lhs_ref[pl.ds(r0, chunk * lag_total), :] = real_q.reshape(chunk * lag_total, -1).astype(jnp.bfloat16)
        lhs_ref[pl.ds(rows + r0, chunk * lag_total), :] = imag_q.reshape(chunk * lag_total, -1).astype(jnp.bfloat16)
        return carry

    lax.fori_loop(0, seg_count // chunk, build, 0)
    dims = (((1,), (1,)), ((), ()))
    lhs = lhs_ref[...]
    with_re = lax.dot_general(lhs, tm_ref[0, 0], dims, preferred_element_type=jnp.float32)
    with_im = lax.dot_general(lhs, tm_ref[0, 1], dims, preferred_element_type=jnp.float32)
    real_sum = with_re[:rows] + with_im[rows:]
    imag_sum = with_re[rows:] - with_im[:rows]
    width = real_sum.shape[1]
    out_ref[:, 0:lag_total, :] += real_sum.reshape(seg_count, lag_total, width)
    out_ref[:, lag_total:, :] += imag_sum.reshape(seg_count, lag_total, width)


def intersect(data, templates, cutoffs, lags, first_block):
    blocks_here, _, seg_count, width = data.shape
    tmpl_local = templates.shape[0]
    lag_total = lags.shape[0]
    block_ids = first_block + jnp.arange(blocks_here, dtype=jnp.int32)
    position = jnp.arange(width, dtype=jnp.int32)
    phase_int = (A * (lags[:, None] * block_ids[None, :] % B))[:, :, None] + (
        lags[:, None] * position[None, :] % LEN
    )[:, None, :]
    phase_angle = (phase_int % LEN).astype(jnp.float32) * (two_pi / LEN)
    phases = jnp.stack([jnp.cos(phase_angle), jnp.sin(phase_angle)], axis=0).transpose(2, 0, 1, 3)
    keep = block_ids[None, None, :, None] < cutoffs[:, None, None, None]
    masked = jnp.where(keep, templates, jnp.zeros_like(templates)).transpose(2, 1, 0, 3)
    rows = seg_count * lag_total
    flops = 2 * 2 * (2 * rows) * width * tmpl_local * blocks_here
    moved = masked.size * 2 + data.size * 2 + phases.size * 4 + seg_count * 2 * lag_total * tmpl_local * 4
    return pl.pallas_call(
        intersect_kernel,
        out_shape=jax.ShapeDtypeStruct((seg_count, 2 * lag_total, tmpl_local), jnp.float32),
        grid=(blocks_here,),
        in_specs=[
            pl.BlockSpec((1, 2, lag_total, width), lambda j: (j, 0, 0, 0)),
            pl.BlockSpec((1, 2, seg_count, width), lambda j: (j, 0, 0, 0)),
            pl.BlockSpec((1, 2, tmpl_local, width), lambda j: (j, 0, 0, 0)),
        ],
        out_specs=pl.BlockSpec((seg_count, 2 * lag_total, tmpl_local), lambda j: (0, 0, 0)),
        scratch_shapes=[pltpu.VMEM((2 * rows, width), jnp.bfloat16)],
        compiler_params=pltpu.CompilerParams(dimension_semantics=("arbitrary",)),
        cost_estimate=pl.CostEstimate(flops=flops, transcendentals=0, bytes_accessed=moved),
    )(phases, data, masked)


def scatter_kernel(axis, size, x_ref, o_ref, recv_ref, send_sem, recv_sem):
    me = lax.axis_index(axis)
    piece = o_ref.shape[0]
    mesh_ids = pl.DeviceIdType.MESH
    barrier = pltpu.get_barrier_semaphore()
    for k in range(1, size):
        peer = lax.rem(me + k, size)
        pl.semaphore_signal(barrier, inc=1, device_id={axis: peer}, device_id_type=mesh_ids)
    pl.semaphore_wait(barrier, size - 1)
    copies = []
    for k in range(1, size):
        peer = lax.rem(me + k, size)
        copy = pltpu.make_async_remote_copy(
            src_ref=x_ref.at[pl.ds(peer * piece, piece)],
            dst_ref=recv_ref.at[k],
            send_sem=send_sem.at[k],
            recv_sem=recv_sem.at[k],
            device_id={axis: peer},
            device_id_type=mesh_ids,
        )
        copy.start()
        copies.append(copy)
    for copy in copies:
        copy.wait()
    total = x_ref[pl.ds(me * piece, piece)]
    for k in range(1, size):
        total = total + recv_ref[k]
    o_ref[...] = total


def scatter_sum(parts, axis, collective_id):
    size = lax.axis_size(axis)
    piece = parts.shape[0] // size
    out_shape = (piece,) + parts.shape[1:]
    vmem = pltpu.VMEM
    return pl.pallas_call(
        functools.partial(scatter_kernel, axis, size),
        out_shape=jax.ShapeDtypeStruct(out_shape, parts.dtype),
        in_specs=[pl.BlockSpec(memory_space=vmem)],
        out_specs=pl.BlockSpec(memory_space=vmem),
        scratch_shapes=[
            vmem((size,) + out_shape, parts.dtype),
            pltpu.SemaphoreType.DMA((size,)),
            pltpu.SemaphoreType.DMA((size,)),
        ],
        compiler_params=pltpu.CompilerParams(collective_id=collective_id, has_side_effects=True),
    )(parts)


def ring4_kernel(axis, x_ref, o_ref, near_ref, far_ref, relay_ref, send_sem, recv_sem):
    me = lax.axis_index(axis)
    piece = o_ref.shape[0]
    half = piece // 2
    mesh_ids = pl.DeviceIdType.MESH
    ahead, across, behind = (lax.rem(me + k, 4) for k in (1, 2, 3))
    barrier = pltpu.get_barrier_semaphore()
    for peer in (ahead, across, behind):
        pl.semaphore_signal(barrier, inc=1, device_id={axis: peer}, device_id_type=mesh_ids)
    pl.semaphore_wait(barrier, 3)

    def send(src, dst, slot, peer):
        return pltpu.make_async_remote_copy(
            src_ref=src, dst_ref=dst, send_sem=send_sem.at[slot], recv_sem=recv_sem.at[slot],
            device_id={axis: peer}, device_id_type=mesh_ids,
        )

    far_start = across * piece
    to_ahead = send(x_ref.at[pl.ds(ahead * piece, piece)], near_ref.at[0], 0, ahead)
    to_behind = send(x_ref.at[pl.ds(behind * piece, piece)], near_ref.at[1], 1, behind)
    direct = send(x_ref.at[pl.ds(far_start, half)], far_ref.at[0], 2, across)
    relay_out = send(x_ref.at[pl.ds(far_start + half, piece - half)], relay_ref, 3, behind)
    for copy in (to_ahead, to_behind, direct, relay_out):
        copy.start()
    relay_out.wait_recv()
    forward = send(relay_ref, far_ref.at[1], 4, behind)
    forward.start()
    to_ahead.wait()
    to_behind.wait()
    direct.wait()
    relay_out.wait_send()
    forward.wait()
    own = x_ref[pl.ds(me * piece, piece)]
    near = near_ref[0] + near_ref[1]
    o_ref[0:half] = own[0:half] + near[0:half] + far_ref[0]
    o_ref[half:] = own[half:] + near[half:] + far_ref[1]


def ring4_sum(parts, axis, collective_id):
    piece = parts.shape[0] // 4
    out_shape = (piece,) + parts.shape[1:]
    half_shape = (piece // 2,) + parts.shape[1:]
    vmem = pltpu.VMEM
    return pl.pallas_call(
        functools.partial(ring4_kernel, axis),
        out_shape=jax.ShapeDtypeStruct(out_shape, parts.dtype),
        in_specs=[pl.BlockSpec(memory_space=vmem)],
        out_specs=pl.BlockSpec(memory_space=vmem),
        scratch_shapes=[
            vmem((2,) + out_shape, parts.dtype),
            vmem((2,) + half_shape, parts.dtype),
            vmem(half_shape, parts.dtype),
            pltpu.SemaphoreType.DMA((5,)),
            pltpu.SemaphoreType.DMA((5,)),
        ],
        compiler_params=pltpu.CompilerParams(collective_id=collective_id, has_side_effects=True),
    )(parts)


def gather_kernel(axis, size, x_ref, o_ref, send_sem, recv_sem):
    me = lax.axis_index(axis)
    mesh_ids = pl.DeviceIdType.MESH
    barrier = pltpu.get_barrier_semaphore()
    for k in range(1, size):
        peer = lax.rem(me + k, size)
        pl.semaphore_signal(barrier, inc=1, device_id={axis: peer}, device_id_type=mesh_ids)
    pl.semaphore_wait(barrier, size - 1)
    copies = []
    for k in range(1, size):
        peer = lax.rem(me + k, size)
        copy = pltpu.make_async_remote_copy(
            src_ref=x_ref,
            dst_ref=o_ref.at[me],
            send_sem=send_sem.at[k],
            recv_sem=recv_sem.at[k],
            device_id={axis: peer},
            device_id_type=mesh_ids,
        )
        copy.start()
        copies.append(copy)
    o_ref[me] = x_ref[...]
    for copy in copies:
        copy.wait()


def gather_all(block, axis, collective_id):
    size = lax.axis_size(axis)
    vmem = pltpu.VMEM
    return pl.pallas_call(
        functools.partial(gather_kernel, axis, size),
        out_shape=jax.ShapeDtypeStruct((size,) + block.shape, block.dtype),
        in_specs=[pl.BlockSpec(memory_space=vmem)],
        out_specs=pl.BlockSpec(memory_space=vmem),
        scratch_shapes=[pltpu.SemaphoreType.DMA((size,)), pltpu.SemaphoreType.DMA((size,))],
        compiler_params=pltpu.CompilerParams(collective_id=collective_id, has_side_effects=True),
    )(block)


def spectrum_blocks(strain, psd):
    freq_count = lax.axis_size(FREQ)
    freq_index = lax.axis_index(FREQ)
    seg_local = strain.shape[0]
    rows_here = A // freq_count
    cols_here = B // freq_count
    highest = lax.Precision.HIGHEST
    first_cos, first_sin = cos_sin_table(
        jnp.arange(A, dtype=jnp.int32), jnp.arange(A, dtype=jnp.int32), A
    )
    first_table = jnp.concatenate([first_cos, -first_sin], axis=0)
    sent = strain.reshape(seg_local, rows_here, freq_count, cols_here).transpose(2, 1, 3, 0)
    sent = sent.reshape(freq_count, rows_here, cols_here * seg_local)
    slab = lax.all_to_all(sent, FREQ, 0, 0, tiled=True).reshape(A, cols_here * seg_local)
    both_parts = jnp.dot(first_table, slab, precision=highest)
    real_part = both_parts[:A]
    imag_part = both_parts[A:]
    time_ids = freq_index * cols_here + jnp.arange(cols_here, dtype=jnp.int32)
    twist_cos, twist_sin = cos_sin_table(jnp.arange(A, dtype=jnp.int32), time_ids, LEN)
    twist_cos = jnp.repeat(twist_cos, seg_local, axis=1)
    twist_sin = jnp.repeat(twist_sin, seg_local, axis=1)
    twisted = jnp.stack(
        [real_part * twist_cos + imag_part * twist_sin, imag_part * twist_cos - real_part * twist_sin]
    )
    p_here = A // freq_count
    twisted = twisted.reshape(2, freq_count, p_here, cols_here, seg_local).transpose(1, 3, 0, 2, 4)
    twisted = twisted.reshape(freq_count, cols_here, 2 * p_here * seg_local)
    columns = lax.all_to_all(twisted, FREQ, 0, 0, tiled=True).reshape(B, 2 * p_here * seg_local)
    split = 32
    j_ids = jnp.arange(NB, dtype=jnp.int32)
    high_cos, high_sin = cos_sin_table(j_ids, split * jnp.arange(B // split, dtype=jnp.int32), B)
    low_cos, low_sin = cos_sin_table(j_ids, jnp.arange(split, dtype=jnp.int32), B)
    second_cos = (
        high_cos[:, :, None] * low_cos[:, None, :] - high_sin[:, :, None] * low_sin[:, None, :]
    ).reshape(NB, B)
    second_sin = (
        high_sin[:, :, None] * low_cos[:, None, :] + high_cos[:, :, None] * low_sin[:, None, :]
    ).reshape(NB, B)
    with_cos = jnp.dot(second_cos, columns, precision=highest).reshape(NB, 2, p_here, seg_local)
    with_sin = jnp.dot(second_sin, columns, precision=highest).reshape(NB, 2, p_here, seg_local)
    amplitude = jnp.sqrt(LEN * psd)[:, :, None]
    real_out = (with_cos[:, 0] + with_sin[:, 1]) / amplitude
    imag_out = (with_cos[:, 1] - with_sin[:, 0]) / amplitude
    whitened = jnp.stack([real_out, imag_out], axis=1).transpose(3, 1, 0, 2).astype(jnp.bfloat16)
    return lax.all_to_all(whitened, FREQ, split_axis=2, concat_axis=3, tiled=True)


def on_device(strain, psd, templates, cutoffs, lags):
    freq_index = lax.axis_index(FREQ)
    local_data = spectrum_blocks(strain, psd)
    seg_piece = gather_all(local_data, "tmpl", 4)
    seg_piece = seg_piece.reshape((-1,) + local_data.shape[1:])
    x_size, z_size, c_size = (lax.axis_size(name) for name in FREQ)
    seg_order = seg_piece.reshape((x_size, z_size, c_size) + seg_piece.shape[1:])
    seg_order = seg_order.transpose(2, 0, 1, 3, 4, 5).reshape(seg_piece.shape)
    data = seg_order.transpose(2, 1, 0, 3)
    j_here = data.shape[0]
    first_block = freq_index * j_here
    partial_sums = intersect(data, templates, cutoffs, lags, first_block)
    partial_sums = scatter_sum(partial_sums, "fc", 1)
    if lax.axis_size("fx") == 4:
        partial_sums = ring4_sum(partial_sums, "fx", 2)
    else:
        partial_sums = scatter_sum(partial_sums, "fx", 2)
    partial_sums = scatter_sum(partial_sums, "fz", 3)
    return partial_sums


def solution(mesh):
    tmpl_size, freq_size = mesh.devices.shape
    split = Mesh(
        mesh.devices.reshape(tmpl_size, 4, freq_size // 8, 2), ("tmpl",) + FREQ
    )
    placed = (P("tmpl", FREQ), P(None, FREQ), P("tmpl", None, FREQ, None), P("tmpl"), P())
    return jax.shard_map(
        on_device, mesh=split, in_specs=placed, out_specs=P(FREQ, None, "tmpl"), check_vma=False
    )
```

```python
import functools
import math

import jax
import jax.numpy as jnp
from jax import lax
from jax.experimental import pallas as pl
from jax.experimental.pallas import tpu as pltpu
from jax.sharding import Mesh, PartitionSpec as P

A = 512
B = 1024
LEN = 524288
NB = 512


two_pi = 2.0 * math.pi
FREQ = ("fx", "fz", "fc")


def cos_sin_table(row_ids, col_ids, modulus):
    product = row_ids[:, None] * col_ids[None, :] % modulus
    phase_angle = product.astype(jnp.float32) * (two_pi / modulus)
    return (jnp.cos(phase_angle), jnp.sin(phase_angle))


def intersect_kernel(ph_ref, dat_ref, tm_ref, out_ref, lhs_ref):
    step = pl.program_id(0)
    seg_count = dat_ref.shape[2]
    lag_total = ph_ref.shape[2]
    rows = seg_count * lag_total
    chunk = 8

    @pl.when(step == 0)
    def _():
        out_ref[...] = jnp.zeros_like(out_ref)

    lag_cos = ph_ref[0, 0][None]
    lag_sin = ph_ref[0, 1][None]

    def build(i, carry):
        s0 = pl.multiple_of(i * chunk, chunk)
        data_real = dat_ref[0, 0, pl.ds(s0, chunk), :].astype(jnp.float32)[:, None, :]
        data_imag = dat_ref[0, 1, pl.ds(s0, chunk), :].astype(jnp.float32)[:, None, :]
        real_q = data_real * lag_cos - data_imag * lag_sin
        imag_q = data_real * lag_sin + data_imag * lag_cos
        r0 = pl.multiple_of(i * chunk * lag_total, chunk * lag_total)
        lhs_ref[pl.ds(r0, chunk * lag_total), :] = real_q.reshape(chunk * lag_total, -1).astype(jnp.bfloat16)
        lhs_ref[pl.ds(rows + r0, chunk * lag_total), :] = imag_q.reshape(chunk * lag_total, -1).astype(jnp.bfloat16)
        return carry

    lax.fori_loop(0, seg_count // chunk, build, 0)
    dims = (((1,), (1,)), ((), ()))
    lhs = lhs_ref[...]
    with_re = lax.dot_general(lhs, tm_ref[0, 0], dims, preferred_element_type=jnp.float32)
    with_im = lax.dot_general(lhs, tm_ref[0, 1], dims, preferred_element_type=jnp.float32)
    real_sum = with_re[:rows] + with_im[rows:]
    imag_sum = with_re[rows:] - with_im[:rows]
    width = real_sum.shape[1]
    out_ref[:, 0:lag_total, :] += real_sum.reshape(seg_count, lag_total, width)
    out_ref[:, lag_total:, :] += imag_sum.reshape(seg_count, lag_total, width)


def intersect(data, templates, cutoffs, lags, first_block):
    blocks_here, _, seg_count, width = data.shape
    tmpl_local = templates.shape[0]
    lag_total = lags.shape[0]
    block_ids = first_block + jnp.arange(blocks_here, dtype=jnp.int32)
    position = jnp.arange(width, dtype=jnp.int32)
    phase_int = (A * (lags[:, None] * block_ids[None, :] % B))[:, :, None] + (
        lags[:, None] * position[None, :] % LEN
    )[:, None, :]
    phase_angle = (phase_int % LEN).astype(jnp.float32) * (two_pi / LEN)
    phases = jnp.stack([jnp.cos(phase_angle), jnp.sin(phase_angle)], axis=0).transpose(2, 0, 1, 3)
    keep = block_ids[None, None, :, None] < cutoffs[:, None, None, None]
    masked = jnp.where(keep, templates, jnp.zeros_like(templates)).transpose(2, 1, 0, 3)
    rows = seg_count * lag_total
    flops = 2 * 2 * (2 * rows) * width * tmpl_local * blocks_here
    moved = masked.size * 2 + data.size * 2 + phases.size * 4 + seg_count * 2 * lag_total * tmpl_local * 4
    return pl.pallas_call(
        intersect_kernel,
        out_shape=jax.ShapeDtypeStruct((seg_count, 2 * lag_total, tmpl_local), jnp.float32),
        grid=(blocks_here,),
        in_specs=[
            pl.BlockSpec((1, 2, lag_total, width), lambda j: (j, 0, 0, 0)),
            pl.BlockSpec((1, 2, seg_count, width), lambda j: (j, 0, 0, 0)),
            pl.BlockSpec((1, 2, tmpl_local, width), lambda j: (j, 0, 0, 0)),
        ],
        out_specs=pl.BlockSpec((seg_count, 2 * lag_total, tmpl_local), lambda j: (0, 0, 0)),
        scratch_shapes=[pltpu.VMEM((2 * rows, width), jnp.bfloat16)],
        compiler_params=pltpu.CompilerParams(dimension_semantics=("arbitrary",)),
        cost_estimate=pl.CostEstimate(flops=flops, transcendentals=0, bytes_accessed=moved),
    )(phases, data, masked)


def scatter_kernel(axis, size, x_ref, o_ref, recv_ref, send_sem, recv_sem):
    me = lax.axis_index(axis)
    piece = o_ref.shape[0]
    mesh_ids = pl.DeviceIdType.MESH
    barrier = pltpu.get_barrier_semaphore()
    for k in range(1, size):
        peer = lax.rem(me + k, size)
        pl.semaphore_signal(barrier, inc=1, device_id={axis: peer}, device_id_type=mesh_ids)
    pl.semaphore_wait(barrier, size - 1)
    copies = []
    for k in sorted(range(1, size), key=lambda k: -min(k, size - k)):
        peer = lax.rem(me + k, size)
        copy = pltpu.make_async_remote_copy(
            src_ref=x_ref.at[pl.ds(peer * piece, piece)],
            dst_ref=recv_ref.at[k],
            send_sem=send_sem.at[k],
            recv_sem=recv_sem.at[k],
            device_id={axis: peer},
            device_id_type=mesh_ids,
        )
        copy.start()
        copies.append(copy)
    for copy in copies:
        copy.wait()
    total = x_ref[pl.ds(me * piece, piece)]
    for k in range(1, size):
        total = total + recv_ref[k]
    o_ref[...] = total


def scatter_sum(parts, axis, collective_id):
    size = lax.axis_size(axis)
    piece = parts.shape[0] // size
    out_shape = (piece,) + parts.shape[1:]
    vmem = pltpu.VMEM
    return pl.pallas_call(
        functools.partial(scatter_kernel, axis, size),
        out_shape=jax.ShapeDtypeStruct(out_shape, parts.dtype),
        in_specs=[pl.BlockSpec(memory_space=vmem)],
        out_specs=pl.BlockSpec(memory_space=vmem),
        scratch_shapes=[
            vmem((size,) + out_shape, parts.dtype),
            pltpu.SemaphoreType.DMA((size,)),
            pltpu.SemaphoreType.DMA((size,)),
        ],
        compiler_params=pltpu.CompilerParams(collective_id=collective_id, has_side_effects=True),
    )(parts)


def gather_kernel(axis, size, x_ref, o_ref, send_sem, recv_sem):
    me = lax.axis_index(axis)
    mesh_ids = pl.DeviceIdType.MESH
    barrier = pltpu.get_barrier_semaphore()
    for k in range(1, size):
        peer = lax.rem(me + k, size)
        pl.semaphore_signal(barrier, inc=1, device_id={axis: peer}, device_id_type=mesh_ids)
    pl.semaphore_wait(barrier, size - 1)
    copies = []
    for k in range(1, size):
        peer = lax.rem(me + k, size)
        copy = pltpu.make_async_remote_copy(
            src_ref=x_ref,
            dst_ref=o_ref.at[me],
            send_sem=send_sem.at[k],
            recv_sem=recv_sem.at[k],
            device_id={axis: peer},
            device_id_type=mesh_ids,
        )
        copy.start()
        copies.append(copy)
    o_ref[me] = x_ref[...]
    for copy in copies:
        copy.wait()


def gather_all(block, axis, collective_id):
    size = lax.axis_size(axis)
    vmem = pltpu.VMEM
    return pl.pallas_call(
        functools.partial(gather_kernel, axis, size),
        out_shape=jax.ShapeDtypeStruct((size,) + block.shape, block.dtype),
        in_specs=[pl.BlockSpec(memory_space=vmem)],
        out_specs=pl.BlockSpec(memory_space=vmem),
        scratch_shapes=[pltpu.SemaphoreType.DMA((size,)), pltpu.SemaphoreType.DMA((size,))],
        compiler_params=pltpu.CompilerParams(collective_id=collective_id, has_side_effects=True),
    )(block)


def spectrum_blocks(strain, psd):
    freq_count = lax.axis_size(FREQ)
    freq_index = lax.axis_index(FREQ)
    seg_local = strain.shape[0]
    rows_here = A // freq_count
    cols_here = B // freq_count
    highest = lax.Precision.HIGHEST
    first_cos, first_sin = cos_sin_table(
        jnp.arange(A, dtype=jnp.int32), jnp.arange(A, dtype=jnp.int32), A
    )
    first_table = jnp.concatenate([first_cos, -first_sin], axis=0)
    sent = strain.reshape(seg_local, rows_here, freq_count, cols_here).transpose(2, 1, 3, 0)
    sent = sent.reshape(freq_count, rows_here, cols_here * seg_local)
    slab = lax.all_to_all(sent, FREQ, 0, 0, tiled=True).reshape(A, cols_here * seg_local)
    both_parts = jnp.dot(first_table, slab, precision=highest)
    real_part = both_parts[:A]
    imag_part = both_parts[A:]
    time_ids = freq_index * cols_here + jnp.arange(cols_here, dtype=jnp.int32)
    twist_cos, twist_sin = cos_sin_table(jnp.arange(A, dtype=jnp.int32), time_ids, LEN)
    twist_cos = jnp.repeat(twist_cos, seg_local, axis=1)
    twist_sin = jnp.repeat(twist_sin, seg_local, axis=1)
    twisted = jnp.stack(
        [real_part * twist_cos + imag_part * twist_sin, imag_part * twist_cos - real_part * twist_sin]
    )
    p_here = A // freq_count
    twisted = twisted.reshape(2, freq_count, p_here, cols_here, seg_local).transpose(1, 3, 0, 2, 4)
    twisted = twisted.reshape(freq_count, cols_here, 2 * p_here * seg_local)
    columns = lax.all_to_all(twisted, FREQ, 0, 0, tiled=True).reshape(B, 2 * p_here * seg_local)
    split = 32
    j_ids = jnp.arange(NB, dtype=jnp.int32)
    high_cos, high_sin = cos_sin_table(j_ids, split * jnp.arange(B // split, dtype=jnp.int32), B)
    low_cos, low_sin = cos_sin_table(j_ids, jnp.arange(split, dtype=jnp.int32), B)
    second_cos = (
        high_cos[:, :, None] * low_cos[:, None, :] - high_sin[:, :, None] * low_sin[:, None, :]
    ).reshape(NB, B)
    second_sin = (
        high_sin[:, :, None] * low_cos[:, None, :] + high_cos[:, :, None] * low_sin[:, None, :]
    ).reshape(NB, B)
    with_cos = jnp.dot(second_cos, columns, precision=highest).reshape(NB, 2, p_here, seg_local)
    with_sin = jnp.dot(second_sin, columns, precision=highest).reshape(NB, 2, p_here, seg_local)
    amplitude = jnp.sqrt(LEN * psd)[:, :, None]
    real_out = (with_cos[:, 0] + with_sin[:, 1]) / amplitude
    imag_out = (with_cos[:, 1] - with_sin[:, 0]) / amplitude
    whitened = jnp.stack([real_out, imag_out], axis=1).transpose(3, 1, 0, 2).astype(jnp.bfloat16)
    return lax.all_to_all(whitened, FREQ, split_axis=2, concat_axis=3, tiled=True)


def on_device(strain, psd, templates, cutoffs, lags):
    freq_index = lax.axis_index(FREQ)
    local_data = spectrum_blocks(strain, psd)
    seg_piece = gather_all(local_data, "tmpl", 4)
    seg_piece = seg_piece.reshape((-1,) + local_data.shape[1:])
    x_size, z_size, c_size = (lax.axis_size(name) for name in FREQ)
    seg_order = seg_piece.reshape((x_size, z_size, c_size) + seg_piece.shape[1:])
    seg_order = seg_order.transpose(2, 0, 1, 3, 4, 5).reshape(seg_piece.shape)
    data = seg_order.transpose(2, 1, 0, 3)
    j_here = data.shape[0]
    first_block = freq_index * j_here
    partial_sums = intersect(data, templates, cutoffs, lags, first_block)
    for collective_id, name in enumerate(("fc", "fx", "fz")):
        partial_sums = scatter_sum(partial_sums, name, collective_id + 1)
    return partial_sums


def solution(mesh):
    tmpl_size, freq_size = mesh.devices.shape
    split = Mesh(
        mesh.devices.reshape(tmpl_size, 4, freq_size // 8, 2), ("tmpl",) + FREQ
    )
    placed = (P("tmpl", FREQ), P(None, FREQ), P("tmpl", None, FREQ, None), P("tmpl"), P())
    return jax.shard_map(
        on_device, mesh=split, in_specs=placed, out_specs=P(FREQ, None, "tmpl"), check_vma=False
    )
```

```python
import functools
import math

import jax
import jax.numpy as jnp
from jax import lax
from jax.experimental import pallas as pl
from jax.experimental.pallas import tpu as pltpu
from jax.sharding import Mesh, PartitionSpec as P

A = 512
B = 1024
LEN = 524288
NB = 512


two_pi = 2.0 * math.pi
FREQ = ("fx", "fz", "fc")


def cos_sin_table(row_ids, col_ids, modulus):
    product = row_ids[:, None] * col_ids[None, :] % modulus
    phase_angle = product.astype(jnp.float32) * (two_pi / modulus)
    return (jnp.cos(phase_angle), jnp.sin(phase_angle))


def intersect_kernel(ph_ref, dat_ref, tm_ref, out_ref, lhs_ref):
    step = pl.program_id(0)
    seg_count = dat_ref.shape[2]
    lag_total = ph_ref.shape[2]
    rows = seg_count * lag_total
    chunk = 8

    @pl.when(step == 0)
    def _():
        out_ref[...] = jnp.zeros_like(out_ref)

    lag_cos = ph_ref[0, 0][None]
    lag_sin = ph_ref[0, 1][None]

    def build(i, carry):
        s0 = pl.multiple_of(i * chunk, chunk)
        data_real = dat_ref[0, 0, pl.ds(s0, chunk), :].astype(jnp.float32)[:, None, :]
        data_imag = dat_ref[0, 1, pl.ds(s0, chunk), :].astype(jnp.float32)[:, None, :]
        real_q = data_real * lag_cos - data_imag * lag_sin
        imag_q = data_real * lag_sin + data_imag * lag_cos
        r0 = pl.multiple_of(i * chunk * lag_total, chunk * lag_total)
        lhs_ref[pl.ds(r0, chunk * lag_total), :] = real_q.reshape(chunk * lag_total, -1).astype(jnp.bfloat16)
        lhs_ref[pl.ds(rows + r0, chunk * lag_total), :] = imag_q.reshape(chunk * lag_total, -1).astype(jnp.bfloat16)
        return carry

    lax.fori_loop(0, seg_count // chunk, build, 0, unroll=True)
    dims = (((1,), (1,)), ((), ()))
    lhs = lhs_ref[...]
    with_re = lax.dot_general(lhs, tm_ref[0, 0], dims, preferred_element_type=jnp.float32)
    with_im = lax.dot_general(lhs, tm_ref[0, 1], dims, preferred_element_type=jnp.float32)
    real_sum = with_re[:rows] + with_im[rows:]
    imag_sum = with_re[rows:] - with_im[:rows]
    width = real_sum.shape[1]
    out_ref[:, 0:lag_total, :] += real_sum.reshape(seg_count, lag_total, width)
    out_ref[:, lag_total:, :] += imag_sum.reshape(seg_count, lag_total, width)


def intersect(data, templates, cutoffs, lags, first_block):
    blocks_here, _, seg_count, width = data.shape
    tmpl_local = templates.shape[0]
    lag_total = lags.shape[0]
    block_ids = first_block + jnp.arange(blocks_here, dtype=jnp.int32)
    position = jnp.arange(width, dtype=jnp.int32)
    phase_int = (A * (lags[:, None] * block_ids[None, :] % B))[:, :, None] + (
        lags[:, None] * position[None, :] % LEN
    )[:, None, :]
    phase_angle = (phase_int % LEN).astype(jnp.float32) * (two_pi / LEN)
    phases = jnp.stack([jnp.cos(phase_angle), jnp.sin(phase_angle)], axis=0).transpose(2, 0, 1, 3)
    keep = block_ids[None, None, :, None] < cutoffs[:, None, None, None]
    masked = jnp.where(keep, templates, jnp.zeros_like(templates)).transpose(2, 1, 0, 3)
    rows = seg_count * lag_total
    flops = 2 * 2 * (2 * rows) * width * tmpl_local * blocks_here
    moved = masked.size * 2 + data.size * 2 + phases.size * 4 + seg_count * 2 * lag_total * tmpl_local * 4
    return pl.pallas_call(
        intersect_kernel,
        out_shape=jax.ShapeDtypeStruct((seg_count, 2 * lag_total, tmpl_local), jnp.float32),
        grid=(blocks_here,),
        in_specs=[
            pl.BlockSpec((1, 2, lag_total, width), lambda j: (j, 0, 0, 0)),
            pl.BlockSpec((1, 2, seg_count, width), lambda j: (j, 0, 0, 0)),
            pl.BlockSpec((1, 2, tmpl_local, width), lambda j: (j, 0, 0, 0)),
        ],
        out_specs=pl.BlockSpec((seg_count, 2 * lag_total, tmpl_local), lambda j: (0, 0, 0)),
        scratch_shapes=[pltpu.VMEM((2 * rows, width), jnp.bfloat16)],
        compiler_params=pltpu.CompilerParams(dimension_semantics=("arbitrary",)),
        cost_estimate=pl.CostEstimate(flops=flops, transcendentals=0, bytes_accessed=moved),
    )(phases, data, masked)


def scatter_kernel(axis, size, x_ref, o_ref, recv_ref, send_sem, recv_sem):
    me = lax.axis_index(axis)
    piece = o_ref.shape[0]
    mesh_ids = pl.DeviceIdType.MESH
    barrier = pltpu.get_barrier_semaphore()
    for k in range(1, size):
        peer = lax.rem(me + k, size)
        pl.semaphore_signal(barrier, inc=1, device_id={axis: peer}, device_id_type=mesh_ids)
    pl.semaphore_wait(barrier, size - 1)
    copies = []
    for k in range(1, size):
        peer = lax.rem(me + k, size)
        copy = pltpu.make_async_remote_copy(
            src_ref=x_ref.at[pl.ds(peer * piece, piece)],
            dst_ref=recv_ref.at[k],
            send_sem=send_sem.at[k],
            recv_sem=recv_sem.at[k],
            device_id={axis: peer},
            device_id_type=mesh_ids,
        )
        copy.start()
        copies.append(copy)
    for copy in copies:
        copy.wait()
    total = x_ref[pl.ds(me * piece, piece)]
    for k in range(1, size):
        total = total + recv_ref[k]
    o_ref[...] = total


def scatter_sum(parts, axis, collective_id):
    size = lax.axis_size(axis)
    piece = parts.shape[0] // size
    out_shape = (piece,) + parts.shape[1:]
    vmem = pltpu.VMEM
    return pl.pallas_call(
        functools.partial(scatter_kernel, axis, size),
        out_shape=jax.ShapeDtypeStruct(out_shape, parts.dtype),
        in_specs=[pl.BlockSpec(memory_space=vmem)],
        out_specs=pl.BlockSpec(memory_space=vmem),
        scratch_shapes=[
            vmem((size,) + out_shape, parts.dtype),
            pltpu.SemaphoreType.DMA((size,)),
            pltpu.SemaphoreType.DMA((size,)),
        ],
        compiler_params=pltpu.CompilerParams(collective_id=collective_id, has_side_effects=True),
    )(parts)


def gather_kernel(axis, size, x_ref, o_ref, send_sem, recv_sem):
    me = lax.axis_index(axis)
    mesh_ids = pl.DeviceIdType.MESH
    barrier = pltpu.get_barrier_semaphore()
    for k in range(1, size):
        peer = lax.rem(me + k, size)
        pl.semaphore_signal(barrier, inc=1, device_id={axis: peer}, device_id_type=mesh_ids)
    pl.semaphore_wait(barrier, size - 1)
    copies = []
    for k in range(1, size):
        peer = lax.rem(me + k, size)
        copy = pltpu.make_async_remote_copy(
            src_ref=x_ref,
            dst_ref=o_ref.at[me],
            send_sem=send_sem.at[k],
            recv_sem=recv_sem.at[k],
            device_id={axis: peer},
            device_id_type=mesh_ids,
        )
        copy.start()
        copies.append(copy)
    o_ref[me] = x_ref[...]
    for copy in copies:
        copy.wait()


def gather_all(block, axis, collective_id):
    size = lax.axis_size(axis)
    vmem = pltpu.VMEM
    return pl.pallas_call(
        functools.partial(gather_kernel, axis, size),
        out_shape=jax.ShapeDtypeStruct((size,) + block.shape, block.dtype),
        in_specs=[pl.BlockSpec(memory_space=vmem)],
        out_specs=pl.BlockSpec(memory_space=vmem),
        scratch_shapes=[pltpu.SemaphoreType.DMA((size,)), pltpu.SemaphoreType.DMA((size,))],
        compiler_params=pltpu.CompilerParams(collective_id=collective_id, has_side_effects=True),
    )(block)


def spectrum_blocks(strain, psd):
    freq_count = lax.axis_size(FREQ)
    freq_index = lax.axis_index(FREQ)
    seg_local = strain.shape[0]
    rows_here = A // freq_count
    cols_here = B // freq_count
    highest = lax.Precision.HIGHEST
    first_cos, first_sin = cos_sin_table(
        jnp.arange(A, dtype=jnp.int32), jnp.arange(A, dtype=jnp.int32), A
    )
    first_table = jnp.concatenate([first_cos, -first_sin], axis=0)
    sent = strain.reshape(seg_local, rows_here, freq_count, cols_here).transpose(2, 1, 3, 0)
    sent = sent.reshape(freq_count, rows_here, cols_here * seg_local)
    slab = lax.all_to_all(sent, FREQ, 0, 0, tiled=True).reshape(A, cols_here * seg_local)
    both_parts = jnp.dot(first_table, slab, precision=highest)
    real_part = both_parts[:A]
    imag_part = both_parts[A:]
    time_ids = freq_index * cols_here + jnp.arange(cols_here, dtype=jnp.int32)
    twist_cos, twist_sin = cos_sin_table(jnp.arange(A, dtype=jnp.int32), time_ids, LEN)
    twist_cos = jnp.repeat(twist_cos, seg_local, axis=1)
    twist_sin = jnp.repeat(twist_sin, seg_local, axis=1)
    twisted = jnp.stack(
        [real_part * twist_cos + imag_part * twist_sin, imag_part * twist_cos - real_part * twist_sin]
    )
    p_here = A // freq_count
    twisted = twisted.reshape(2, freq_count, p_here, cols_here, seg_local).transpose(1, 3, 0, 2, 4)
    twisted = twisted.reshape(freq_count, cols_here, 2 * p_here * seg_local)
    columns = lax.all_to_all(twisted, FREQ, 0, 0, tiled=True).reshape(B, 2 * p_here * seg_local)
    split = 32
    j_ids = jnp.arange(NB, dtype=jnp.int32)
    high_cos, high_sin = cos_sin_table(j_ids, split * jnp.arange(B // split, dtype=jnp.int32), B)
    low_cos, low_sin = cos_sin_table(j_ids, jnp.arange(split, dtype=jnp.int32), B)
    second_cos = (
        high_cos[:, :, None] * low_cos[:, None, :] - high_sin[:, :, None] * low_sin[:, None, :]
    ).reshape(NB, B)
    second_sin = (
        high_sin[:, :, None] * low_cos[:, None, :] + high_cos[:, :, None] * low_sin[:, None, :]
    ).reshape(NB, B)
    with_cos = jnp.dot(second_cos, columns, precision=highest).reshape(NB, 2, p_here, seg_local)
    with_sin = jnp.dot(second_sin, columns, precision=highest).reshape(NB, 2, p_here, seg_local)
    amplitude = jnp.sqrt(LEN * psd)[:, :, None]
    real_out = (with_cos[:, 0] + with_sin[:, 1]) / amplitude
    imag_out = (with_cos[:, 1] - with_sin[:, 0]) / amplitude
    whitened = jnp.stack([real_out, imag_out], axis=1).transpose(3, 1, 0, 2).astype(jnp.bfloat16)
    return lax.all_to_all(whitened, FREQ, split_axis=2, concat_axis=3, tiled=True)


def on_device(strain, psd, templates, cutoffs, lags):
    freq_index = lax.axis_index(FREQ)
    local_data = spectrum_blocks(strain, psd)
    seg_piece = gather_all(local_data, "tmpl", 4)
    seg_piece = seg_piece.reshape((-1,) + local_data.shape[1:])
    x_size, z_size, c_size = (lax.axis_size(name) for name in FREQ)
    seg_order = seg_piece.reshape((x_size, z_size, c_size) + seg_piece.shape[1:])
    seg_order = seg_order.transpose(2, 0, 1, 3, 4, 5).reshape(seg_piece.shape)
    data = seg_order.transpose(2, 1, 0, 3)
    j_here = data.shape[0]
    first_block = freq_index * j_here
    partial_sums = intersect(data, templates, cutoffs, lags, first_block)
    for collective_id, name in enumerate(("fc", "fx", "fz")):
        partial_sums = scatter_sum(partial_sums, name, collective_id + 1)
    return partial_sums


def solution(mesh):
    tmpl_size, freq_size = mesh.devices.shape
    split = Mesh(
        mesh.devices.reshape(tmpl_size, 4, freq_size // 8, 2), ("tmpl",) + FREQ
    )
    placed = (P("tmpl", FREQ), P(None, FREQ), P("tmpl", None, FREQ, None), P("tmpl"), P())
    return jax.shard_map(
        on_device, mesh=split, in_specs=placed, out_specs=P(FREQ, None, "tmpl"), check_vma=False
    )
```

```python
import functools
import math

import jax
import jax.numpy as jnp
from jax import lax
from jax.experimental import pallas as pl
from jax.experimental.pallas import tpu as pltpu
from jax.sharding import Mesh, PartitionSpec as P

A = 512
B = 1024
LEN = 524288
NB = 512


two_pi = 2.0 * math.pi
FREQ = ("fx", "fz", "fc")


def cos_sin_table(row_ids, col_ids, modulus):
    product = row_ids[:, None] * col_ids[None, :] % modulus
    phase_angle = product.astype(jnp.float32) * (two_pi / modulus)
    return (jnp.cos(phase_angle), jnp.sin(phase_angle))


def intersect_kernel(ph_ref, dat_ref, tm_ref, out_ref, lhs_ref):
    step = pl.program_id(0)
    seg_count = dat_ref.shape[2]
    lag_total = ph_ref.shape[2]
    rows = seg_count * lag_total
    chunk = 8

    @pl.when(step == 0)
    def _():
        out_ref[...] = jnp.zeros_like(out_ref)

    lag_cos = ph_ref[0, 0][None]
    lag_sin = ph_ref[0, 1][None]

    def build(i, carry):
        s0 = pl.multiple_of(i * chunk, chunk)
        data_real = dat_ref[0, 0, pl.ds(s0, chunk), :].astype(jnp.float32)[:, None, :]
        data_imag = dat_ref[0, 1, pl.ds(s0, chunk), :].astype(jnp.float32)[:, None, :]
        real_q = data_real * lag_cos - data_imag * lag_sin
        imag_q = data_real * lag_sin + data_imag * lag_cos
        r0 = pl.multiple_of(i * chunk * lag_total, chunk * lag_total)
        lhs_ref[pl.ds(r0, chunk * lag_total), :] = real_q.reshape(chunk * lag_total, -1).astype(jnp.bfloat16)
        lhs_ref[pl.ds(rows + r0, chunk * lag_total), :] = imag_q.reshape(chunk * lag_total, -1).astype(jnp.bfloat16)
        return carry

    lax.fori_loop(0, seg_count // chunk, build, 0, unroll=True)
    dims = (((1,), (0,)), ((), ()))
    lhs = lhs_ref[...]
    with_re = lax.dot_general(lhs, tm_ref[0, 0], dims, preferred_element_type=jnp.float32)
    with_im = lax.dot_general(lhs, tm_ref[0, 1], dims, preferred_element_type=jnp.float32)
    real_sum = with_re[:rows] + with_im[rows:]
    imag_sum = with_re[rows:] - with_im[:rows]
    width = real_sum.shape[1]
    out_ref[:, 0:lag_total, :] += real_sum.reshape(seg_count, lag_total, width)
    out_ref[:, lag_total:, :] += imag_sum.reshape(seg_count, lag_total, width)


def intersect(data, templates, cutoffs, lags, first_block):
    blocks_here, _, seg_count, width = data.shape
    tmpl_local = templates.shape[0]
    lag_total = lags.shape[0]
    block_ids = first_block + jnp.arange(blocks_here, dtype=jnp.int32)
    position = jnp.arange(width, dtype=jnp.int32)
    phase_int = (A * (lags[:, None] * block_ids[None, :] % B))[:, :, None] + (
        lags[:, None] * position[None, :] % LEN
    )[:, None, :]
    phase_angle = (phase_int % LEN).astype(jnp.float32) * (two_pi / LEN)
    phases = jnp.stack([jnp.cos(phase_angle), jnp.sin(phase_angle)], axis=0).transpose(2, 0, 1, 3)
    keep = block_ids[None, None, :, None] < cutoffs[:, None, None, None]
    masked = jnp.where(keep, templates, jnp.zeros_like(templates)).transpose(2, 1, 3, 0)
    rows = seg_count * lag_total
    flops = 2 * 2 * (2 * rows) * width * tmpl_local * blocks_here
    moved = masked.size * 2 + data.size * 2 + phases.size * 4 + seg_count * 2 * lag_total * tmpl_local * 4
    return pl.pallas_call(
        intersect_kernel,
        out_shape=jax.ShapeDtypeStruct((seg_count, 2 * lag_total, tmpl_local), jnp.float32),
        grid=(blocks_here,),
        in_specs=[
            pl.BlockSpec((1, 2, lag_total, width), lambda j: (j, 0, 0, 0)),
            pl.BlockSpec((1, 2, seg_count, width), lambda j: (j, 0, 0, 0)),
            pl.BlockSpec((1, 2, width, tmpl_local), lambda j: (j, 0, 0, 0)),
        ],
        out_specs=pl.BlockSpec((seg_count, 2 * lag_total, tmpl_local), lambda j: (0, 0, 0)),
        scratch_shapes=[pltpu.VMEM((2 * rows, width), jnp.bfloat16)],
        compiler_params=pltpu.CompilerParams(dimension_semantics=("arbitrary",)),
        cost_estimate=pl.CostEstimate(flops=flops, transcendentals=0, bytes_accessed=moved),
    )(phases, data, masked)


def scatter_kernel(axis, size, x_ref, o_ref, recv_ref, send_sem, recv_sem):
    me = lax.axis_index(axis)
    piece = o_ref.shape[0]
    mesh_ids = pl.DeviceIdType.MESH
    barrier = pltpu.get_barrier_semaphore()
    for k in range(1, size):
        peer = lax.rem(me + k, size)
        pl.semaphore_signal(barrier, inc=1, device_id={axis: peer}, device_id_type=mesh_ids)
    pl.semaphore_wait(barrier, size - 1)
    copies = []
    for k in range(1, size):
        peer = lax.rem(me + k, size)
        copy = pltpu.make_async_remote_copy(
            src_ref=x_ref.at[pl.ds(peer * piece, piece)],
            dst_ref=recv_ref.at[k],
            send_sem=send_sem.at[k],
            recv_sem=recv_sem.at[k],
            device_id={axis: peer},
            device_id_type=mesh_ids,
        )
        copy.start()
        copies.append(copy)
    for copy in copies:
        copy.wait()
    total = x_ref[pl.ds(me * piece, piece)]
    for k in range(1, size):
        total = total + recv_ref[k]
    o_ref[...] = total


def scatter_sum(parts, axis, collective_id):
    size = lax.axis_size(axis)
    piece = parts.shape[0] // size
    out_shape = (piece,) + parts.shape[1:]
    vmem = pltpu.VMEM
    return pl.pallas_call(
        functools.partial(scatter_kernel, axis, size),
        out_shape=jax.ShapeDtypeStruct(out_shape, parts.dtype),
        in_specs=[pl.BlockSpec(memory_space=vmem)],
        out_specs=pl.BlockSpec(memory_space=vmem),
        scratch_shapes=[
            vmem((size,) + out_shape, parts.dtype),
            pltpu.SemaphoreType.DMA((size,)),
            pltpu.SemaphoreType.DMA((size,)),
        ],
        compiler_params=pltpu.CompilerParams(collective_id=collective_id, has_side_effects=True),
    )(parts)


def gather_kernel(axis, size, x_ref, o_ref, send_sem, recv_sem):
    me = lax.axis_index(axis)
    mesh_ids = pl.DeviceIdType.MESH
    barrier = pltpu.get_barrier_semaphore()
    for k in range(1, size):
        peer = lax.rem(me + k, size)
        pl.semaphore_signal(barrier, inc=1, device_id={axis: peer}, device_id_type=mesh_ids)
    pl.semaphore_wait(barrier, size - 1)
    copies = []
    for k in range(1, size):
        peer = lax.rem(me + k, size)
        copy = pltpu.make_async_remote_copy(
            src_ref=x_ref,
            dst_ref=o_ref.at[me],
            send_sem=send_sem.at[k],
            recv_sem=recv_sem.at[k],
            device_id={axis: peer},
            device_id_type=mesh_ids,
        )
        copy.start()
        copies.append(copy)
    o_ref[me] = x_ref[...]
    for copy in copies:
        copy.wait()


def gather_all(block, axis, collective_id):
    size = lax.axis_size(axis)
    vmem = pltpu.VMEM
    return pl.pallas_call(
        functools.partial(gather_kernel, axis, size),
        out_shape=jax.ShapeDtypeStruct((size,) + block.shape, block.dtype),
        in_specs=[pl.BlockSpec(memory_space=vmem)],
        out_specs=pl.BlockSpec(memory_space=vmem),
        scratch_shapes=[pltpu.SemaphoreType.DMA((size,)), pltpu.SemaphoreType.DMA((size,))],
        compiler_params=pltpu.CompilerParams(collective_id=collective_id, has_side_effects=True),
    )(block)


def spectrum_blocks(strain, psd):
    freq_count = lax.axis_size(FREQ)
    freq_index = lax.axis_index(FREQ)
    seg_local = strain.shape[0]
    rows_here = A // freq_count
    cols_here = B // freq_count
    highest = lax.Precision.HIGHEST
    first_cos, first_sin = cos_sin_table(
        jnp.arange(A, dtype=jnp.int32), jnp.arange(A, dtype=jnp.int32), A
    )
    first_table = jnp.concatenate([first_cos, -first_sin], axis=0)
    sent = strain.reshape(seg_local, rows_here, freq_count, cols_here).transpose(2, 1, 3, 0)
    sent = sent.reshape(freq_count, rows_here, cols_here * seg_local)
    slab = lax.all_to_all(sent, FREQ, 0, 0, tiled=True).reshape(A, cols_here * seg_local)
    both_parts = jnp.dot(first_table, slab, precision=highest)
    real_part = both_parts[:A]
    imag_part = both_parts[A:]
    time_ids = freq_index * cols_here + jnp.arange(cols_here, dtype=jnp.int32)
    twist_cos, twist_sin = cos_sin_table(jnp.arange(A, dtype=jnp.int32), time_ids, LEN)
    twist_cos = jnp.repeat(twist_cos, seg_local, axis=1)
    twist_sin = jnp.repeat(twist_sin, seg_local, axis=1)
    twisted = jnp.stack(
        [real_part * twist_cos + imag_part * twist_sin, imag_part * twist_cos - real_part * twist_sin]
    )
    p_here = A // freq_count
    twisted = twisted.reshape(2, freq_count, p_here, cols_here, seg_local).transpose(1, 3, 0, 2, 4)
    twisted = twisted.reshape(freq_count, cols_here, 2 * p_here * seg_local)
    columns = lax.all_to_all(twisted, FREQ, 0, 0, tiled=True).reshape(B, 2 * p_here * seg_local)
    split = 32
    j_ids = jnp.arange(NB, dtype=jnp.int32)
    high_cos, high_sin = cos_sin_table(j_ids, split * jnp.arange(B // split, dtype=jnp.int32), B)
    low_cos, low_sin = cos_sin_table(j_ids, jnp.arange(split, dtype=jnp.int32), B)
    second_cos = (
        high_cos[:, :, None] * low_cos[:, None, :] - high_sin[:, :, None] * low_sin[:, None, :]
    ).reshape(NB, B)
    second_sin = (
        high_sin[:, :, None] * low_cos[:, None, :] + high_cos[:, :, None] * low_sin[:, None, :]
    ).reshape(NB, B)
    with_cos = jnp.dot(second_cos, columns, precision=highest).reshape(NB, 2, p_here, seg_local)
    with_sin = jnp.dot(second_sin, columns, precision=highest).reshape(NB, 2, p_here, seg_local)
    amplitude = jnp.sqrt(LEN * psd)[:, :, None]
    real_out = (with_cos[:, 0] + with_sin[:, 1]) / amplitude
    imag_out = (with_cos[:, 1] - with_sin[:, 0]) / amplitude
    whitened = jnp.stack([real_out, imag_out], axis=1).transpose(3, 1, 0, 2).astype(jnp.bfloat16)
    return lax.all_to_all(whitened, FREQ, split_axis=2, concat_axis=3, tiled=True)


def on_device(strain, psd, templates, cutoffs, lags):
    freq_index = lax.axis_index(FREQ)
    local_data = spectrum_blocks(strain, psd)
    seg_piece = gather_all(local_data, "tmpl", 4)
    seg_piece = seg_piece.reshape((-1,) + local_data.shape[1:])
    x_size, z_size, c_size = (lax.axis_size(name) for name in FREQ)
    seg_order = seg_piece.reshape((x_size, z_size, c_size) + seg_piece.shape[1:])
    seg_order = seg_order.transpose(2, 0, 1, 3, 4, 5).reshape(seg_piece.shape)
    data = seg_order.transpose(2, 1, 0, 3)
    j_here = data.shape[0]
    first_block = freq_index * j_here
    partial_sums = intersect(data, templates, cutoffs, lags, first_block)
    for collective_id, name in enumerate(("fc", "fx", "fz")):
        partial_sums = scatter_sum(partial_sums, name, collective_id + 1)
    return partial_sums


def solution(mesh):
    tmpl_size, freq_size = mesh.devices.shape
    split = Mesh(
        mesh.devices.reshape(tmpl_size, 4, freq_size // 8, 2), ("tmpl",) + FREQ
    )
    placed = (P("tmpl", FREQ), P(None, FREQ), P("tmpl", None, FREQ, None), P("tmpl"), P())
    return jax.shard_map(
        on_device, mesh=split, in_specs=placed, out_specs=P(FREQ, None, "tmpl"), check_vma=False
    )
```
